256 devices in a mesh: lev: 2 (over x_lo), gx: 16 (over x_hi, z), gy: 8 (over y, core).
Axes of the slice: x: 4 (x_hi: 2, x_lo: 2; x = x_hi * 2 + x_lo), y: 4, z: 8, core: 2. Of those that a mesh axis runs over, the one named last changes fastest.
Arguments:
- initial_conc: float32 [4, 4, 1024, 1024], P(None, 'lev', 'gx', 'gy'), may hold values from -6 to 6
- diffusivity: float32 [4, 1024, 1024], P('lev', 'gx', 'gy'), may hold values from 0.02 to 0.2
- wind_east: float32 [4, 1024, 1024], P('lev', 'gx', 'gy'), may hold values from -0.4 to 0.4
- wind_north: float32 [4, 1024, 1024], P('lev', 'gx', 'gy'), may hold values from -0.4 to 0.4
- level_weight: float32 [4, 4], P(None, 'lev'), may hold values from 0.05 to 0.5
- sounding_owner: int32 [65536, 1], P(('gx', 'gy')), may hold values from 0 to 127; in each aligned block of 512 rows (0 to 511, 512 to 1023, ...) at most 16 rows name the same one
- sounding_column: int32 [65536], P(('gx', 'gy')), may hold values from 0 to 8191
- observed: float32 [65536], P(('gx', 'gy')), may hold values from -15 to 15
Outputs:
- forecast: float32 [4, 4, 1024, 1024], P(None, 'lev', 'gx', 'gy')
- model_column: float32 [65536], P(('gx', 'gy'))
- gradient: float32 [4, 4, 1024, 1024], P(None, 'lev', 'gx', 'gy')
The draws below stay inside these ranges and needn't reach their ends.
Inputs may be any that keep to these rules, and one draw needn't show every extreme that they name: `sounding_owner`: among the 512 soundings of one device, at most 16 have the same owner, and this many is reached.
All inputs are finite; a program needn't handle non-finite values.
Results may differ from the reference program's by a relative error of at most 0.00002.
Values sent between devices are 32-bit elements; how exact they have to be, the bound alone decides.
No kernel may reach another device: no remote copies, remote signals or barrier semaphores. Data moves between devices by JAX's collectives and lax.ppermute only.
A program may use at most 64 MiB of HBM per device.

```python
import math
import jax
import jax.numpy as jnp
import numpy as np

TRACERS = 4
STEPS = 4
CX = 64
CY = 128
SND_DEV = 512
CAP = 16
LEVELS = 4
NX = 1024
NY = 1024
SOUNDINGS = 65536
N_GX = 16
N_GY = 8


def set_ends(entries, own_key, low, top_value):
    longest = entries.shape.index(max(entries.shape))
    spots = []
    for shift in (0, 1):
        where = [jax.random.randint(jax.random.fold_in(own_key, axis), (), 0, length) for axis, length in enumerate(entries.shape)]
        where[longest] = (where[longest] + shift) % entries.shape[longest]
        spots.append(tuple(where))
    return entries.at[spots[0]].set(low).at[spots[1]].set(top_value)


def level_of(key, extent, pieces, least, largest):
    def one(axis_at, shards_of):
        steps = jax.random.uniform(jax.random.fold_in(jax.random.fold_in(key, 6), axis_at), (shards_of,), jnp.float32, least / len(pieces), largest / len(pieces))
        return jnp.repeat(jnp.exp(steps), extent[axis_at] // shards_of).reshape((-1,) + (1,) * (len(extent) - axis_at - 1))

    gain = one(*pieces[0])
    for cut in pieces[1:]:
        gain = gain * one(*cut)
    return gain


def shared_out(stream_key, own, number, rows, amount, top, reach, slope):
    sequence = jax.random.permutation(stream_key, amount)
    heavy_load, common = portions_of(amount, rows * top, reach, slope, True), portions_of(amount, rows * top, reach, slope, False)
    places = jnp.arange(amount)

    def named(sizes, rotation):
        used = int((sizes > 0).sum())
        fixed = max(1, used // 4)
        passed = fixed + (places - fixed + rotation * (used - fixed)) % max(1, amount - fixed)
        return jnp.zeros((amount,), jnp.int32).at[sequence[jnp.where(places < fixed, places, passed)]].set(jnp.asarray(sizes, jnp.int32))

    sizes = jnp.where(number % 4 == 0, named(heavy_load, number // 4), named(common, number - number // 4 - 1))
    mixed = jax.random.permutation(jax.random.fold_in(own, 3), amount)
    source_of, sink = mixed[0:amount // 2 * 2:2], mixed[1:amount // 2 * 2:2]
    slack = jnp.minimum(sizes[source_of] - 1, reach - sizes[sink]) // 2
    slack = jnp.where((source_of == sequence[0]) | (sink == sequence[0]) | (sizes[sink] == 0), 0, jnp.maximum(slack, 0))
    passed = jax.random.randint(jax.random.fold_in(own, 4), (amount // 2,), 0, 1 << 20) % (slack + 1)
    sizes = sizes.at[source_of].add(-passed).at[sink].add(passed)
    items = jnp.searchsorted(jnp.cumsum(sizes), jnp.arange(rows * top), side="right").astype(jnp.int32)
    table = items.reshape(top, rows).T
    table = table[jax.random.permutation(jax.random.fold_in(own, 1), rows)]
    rotation = jax.random.randint(jax.random.fold_in(own, 2), (rows, 1), 0, top)
    return jnp.take_along_axis(table, (jnp.arange(top)[None, :] + rotation) % top, axis=1)


def portions_of(count, total, reach, slope, full):
    weights = [(1 << 20) // math.isqrt(standing ** slope) + 1 for standing in range(1, count + 1)]
    largest = reach if full else min(reach, max(-(-total // count), total * weights[0] // sum(weights)))
    least = 1 if total - largest >= count - 1 else 0
    holding, rest = [largest] + [least] * (count - 1), total - largest - least * (count - 1)
    while rest > 0:
        movable = [i for i in range(1, count) if holding[i] < largest] or [i for i in range(1, count) if holding[i] < reach]
        whole, left = sum([weights[i] for i in movable]), rest
        for i in movable:
            addition = min(reach - holding[i], max(1, left * weights[i] // whole), rest)
            holding[i] = holding[i] + addition
            rest = rest - addition
    return np.array(holding)


def centred(rng, extent, spread, bound, cuts=(), kind=jnp.bfloat16):
    drawn = jax.random.normal(rng, extent, jnp.float32) * spread
    if len(cuts) > 0:
        drawn = level_of(rng, extent, cuts, -0.22, 0.18) * drawn
    return jnp.clip(drawn, min=-bound, max=bound).astype(kind)


def setup_inputs(seed: int = 0) -> dict:
    arg_keys = jax.random.split(jax.random.key(seed), 9)
    initial_conc = centred(arg_keys[0], (TRACERS, LEVELS, NX, NY), 1.0, 6.0, ((1, 2), (2, 16), (3, 8)), jnp.float32)
    diffusivity = jnp.clip(jnp.exp(math.log(0.2) - 2.3025851 * jax.random.uniform(arg_keys[1], (LEVELS, NX, NY), jnp.float32) ** level_of(arg_keys[1], (LEVELS, NX, NY), ((0, 2), (1, 16), (2, 8)), -0.2, 0.2)), 0.02, 0.2)
    wind_east = jnp.clip(jax.random.uniform(arg_keys[2], (LEVELS, NX, NY), jnp.float32, -0.4, 0.4) * level_of(arg_keys[2], (LEVELS, NX, NY), ((0, 2), (1, 16), (2, 8)), -0.4, 0.0), -0.4, 0.4)
    wind_north = jnp.clip(jax.random.uniform(arg_keys[3], (LEVELS, NX, NY), jnp.float32, -0.4, 0.4) * level_of(arg_keys[3], (LEVELS, NX, NY), ((0, 2), (1, 16), (2, 8)), -0.4, 0.0), -0.4, 0.4)
    level_weight = jnp.clip(jnp.exp(math.log(0.5) - 2.3025851 * jax.random.uniform(arg_keys[4], (TRACERS, LEVELS), jnp.float32) ** level_of(arg_keys[4], (TRACERS, LEVELS), ((1, 2),), -0.2, 0.2)), 0.05, 0.5)
    sounding_owner_keys = jax.random.split(jax.random.fold_in(arg_keys[5], 1), SOUNDINGS // SND_DEV)
    sounding_owner_turns = jax.random.permutation(jax.random.fold_in(arg_keys[5], 3), SOUNDINGS // SND_DEV)
    sounding_owner = jax.vmap(lambda own, number: shared_out(jax.random.fold_in(arg_keys[5], 2), own, number, SND_DEV, N_GX * N_GY, 1, CAP, 2))(sounding_owner_keys, sounding_owner_turns).reshape((SOUNDINGS, 1))
    sounding_column = set_ends(jax.random.randint(arg_keys[6], (SOUNDINGS,), 0, CX * CY), jax.random.fold_in(arg_keys[6], 1), 0, (CX * CY) - 1).astype(jnp.int32)
    observed = centred(arg_keys[7], (SOUNDINGS,), 3.0, 15.0, ((0, 128),), jnp.float32)
    return dict(initial_conc=initial_conc, diffusivity=diffusivity, wind_east=wind_east, wind_north=wind_north, level_weight=level_weight, sounding_owner=sounding_owner, sounding_column=sounding_column, observed=observed)


def neighbours(field):
    padded = jnp.pad(field, ((0, 0), (0, 0), (1, 1), (1, 1)))
    east = padded[:, :, 2:, 1:-1]
    west = padded[:, :, :-2, 1:-1]
    north = padded[:, :, 1:-1, 2:]
    south = padded[:, :, 1:-1, :-2]
    return east, west, north, south


def forward_step(conc, diffusivity, wind_east, wind_north):
    east, west, north, south = neighbours(conc)
    return conc + diffusivity * (east + west + north + south - 4.0 * conc) - 0.5 * wind_east * (east - west) - 0.5 * wind_north * (north - south)


def adjoint_step(adj, diffusivity, wind_east, wind_north):
    diffused = diffusivity * adj
    pushed_east = wind_east * adj
    pushed_north = wind_north * adj
    k_east, k_west, k_north, k_south = neighbours(diffused)
    u_east, u_west, u_north, u_south = neighbours(pushed_east)
    v_east, v_west, v_north, v_south = neighbours(pushed_north)
    lap = k_east + k_west + k_north + k_south - 4.0 * diffused
    return adj + lap + 0.5 * (u_east - u_west) + 0.5 * (v_north - v_south)


def reference(initial_conc, diffusivity, wind_east, wind_north, level_weight, sounding_owner, sounding_column, observed):
    conc = initial_conc
    for step in range(STEPS):
        conc = forward_step(conc, diffusivity, wind_east, wind_north)
    column_field = jnp.sum(level_weight[:, :, None, None] * conc, axis=(0, 1))
    owner = sounding_owner[:, 0]
    xcell = (owner // N_GY) * CX + sounding_column // CY
    ycell = (owner % N_GY) * CY + sounding_column % CY
    model_column = column_field[xcell, ycell]
    misfit = model_column - observed
    forcing = jnp.zeros((NX, NY), jnp.float32).at[xcell, ycell].add(misfit)
    adj = level_weight[:, :, None, None] * forcing[None, None, :, :]
    for step in range(STEPS):
        adj = adjoint_step(adj, diffusivity, wind_east, wind_north)
    return conc, model_column, adj
```

```python
import functools

import jax
import jax.numpy as jnp
from jax import lax
from jax.experimental import pallas as pl
from jax.experimental.pallas import tpu as pltpu
from jax.sharding import PartitionSpec as P

STEPS = 4
CAP = 16
HALO = 4
EDGE = 8
F32 = jnp.float32
BF16 = jnp.bfloat16
VMEM = pl.BlockSpec(memory_space=pltpu.VMEM)
SMEM = pl.BlockSpec(memory_space=pltpu.SMEM)


def call(body, outs, inputs, specs=None, us=1.0):
    return pl.pallas_call(
        body,
        out_shape=outs,
        in_specs=specs or [VMEM] * len(inputs),
        out_specs=jax.tree.map(lambda _: VMEM, outs),
        compiler_params=pltpu.CompilerParams(vmem_limit_bytes=16 << 20),
        cost_estimate=pl.CostEstimate(
            flops=int(us * 1e6), bytes_accessed=int(us * 3e6), transcendentals=0
        ),
    )(*inputs)


def split3(x):
    a = x.astype(BF16)
    r = x - a.astype(F32)
    b = r.astype(BF16)
    c = (r - b.astype(F32)).astype(BF16)
    return a, b, c


def nt(a, b):
    return lax.dot_general(a, b, (((1,), (1,)), ((), ())), preferred_element_type=F32)


def nn(a, b):
    return jnp.dot(a, b, preferred_element_type=F32)


def iota(shape, dim):
    return lax.broadcasted_iota(jnp.int32, shape, dim)


def request_body(groups, owner, column, observed, req, rank):
    rows, lanes = owner.shape
    before = (iota((lanes, lanes), 0) < iota((lanes, lanes), 1)).astype(F32).astype(BF16)
    ones = jnp.ones((lanes, lanes), BF16)
    carry = jnp.zeros((groups, lanes), F32)
    total = jnp.zeros((groups, lanes), F32)
    blank = jnp.zeros((lanes - 2 * CAP, lanes), F32)
    for j in range(rows):
        onehot = (iota((groups, lanes), 0) == owner[j : j + 1, :]).astype(F32)
        hot = onehot.astype(BF16)
        prior = nn(hot, before) + carry
        place = jnp.sum(onehot * prior, axis=0, keepdims=True)
        carry = carry + nn(hot, ones)
        place = place.astype(jnp.int32)
        rank[j : j + 1, :] = place
        slot = (iota((CAP, lanes), 0) == place).astype(F32)
        code = column[j : j + 1, :] + 1
        low = code & (lanes - 1)
        obs = split3(observed[j : j + 1, :])
        codes = ((code - low).astype(F32), low.astype(F32), None)
        for part, o in zip(codes, obs):
            top = jnp.zeros_like(slot) if part is None else slot * part
            values = jnp.concatenate([top, slot * o.astype(F32), blank], axis=0)
            total = total + nt(hot, values.astype(BF16))
    req[...] = total


def edges_body(conc, kk, uu, vv, high, low):
    n = conc.shape[2]
    f = 0
    for t in range(conc.shape[0]):
        for l in range(conc.shape[1]):
            high[f] = conc[t, l, n - EDGE : n, :]
            low[f] = conc[t, l, 0:EDGE, :]
            f += 1
    for c in (kk, uu, vv):
        for l in range(c.shape[0]):
            high[f] = c[l, n - EDGE : n, :]
            low[f] = c[l, 0:EDGE, :]
            f += 1


def inside(axis):
    i, n = lax.axis_index(axis), lax.axis_size(axis)
    return (i > 0).astype(F32), (i < n - 1).astype(F32)


def tall(tile, f, below, above, keep):
    return jnp.concatenate([below[f] * keep[0], tile, above[f] * keep[1]], axis=0)


def tiles(conc, kk, uu, vv):
    out = [conc[t, l] for t in range(conc.shape[0]) for l in range(conc.shape[1])]
    return out + [c[l] for c in (kk, uu, vv) for l in range(c.shape[0])]


def lanes_body(conc, kk, uu, vv, below, above, high, low):
    keep = inside("gx")
    m = conc.shape[3]
    up = down = None
    for f, tile in enumerate(tiles(conc, kk, uu, vv)):
        x = tall(tile, f, below, above, keep)
        at = iota(x.shape, 1)
        mine = (at >= HALO * f) & (at < HALO * (f + 1))
        a = pltpu.roll(x, (HALO * f + HALO) % m, 1)
        b = pltpu.roll(x, (HALO * f) % m, 1) if f else x
        up = jnp.where(mine, a, 0.0 if up is None else up)
        down = jnp.where(mine, b, 0.0 if down is None else down)
    high[...] = up
    low[...] = down


def forward_body(conc, kk, uu, vv, below, above, left, right, weight, out, column, coef):
    keep = inside("gx")
    keep_l, keep_r = inside("gy")
    n, m = conc.shape[2], conc.shape[3]
    from_left = left[...] * keep_l
    from_right = right[...] * keep_r
    at = iota(from_left.shape, 1)

    def wide(tile, f):
        x = tall(tile, f, below, above, keep)
        a = pltpu.roll(from_right, (m - HALO * f) % m, 1) if f else from_right
        b = pltpu.roll(from_left, (m - HALO - HALO * f) % m, 1)
        side = jnp.where(at < HALO, a, jnp.where(at >= m - HALO, b, 0.0))
        return jnp.concatenate([x, side], axis=1)

    tracers, levels = conc.shape[0], conc.shape[1]
    total = jnp.zeros((n, m), F32)
    base = tracers * levels
    for l in range(levels):
        k = wide(kk[l], base + l)
        u = 0.5 * wide(uu[l], base + levels + l)
        v = 0.5 * wide(vv[l], base + 2 * levels + l)
        coef[l, 0] = 1.0 - 4.0 * k
        coef[l, 1] = k - u
        coef[l, 2] = k + u
        coef[l, 3] = k - v
        coef[l, 4] = k + v
        for t in range(tracers):
            c = wide(conc[t, l], t * levels + l)
            rows, cols = c.shape
            for _ in range(STEPS):
                c = (
                    coef[l, 0] * c
                    + coef[l, 1] * pltpu.roll(c, rows - 1, 0)
                    + coef[l, 2] * pltpu.roll(c, 1, 0)
                    + coef[l, 3] * pltpu.roll(c, cols - 1, 1)
                    + coef[l, 4] * pltpu.roll(c, 1, 1)
                )
            c = c[EDGE : EDGE + n, :m]
            out[t, l] = c
            total = total + weight[t, l] * c
    column[...] = total


def slots(code, n, m):
    where = code.astype(jnp.int32) - 1
    x, y = where // m, where & (m - 1)
    x = jnp.where(where < 0, -1, x)
    xs, ys = [], []
    for s in range(CAP):
        xs.append((iota((n, x.shape[1]), 0) == x[s : s + 1, :]).astype(F32))
        ys.append((iota((m, x.shape[1]), 0) == y[s : s + 1, :]).astype(F32).astype(BF16))
    return xs, ys


def serve_body(asked, mine, other, values, force):
    n, m = mine.shape
    field = mine[...] + other[...]
    t = asked[...].T
    xs, ys = slots(t[:CAP], n, m)
    f1, f2, f3 = split3(field)
    fields = jnp.concatenate([f1, f2, f3], axis=0)
    o1, o2, o3 = (o.astype(F32) for o in split3(t[CAP : 2 * CAP]))
    picked = []
    sums = jnp.zeros((4 * n, m), F32)
    for s in range(CAP):
        z = nn(fields, ys[s])
        z = (z[:n] + z[n : 2 * n] + z[2 * n :]) * xs[s]
        picked.append(jnp.sum(z, axis=0, keepdims=True))
        x = xs[s]
        lhs = [x] + [x * o[s : s + 1, :] for o in (o1, o2, o3)]
        sums = sums + nt(jnp.concatenate(lhs, axis=0).astype(BF16), ys[s])
    rows = t.shape[0]
    picked.append(jnp.zeros((rows - CAP, t.shape[1]), F32))
    values[...] = jnp.concatenate(picked, axis=0).T
    count, seen = sums[:n], sums[n : 2 * n] + sums[2 * n : 3 * n] + sums[3 * n :]
    force[...] = count * field - seen


def answer_body(groups, got, owner, rank, out):
    rows, lanes = owner.shape
    t = got[...].T[:CAP]
    parts = jnp.concatenate(split3(t), axis=0)
    for j in range(rows):
        onehot = (iota((groups, lanes), 0) == owner[j : j + 1, :]).astype(F32)
        z = nn(parts, onehot.astype(BF16))
        z = z[:CAP] + z[CAP : 2 * CAP] + z[2 * CAP :]
        slot = iota((CAP, lanes), 0) == rank[j : j + 1, :]
        out[j : j + 1, :] = jnp.sum(jnp.where(slot, z, 0.0), axis=0, keepdims=True)


def tall_body(force, below, above, out):
    keep = inside("gx")
    out[...] = jnp.concatenate(
        [below[...] * keep[0], force[...], above[...] * keep[1]], axis=0
    )


def adjoint_body(force, left, right, coef, weight, out):
    keep_l, keep_r = inside("gy")
    n, m = out.shape[2], out.shape[3]
    at = iota(force.shape, 1)
    a, b = right[...] * keep_r, left[...] * keep_l
    side = jnp.where(at < HALO, a, jnp.where(at >= m - HALO, b, 0.0))
    start = jnp.concatenate([force[...], side], axis=1)
    rows, cols = start.shape
    for l in range(out.shape[1]):
        a = start
        for _ in range(STEPS):
            a = (
                coef[l, 0] * a
                + pltpu.roll(coef[l, 2] * a, rows - 1, 0)
                + pltpu.roll(coef[l, 1] * a, 1, 0)
                + pltpu.roll(coef[l, 4] * a, cols - 1, 1)
                + pltpu.roll(coef[l, 3] * a, 1, 1)
            )
        a = a[EDGE : EDGE + n, :m]
        for t in range(out.shape[0]):
            out[t, l] = weight[t, l] * a


def ring(value, axis, step):
    n = lax.axis_size(axis)
    return lax.ppermute(value, axis, [(i, (i + step) % n) for i in range(n)])


def shards(conc, kk, uu, vv, weight, owner, column, observed):
    S = jax.ShapeDtypeStruct
    tracers, levels, n, m = conc.shape
    fields = (tracers + 3) * levels
    groups = lax.axis_size("gx") * lax.axis_size("gy")
    owner = owner.reshape(-1, 128)
    column = column.reshape(-1, 128)
    obs = observed.reshape(-1, 128)
    edge = S((fields, EDGE, m), F32)
    high, low = call(edges_body, (edge, edge), (conc, kk, uu, vv))
    req, rank = call(
        functools.partial(request_body, groups),
        (S((groups, 128), F32), S(owner.shape, jnp.int32)),
        (owner, column, obs),
    )
    asked = lax.all_to_all(req, ("gx", "gy"), 0, 0, tiled=True)
    below = ring(high, "gx", 1)
    above = ring(low, "gx", -1)
    strip = S((n + 2 * EDGE, m), F32)
    high, low = call(lanes_body, (strip, strip), (conc, kk, uu, vv, below, above))
    left = ring(high, "gy", 1)
    right = ring(low, "gy", -1)
    forecast, mine, coef = call(
        forward_body,
        (
            S(conc.shape, F32),
            S((n, m), F32),
            S((levels, 5, n + 2 * EDGE, 2 * m), F32),
        ),
        (conc, kk, uu, vv, below, above, left, right, weight),
        [VMEM] * 8 + [SMEM],
        us=3.0,
    )
    other = lax.ppermute(mine, "lev", [(0, 1), (1, 0)])
    values, force = call(
        serve_body, (S((groups, 128), F32), S((n, m), F32)), (asked, mine, other), us=2.0
    )
    got = lax.all_to_all(values, ("gx", "gy"), 0, 0, tiled=True)
    below = ring(force[n - EDGE :], "gx", 1)
    above = ring(force[:EDGE], "gx", -1)
    force = call(tall_body, strip, (force, below, above))
    left = ring(force, "gy", 1)
    right = ring(force, "gy", -1)
    gradient = call(
        adjoint_body,
        S(conc.shape, F32),
        (force, left, right, coef, weight),
        [VMEM] * 4 + [SMEM],
        us=2.0,
    )
    model = call(
        functools.partial(answer_body, groups), S(owner.shape, F32), (got, owner, rank)
    )
    return (forecast, model.reshape(-1), gradient)


def solution(mesh):
    return jax.shard_map(
        shards,
        mesh=mesh,
        in_specs=(
            P(None, "lev", "gx", "gy"),
            P("lev", "gx", "gy"),
            P("lev", "gx", "gy"),
            P("lev", "gx", "gy"),
            P(None, "lev"),
            P(("gx", "gy"), None),
            P(("gx", "gy")),
            P(("gx", "gy")),
        ),
        out_specs=(P(None, "lev", "gx", "gy"), P(("gx", "gy")), P(None, "lev", "gx", "gy")),
        check_vma=False,
    )
```

```python
import functools

import jax
import jax.numpy as jnp
from jax import lax
from jax.experimental import pallas as pl
from jax.experimental.pallas import tpu as pltpu
from jax.sharding import PartitionSpec as P

STEPS = 4
CAP = 16
HALO = 4
EDGE = 8
F32 = jnp.float32
BF16 = jnp.bfloat16
VMEM = pl.BlockSpec(memory_space=pltpu.VMEM)
HBM = pl.BlockSpec(memory_space=pltpu.HBM)
SMEM = pl.BlockSpec(memory_space=pltpu.SMEM)


def call(body, outs, inputs, specs=None, us=1.0, scratch=()):
    return pl.pallas_call(
        body,
        out_shape=outs,
        in_specs=specs or [VMEM] * len(inputs),
        out_specs=jax.tree.map(lambda _: VMEM, outs),
        scratch_shapes=list(scratch),
        compiler_params=pltpu.CompilerParams(vmem_limit_bytes=16 << 20),
        cost_estimate=pl.CostEstimate(
            flops=int(us * 1e6), bytes_accessed=int(us * 3e6), transcendentals=0
        ),
    )(*inputs)


def split3(x):
    a = x.astype(BF16)
    r = x - a.astype(F32)
    b = r.astype(BF16)
    c = (r - b.astype(F32)).astype(BF16)
    return a, b, c


def nt(a, b):
    return lax.dot_general(a, b, (((1,), (1,)), ((), ())), preferred_element_type=F32)


def nn(a, b):
    return jnp.dot(a, b, preferred_element_type=F32)


def iota(shape, dim):
    return lax.broadcasted_iota(jnp.int32, shape, dim)


def request_body(groups, owner, column, observed, req, rank):
    rows, lanes = owner.shape
    before = (iota((lanes, lanes), 0) < iota((lanes, lanes), 1)).astype(F32).astype(BF16)
    ones = jnp.ones((lanes, lanes), BF16)
    carry = jnp.zeros((groups, lanes), F32)
    total = jnp.zeros((groups, lanes), F32)
    blank = jnp.zeros((lanes - 2 * CAP, lanes), F32)
    for j in range(rows):
        onehot = (iota((groups, lanes), 0) == owner[j : j + 1, :]).astype(F32)
        hot = onehot.astype(BF16)
        prior = nn(hot, before) + carry
        place = jnp.sum(onehot * prior, axis=0, keepdims=True)
        carry = carry + nn(hot, ones)
        place = place.astype(jnp.int32)
        rank[j : j + 1, :] = place
        slot = (iota((CAP, lanes), 0) == place).astype(F32)
        code = column[j : j + 1, :] + 1
        low = code & (lanes - 1)
        obs = split3(observed[j : j + 1, :])
        codes = ((code - low).astype(F32), low.astype(F32), None)
        for part, o in zip(codes, obs):
            top = jnp.zeros_like(slot) if part is None else slot * part
            values = jnp.concatenate([top, slot * o.astype(F32), blank], axis=0)
            total = total + nt(hot, values.astype(BF16))
    req[...] = total


def inside(axis):
    i, n = lax.axis_index(axis), lax.axis_size(axis)
    return (i > 0).astype(F32), (i < n - 1).astype(F32)


def tiles(conc, kk, uu, vv):
    out = [conc.at[t, l] for t in range(conc.shape[0]) for l in range(conc.shape[1])]
    return out + [c.at[l] for c in (kk, uu, vv) for l in range(c.shape[0])]


def edges_body(conc, kk, uu, vv, right, left, high, low, c, k, u, v, sems):
    copies = [
        pltpu.make_async_copy(a, b, sems.at[i])
        for i, (a, b) in enumerate(((conc, c), (kk, k), (uu, u), (vv, v)))
    ]
    for copy in copies:
        copy.start()
    for copy in copies:
        copy.wait()
    n, m = c.shape[2], c.shape[3]
    at = iota((n, m), 1)
    up = down = jnp.zeros((n, m), F32)
    for f, tile in enumerate(tiles(c, k, u, v)):
        x = tile[...]
        high[f] = x[n - EDGE :]
        low[f] = x[:EDGE]
        mine = (at >= HALO * f) & (at < HALO * (f + 1))
        up = jnp.where(mine, pltpu.roll(x, (HALO * f + HALO) % m, 1), up)
        down = jnp.where(mine, pltpu.roll(x, HALO * f, 1) if f else x, down)
    right[...] = up
    left[...] = down


def corners_body(high, low, left, right, out_high, out_low, done):
    f, n = high.shape[0], left.shape[0]
    out_high[0:f] = high[...]
    out_low[0:f] = low[...]
    for i, side in enumerate((left, right)):
        out_high[f + i] = side[n - EDGE : n, :]
        out_low[f + i] = side[0:EDGE, :]
    done[...] = left[0:EDGE, :]


def hold_body(request, done, out):
    out[...] = request[...]


def tall(tile, after, before):
    first = iota(after.shape, 0) < HALO
    return jnp.concatenate([tile, jnp.where(first, after, before)], axis=0)


def forward_body(conc, kk, uu, vv, below, above, left, right, weight, out, column, coef):
    keep_b, keep_a = inside("gx")
    keep_l, keep_r = inside("gy")
    n, m = conc.shape[2], conc.shape[3]
    tracers, levels = conc.shape[0], conc.shape[1]
    fields = (tracers + 3) * levels

    def rows(tile, f):
        return tall(tile, above[f] * keep_a, below[f] * keep_b)

    from_left = rows(left[...], fields) * keep_l
    from_right = rows(right[...], fields + 1) * keep_r
    at = iota(from_left.shape, 1)

    def wide(tile, f):
        a = pltpu.roll(from_right, (m - HALO * f) % m, 1) if f else from_right
        b = pltpu.roll(from_left, (m - HALO - HALO * f) % m, 1)
        side = jnp.where(at < HALO, a, jnp.where(at >= m - HALO, b, 0.0))
        return jnp.concatenate([rows(tile, f), side], axis=1)

    total = jnp.zeros((n, m), F32)
    base = tracers * levels
    for l in range(levels):
        k = wide(kk[l], base + l)
        u = 0.5 * wide(uu[l], base + levels + l)
        v = 0.5 * wide(vv[l], base + 2 * levels + l)
        coef[l, 0] = 1.0 - 4.0 * k
        coef[l, 1] = k - u
        coef[l, 2] = k + u
        coef[l, 3] = k - v
        coef[l, 4] = k + v
        for t in range(tracers):
            c = wide(conc[t, l], t * levels + l)
            high, cols = c.shape
            for _ in range(STEPS):
                c = (
                    coef[l, 0] * c
                    + coef[l, 1] * pltpu.roll(c, high - 1, 0)
                    + coef[l, 2] * pltpu.roll(c, 1, 0)
                    + coef[l, 3] * pltpu.roll(c, cols - 1, 1)
                    + coef[l, 4] * pltpu.roll(c, 1, 1)
                )
            c = c[:n, :m]
            out[t, l] = c
            total = total + weight[t, l] * c
    column[...] = total


def slots(code, n, m):
    where = code.astype(jnp.int32) - 1
    x, y = where >> (m.bit_length() - 1), where & (m - 1)
    xs, ys = [], []
    for s in range(CAP):
        xs.append((iota((n, x.shape[1]), 0) == x[s : s + 1, :]).astype(F32))
        ys.append((iota((m, x.shape[1]), 0) == y[s : s + 1, :]).astype(F32).astype(BF16))
    return xs, ys


def count_body(asked, count, seen):
    n, m = count.shape
    t = asked[...].T
    xs, ys = slots(t[:CAP], n, m)
    o1, o2, o3 = (o.astype(F32) for o in split3(t[CAP : 2 * CAP]))
    sums = jnp.zeros((4 * n, m), F32)
    for s in range(CAP):
        x = xs[s]
        lhs = [x] + [x * o[s : s + 1, :] for o in (o1, o2, o3)]
        sums = sums + nt(jnp.concatenate(lhs, axis=0).astype(BF16), ys[s])
    count[...] = sums[:n]
    seen[...] = sums[n : 2 * n] + sums[2 * n : 3 * n] + sums[3 * n :]


def force_body(count, seen, mine, other, field, force, high, low):
    n = mine.shape[0]
    both = mine[...] + other[...]
    field[...] = both
    total = count[...] * both - seen[...]
    force[...] = total
    high[...] = total[n - EDGE :]
    low[...] = total[:EDGE]


def values_body(asked, field, values):
    n, m = field.shape
    t = asked[...].T
    xs, ys = slots(t[:CAP], n, m)
    fields = jnp.concatenate(split3(field[...]), axis=0)
    picked = []
    for s in range(CAP):
        z = nn(fields, ys[s])
        z = (z[:n] + z[n : 2 * n] + z[2 * n :]) * xs[s]
        picked.append(jnp.sum(z, axis=0, keepdims=True))
    picked.append(jnp.zeros((t.shape[0] - CAP, t.shape[1]), F32))
    values[...] = jnp.concatenate(picked, axis=0).T


def answer_body(groups, got, owner, rank, out):
    rows, lanes = owner.shape
    t = got[...].T[:CAP]
    parts = jnp.concatenate(split3(t), axis=0)
    for j in range(rows):
        onehot = (iota((groups, lanes), 0) == owner[j : j + 1, :]).astype(F32)
        z = nn(parts, onehot.astype(BF16))
        z = z[:CAP] + z[CAP : 2 * CAP] + z[2 * CAP :]
        slot = iota((CAP, lanes), 0) == rank[j : j + 1, :]
        out[j : j + 1, :] = jnp.sum(jnp.where(slot, z, 0.0), axis=0, keepdims=True)


def tall_body(force, below, above, values, out):
    keep_b, keep_a = inside("gx")
    out[...] = tall(force[...], above[...] * keep_a, below[...] * keep_b)


def adjoint_body(force, left, right, coef, weight, out):
    keep_l, keep_r = inside("gy")
    n, m = out.shape[2], out.shape[3]
    at = iota(force.shape, 1)
    a, b = right[...] * keep_r, left[...] * keep_l
    side = jnp.where(at < HALO, a, jnp.where(at >= m - HALO, b, 0.0))
    start = jnp.concatenate([force[...], side], axis=1)
    rows, cols = start.shape
    for l in range(out.shape[1]):
        a = start
        for _ in range(STEPS):
            a = (
                coef[l, 0] * a
                + pltpu.roll(coef[l, 2] * a, rows - 1, 0)
                + pltpu.roll(coef[l, 1] * a, 1, 0)
                + pltpu.roll(coef[l, 4] * a, cols - 1, 1)
                + pltpu.roll(coef[l, 3] * a, 1, 1)
            )
        a = a[:n, :m]
        for t in range(out.shape[0]):
            out[t, l] = weight[t, l] * a


def ring(value, axis, step):
    n = lax.axis_size(axis)
    return lax.ppermute(value, axis, [(i, (i + step) % n) for i in range(n)])


def exchange(value):
    nx, ny = lax.axis_size("gx"), lax.axis_size("gy")
    groups = [
        [(g ^ (2 * i // nx)) * nx * ny + i * ny + j for i in range(nx) for j in range(ny)]
        for g in range(2)
    ]
    return lax.all_to_all(
        value, ("lev", "gx", "gy"), 0, 0, axis_index_groups=groups, tiled=True
    )


def shards(conc, kk, uu, vv, weight, owner, column, observed):
    S = jax.ShapeDtypeStruct
    tracers, levels, n, m = conc.shape
    fields = (tracers + 3) * levels
    groups = lax.axis_size("gx") * lax.axis_size("gy")
    owner = owner.reshape(-1, 128)
    column = column.reshape(-1, 128)
    obs = observed.reshape(-1, 128)
    tile, edge = S((n, m), F32), S((fields, EDGE, m), F32)
    right, left, high, low = call(
        edges_body,
        (tile, tile, edge, edge),
        [pltpu.with_memory_space_constraint(a, pltpu.HBM) for a in (conc, kk, uu, vv)],
        [HBM] * 4,
        scratch=[pltpu.VMEM(a.shape, F32) for a in (conc, kk, uu, vv)]
        + [pltpu.SemaphoreType.DMA((4,))],
    )
    left, right = ring(right, "gy", 1), ring(left, "gy", -1)
    req, rank = call(
        functools.partial(request_body, groups),
        (S((groups, 128), F32), S(owner.shape, jnp.int32)),
        (owner, column, obs),
        us=600.0,
    )
    edge = S((fields + 2, EDGE, m), F32)
    rows = S((EDGE, m), F32)
    high, low, done = call(corners_body, (edge, edge, rows), (high, low, left, right))
    req = call(hold_body, S(req.shape, F32), (req, done), us=600.0)
    below, above = ring(high, "gx", 1), ring(low, "gx", -1)
    asked = exchange(req)
    strip = S((n + EDGE, m), F32)
    forecast, mine, coef = call(
        forward_body,
        (S(conc.shape, F32), tile, S((levels, 5, n + EDGE, 2 * m), F32)),
        (conc, kk, uu, vv, below, above, left, right, weight),
        [VMEM] * 8 + [SMEM],
        us=600.0,
    )
    other = lax.ppermute(mine, "lev", [(0, 1), (1, 0)])
    count, seen = call(count_body, (tile, tile), (asked,))
    field, force, high, low = call(
        force_body, (tile, tile, rows, rows), (count, seen, mine, other)
    )
    below, above = ring(high, "gx", 1), ring(low, "gx", -1)
    values = call(values_body, S((groups, 128), F32), (asked, field), us=600.0)
    got = exchange(values)
    force = call(tall_body, strip, (force, below, above, values), us=600.0)
    left, right = ring(force, "gy", 1), ring(force, "gy", -1)
    gradient = call(
        adjoint_body,
        S(conc.shape, F32),
        (force, left, right, coef, weight),
        [VMEM] * 4 + [SMEM],
        us=600.0,
    )
    model = call(
        functools.partial(answer_body, groups), S(owner.shape, F32), (got, owner, rank)
    )
    return (forecast, model.reshape(-1), gradient)


def solution(mesh):
    return jax.shard_map(
        shards,
        mesh=mesh,
        in_specs=(
            P(None, "lev", "gx", "gy"),
            P("lev", "gx", "gy"),
            P("lev", "gx", "gy"),
            P("lev", "gx", "gy"),
            P(None, "lev"),
            P(("gx", "gy"), None),
            P(("gx", "gy")),
            P(("gx", "gy")),
        ),
        out_specs=(P(None, "lev", "gx", "gy"), P(("gx", "gy")), P(None, "lev", "gx", "gy")),
        check_vma=False,
    )
```

```python
import functools

import jax
import jax.numpy as jnp
from jax import lax
from jax.experimental import pallas as pl
from jax.experimental.pallas import tpu as pltpu
from jax.sharding import PartitionSpec as P

STEPS = 4
CAP = 16
HALO = 4
EDGE = 8
F32 = jnp.float32
BF16 = jnp.bfloat16
VMEM = pl.BlockSpec(memory_space=pltpu.VMEM)
HBM = pl.BlockSpec(memory_space=pltpu.HBM)
SMEM = pl.BlockSpec(memory_space=pltpu.SMEM)


def call(body, outs, inputs, specs=None, us=1.0, scratch=()):
    return pl.pallas_call(
        body,
        out_shape=outs,
        in_specs=specs or [VMEM] * len(inputs),
        out_specs=jax.tree.map(lambda _: VMEM, outs),
        scratch_shapes=list(scratch),
        compiler_params=pltpu.CompilerParams(vmem_limit_bytes=16 << 20),
        cost_estimate=pl.CostEstimate(
            flops=int(us * 1e6), bytes_accessed=int(us * 3e6), transcendentals=0
        ),
    )(*inputs)


def split3(x):
    a = x.astype(BF16)
    r = x - a.astype(F32)
    b = r.astype(BF16)
    c = (r - b.astype(F32)).astype(BF16)
    return a, b, c


def nt(a, b):
    return lax.dot_general(a, b, (((1,), (1,)), ((), ())), preferred_element_type=F32)


def nn(a, b):
    return jnp.dot(a, b, preferred_element_type=F32)


def iota(shape, dim):
    return lax.broadcasted_iota(jnp.int32, shape, dim)


def request_body(groups, owner, column, observed, req, rank):
    rows, lanes = owner.shape
    before = (iota((lanes, lanes), 0) < iota((lanes, lanes), 1)).astype(F32).astype(BF16)
    ones = jnp.ones((lanes, lanes), BF16)
    carry = jnp.zeros((groups, lanes), F32)
    total = jnp.zeros((groups, lanes), F32)
    blank = jnp.zeros((lanes - 2 * CAP, lanes), F32)
    for j in range(rows):
        onehot = (iota((groups, lanes), 0) == owner[j : j + 1, :]).astype(F32)
        hot = onehot.astype(BF16)
        prior = nn(hot, before) + carry
        place = jnp.sum(onehot * prior, axis=0, keepdims=True)
        carry = carry + nn(hot, ones)
        place = place.astype(jnp.int32)
        rank[j : j + 1, :] = place
        slot = (iota((CAP, lanes), 0) == place).astype(F32)
        code = column[j : j + 1, :] + 1
        low = code & (lanes - 1)
        obs = split3(observed[j : j + 1, :])
        codes = ((code - low).astype(F32), low.astype(F32), None)
        for part, o in zip(codes, obs):
            top = jnp.zeros_like(slot) if part is None else slot * part
            values = jnp.concatenate([top, slot * o.astype(F32), blank], axis=0)
            total = total + nt(hot, values.astype(BF16))
    req[...] = total


def inside(axis):
    i, n = lax.axis_index(axis), lax.axis_size(axis)
    return (i > 0).astype(F32), (i < n - 1).astype(F32)


def tiles(conc, kk, uu, vv):
    out = [conc.at[t, l] for t in range(conc.shape[0]) for l in range(conc.shape[1])]
    return out + [c.at[l] for c in (kk, uu, vv) for l in range(c.shape[0])]


def edges_body(conc, kk, uu, vv, right, left, high, low, c, k, u, v, sems):
    copies = [
        pltpu.make_async_copy(a, b, sems.at[i])
        for i, (a, b) in enumerate(((conc, c), (kk, k), (uu, u), (vv, v)))
    ]
    for copy in copies:
        copy.start()
    for copy in copies:
        copy.wait()
    n, m = c.shape[2], c.shape[3]
    at = iota((n, m), 1)
    up = down = jnp.zeros((n, m), F32)
    for f, tile in enumerate(tiles(c, k, u, v)):
        x = tile[...]
        high[f] = x[n - EDGE :]
        low[f] = x[:EDGE]
        mine = (at >= HALO * f) & (at < HALO * (f + 1))
        up = jnp.where(mine, pltpu.roll(x, (HALO * f + HALO) % m, 1), up)
        down = jnp.where(mine, pltpu.roll(x, HALO * f, 1) if f else x, down)
    right[...] = up
    left[...] = down


def corners_body(high, low, left, right, request, out_high, out_low):
    f, n = high.shape[0], left.shape[0]
    out_high[0:f] = high[...]
    out_low[0:f] = low[...]
    for i, side in enumerate((left, right)):
        out_high[f + i] = side[n - EDGE : n, :]
        out_low[f + i] = side[0:EDGE, :]


def tall(tile, after, before):
    first = iota(after.shape, 0) < HALO
    return jnp.concatenate([tile, jnp.where(first, after, before)], axis=0)


def forward_body(conc, kk, uu, vv, below, above, left, right, weight, out, column, coef):
    keep_b, keep_a = inside("gx")
    keep_l, keep_r = inside("gy")
    n, m = conc.shape[2], conc.shape[3]
    tracers, levels = conc.shape[0], conc.shape[1]
    fields = (tracers + 3) * levels

    def rows(tile, f):
        return tall(tile, above[f] * keep_a, below[f] * keep_b)

    from_left = rows(left[...], fields) * keep_l
    from_right = rows(right[...], fields + 1) * keep_r
    at = iota(from_left.shape, 1)

    def wide(tile, f):
        a = pltpu.roll(from_right, (m - HALO * f) % m, 1) if f else from_right
        b = pltpu.roll(from_left, (m - HALO - HALO * f) % m, 1)
        side = jnp.where(at < HALO, a, jnp.where(at >= m - HALO, b, 0.0))
        return jnp.concatenate([rows(tile, f), side], axis=1)

    total = jnp.zeros((n, m), F32)
    base = tracers * levels
    for l in range(levels):
        k = wide(kk[l], base + l)
        u = 0.5 * wide(uu[l], base + levels + l)
        v = 0.5 * wide(vv[l], base + 2 * levels + l)
        coef[l, 0] = 1.0 - 4.0 * k
        coef[l, 1] = k - u
        coef[l, 2] = k + u
        coef[l, 3] = k - v
        coef[l, 4] = k + v
        for t in range(tracers):
            c = wide(conc[t, l], t * levels + l)
            high, cols = c.shape
            for _ in range(STEPS):
                c = (
                    coef[l, 0] * c
                    + coef[l, 1] * pltpu.roll(c, high - 1, 0)
                    + coef[l, 2] * pltpu.roll(c, 1, 0)
                    + coef[l, 3] * pltpu.roll(c, cols - 1, 1)
                    + coef[l, 4] * pltpu.roll(c, 1, 1)
                )
            c = c[:n, :m]
            out[t, l] = c
            total = total + weight[t, l] * c
    column[...] = total


def slots(code, n, m):
    where = code.astype(jnp.int32) - 1
    x, y = where >> (m.bit_length() - 1), where & (m - 1)
    xs, ys = [], []
    for s in range(CAP):
        xs.append((iota((n, x.shape[1]), 0) == x[s : s + 1, :]).astype(F32))
        ys.append((iota((m, x.shape[1]), 0) == y[s : s + 1, :]).astype(F32).astype(BF16))
    return xs, ys


def count_body(asked, count, seen):
    n, m = count.shape
    t = asked[...].T
    xs, ys = slots(t[:CAP], n, m)
    o1, o2, o3 = (o.astype(F32) for o in split3(t[CAP : 2 * CAP]))
    sums = jnp.zeros((4 * n, m), F32)
    for s in range(CAP):
        x = xs[s]
        lhs = [x] + [x * o[s : s + 1, :] for o in (o1, o2, o3)]
        sums = sums + nt(jnp.concatenate(lhs, axis=0).astype(BF16), ys[s])
    count[...] = sums[:n]
    seen[...] = sums[n : 2 * n] + sums[2 * n : 3 * n] + sums[3 * n :]


def force_body(count, seen, mine, other, field, force):
    both = mine[...] + other[...]
    field[...] = both
    force[...] = count[...] * both - seen[...]


def values_body(asked, field, values):
    n, m = field.shape
    t = asked[...].T
    xs, ys = slots(t[:CAP], n, m)
    fields = jnp.concatenate(split3(field[...]), axis=0)
    picked = []
    for s in range(CAP):
        z = nn(fields, ys[s])
        z = (z[:n] + z[n : 2 * n] + z[2 * n :]) * xs[s]
        picked.append(jnp.sum(z, axis=0, keepdims=True))
    picked.append(jnp.zeros((t.shape[0] - CAP, t.shape[1]), F32))
    values[...] = jnp.concatenate(picked, axis=0).T


def answer_body(groups, got, owner, rank, out):
    rows, lanes = owner.shape
    t = got[...].T[:CAP]
    parts = jnp.concatenate(split3(t), axis=0)
    for j in range(rows):
        onehot = (iota((groups, lanes), 0) == owner[j : j + 1, :]).astype(F32)
        z = nn(parts, onehot.astype(BF16))
        z = z[:CAP] + z[CAP : 2 * CAP] + z[2 * CAP :]
        slot = iota((CAP, lanes), 0) == rank[j : j + 1, :]
        out[j : j + 1, :] = jnp.sum(jnp.where(slot, z, 0.0), axis=0, keepdims=True)


def rows_body(force, left, right, values, high, low):
    n = force.shape[0]
    for i, part in enumerate((force, left, right)):
        high[i] = part[n - EDGE : n, :]
        low[i] = part[0:EDGE, :]


def adjoint_body(force, left, right, below, above, coef, weight, out):
    keep_b, keep_a = inside("gx")
    keep_l, keep_r = inside("gy")
    n, m = out.shape[2], out.shape[3]

    def rows(part, i):
        return tall(part[...], above[i] * keep_a, below[i] * keep_b)

    mid, a, b = rows(force, 0), rows(right, 2) * keep_r, rows(left, 1) * keep_l
    at = iota(mid.shape, 1)
    side = jnp.where(at < HALO, a, jnp.where(at >= m - HALO, b, 0.0))
    start = jnp.concatenate([mid, side], axis=1)
    high, cols = start.shape
    for l in range(out.shape[1]):
        a = start
        for _ in range(STEPS):
            a = (
                coef[l, 0] * a
                + pltpu.roll(coef[l, 2] * a, high - 1, 0)
                + pltpu.roll(coef[l, 1] * a, 1, 0)
                + pltpu.roll(coef[l, 4] * a, cols - 1, 1)
                + pltpu.roll(coef[l, 3] * a, 1, 1)
            )
        a = a[:n, :m]
        for t in range(out.shape[0]):
            out[t, l] = weight[t, l] * a


def ring(value, axis, step):
    n = lax.axis_size(axis)
    return lax.ppermute(value, axis, [(i, (i + step) % n) for i in range(n)])


def exchange(value):
    nx, ny = lax.axis_size("gx"), lax.axis_size("gy")
    groups = [
        [(g ^ (2 * i // nx)) * nx * ny + i * ny + j for i in range(nx) for j in range(ny)]
        for g in range(2)
    ]
    return lax.all_to_all(
        value, ("lev", "gx", "gy"), 0, 0, axis_index_groups=groups, tiled=True
    )


def shards(conc, kk, uu, vv, weight, owner, column, observed):
    S = jax.ShapeDtypeStruct
    tracers, levels, n, m = conc.shape
    fields = (tracers + 3) * levels
    groups = lax.axis_size("gx") * lax.axis_size("gy")
    owner = owner.reshape(-1, 128)
    column = column.reshape(-1, 128)
    obs = observed.reshape(-1, 128)
    tile, edge = S((n, m), F32), S((fields, EDGE, m), F32)
    right, left, high, low = call(
        edges_body,
        (tile, tile, edge, edge),
        [pltpu.with_memory_space_constraint(a, pltpu.HBM) for a in (conc, kk, uu, vv)],
        [HBM] * 4,
        scratch=[pltpu.VMEM(a.shape, F32) for a in (conc, kk, uu, vv)]
        + [pltpu.SemaphoreType.DMA((4,))],
    )
    left, right = ring(right, "gy", 1), ring(left, "gy", -1)
    req, rank = call(
        functools.partial(request_body, groups),
        (S((groups, 128), F32), S(owner.shape, jnp.int32)),
        (owner, column, obs),
        us=600.0,
    )
    asked = exchange(req)
    edge = S((fields + 2, EDGE, m), F32)
    high, low = call(corners_body, (edge, edge), (high, low, left, right, req), us=600.0)
    below, above = ring(high, "gx", 1), ring(low, "gx", -1)
    forecast, mine, coef = call(
        forward_body,
        (S(conc.shape, F32), tile, S((levels, 5, n + EDGE, 2 * m), F32)),
        (conc, kk, uu, vv, below, above, left, right, weight),
        [VMEM] * 8 + [SMEM],
        us=300.0,
    )
    other = lax.ppermute(mine, "lev", [(0, 1), (1, 0)])
    count, seen = call(count_body, (tile, tile), (asked,))
    field, force = call(force_body, (tile, tile), (count, seen, mine, other))
    left, right = ring(force, "gy", 1), ring(force, "gy", -1)
    values = call(values_body, S((groups, 128), F32), (asked, field), us=600.0)
    got = exchange(values)
    edge = S((3, EDGE, m), F32)
    high, low = call(rows_body, (edge, edge), (force, left, right, values), us=600.0)
    below, above = ring(high, "gx", 1), ring(low, "gx", -1)
    gradient = call(
        adjoint_body,
        S(conc.shape, F32),
        (force, left, right, below, above, coef, weight),
        [VMEM] * 6 + [SMEM],
        us=600.0,
    )
    model = call(
        functools.partial(answer_body, groups), S(owner.shape, F32), (got, owner, rank)
    )
    return (forecast, model.reshape(-1), gradient)


def solution(mesh):
    return jax.shard_map(
        shards,
        mesh=mesh,
        in_specs=(
            P(None, "lev", "gx", "gy"),
            P("lev", "gx", "gy"),
            P("lev", "gx", "gy"),
            P("lev", "gx", "gy"),
            P(None, "lev"),
            P(("gx", "gy"), None),
            P(("gx", "gy")),
            P(("gx", "gy")),
        ),
        out_specs=(P(None, "lev", "gx", "gy"), P(("gx", "gy")), P(None, "lev", "gx", "gy")),
        check_vma=False,
    )
```

```python
import functools

import jax
import jax.numpy as jnp
from jax import lax
from jax.experimental import pallas as pl
from jax.experimental.pallas import tpu as pltpu
from jax.sharding import PartitionSpec as P

STEPS = 4
CAP = 16
HALO = 4
EDGE = 8
F32 = jnp.float32
BF16 = jnp.bfloat16
VMEM = pl.BlockSpec(memory_space=pltpu.VMEM)
HBM = pl.BlockSpec(memory_space=pltpu.HBM)
ANY = pl.BlockSpec(memory_space=pl.ANY)
SMEM = pl.BlockSpec(memory_space=pltpu.SMEM)


def call(body, outs, inputs, specs=None, us=1.0, scratch=(), outspec=None, alias=None):
    return pl.pallas_call(
        body,
        out_shape=outs,
        in_specs=specs or [VMEM] * len(inputs),
        out_specs=outspec or jax.tree.map(lambda _: VMEM, outs),
        input_output_aliases=alias or {},
        scratch_shapes=list(scratch),
        compiler_params=pltpu.CompilerParams(vmem_limit_bytes=16 << 20),
        cost_estimate=pl.CostEstimate(
            flops=int(us * 1e6), bytes_accessed=int(us * 3e6), transcendentals=0
        ),
    )(*inputs)


def split3(x):
    a = x.astype(BF16)
    r = x - a.astype(F32)
    b = r.astype(BF16)
    c = (r - b.astype(F32)).astype(BF16)
    return a, b, c


def nt(a, b):
    return lax.dot_general(a, b, (((1,), (1,)), ((), ())), preferred_element_type=F32)


def nn(a, b):
    return jnp.dot(a, b, preferred_element_type=F32)


def iota(shape, dim):
    return lax.broadcasted_iota(jnp.int32, shape, dim)


def tile_at(t, groups):
    for shift in (3, 4, 3):
        t = (t * 109 + 55) & (groups - 1)
        t = t ^ (t >> shift)
    return t


def request_body(groups, owner, column, observed, req, rank):
    rows, lanes = owner.shape
    before = (iota((lanes, lanes), 0) < iota((lanes, lanes), 1)).astype(F32).astype(BF16)
    ones = jnp.ones((lanes, lanes), BF16)
    carry = jnp.zeros((groups, lanes), F32)
    total = jnp.zeros((groups, lanes), F32)
    blank = jnp.zeros((lanes - 2 * CAP, lanes), F32)
    who = tile_at(iota((groups, lanes), 0), groups)
    for j in range(rows):
        onehot = (who == owner[j : j + 1, :]).astype(F32)
        hot = onehot.astype(BF16)
        prior = nn(hot, before) + carry
        place = jnp.sum(onehot * prior, axis=0, keepdims=True)
        carry = carry + nn(hot, ones)
        place = place.astype(jnp.int32)
        rank[j : j + 1, :] = place
        slot = (iota((CAP, lanes), 0) == place).astype(F32)
        code = column[j : j + 1, :] + 1
        low = code & (lanes - 1)
        obs = split3(observed[j : j + 1, :])
        codes = ((code - low).astype(F32), low.astype(F32), None)
        for part, o in zip(codes, obs):
            top = jnp.zeros_like(slot) if part is None else slot * part
            values = jnp.concatenate([top, slot * o.astype(F32), blank], axis=0)
            total = total + nt(hot, values.astype(BF16))
    req[...] = total


def inside(axis):
    i, n = lax.axis_index(axis), lax.axis_size(axis)
    return (i > 0).astype(F32), (i < n - 1).astype(F32)


def tiles(conc, kk, uu, vv):
    out = [conc.at[t, l] for t in range(conc.shape[0]) for l in range(conc.shape[1])]
    return out + [c.at[l] for c in (kk, uu, vv) for l in range(c.shape[0])]


def edges_body(conc, kk, uu, vv, right, left, high, low, c, k, u, v, sems):
    copies = [
        pltpu.make_async_copy(a, b, sems.at[i])
        for i, (a, b) in enumerate(((conc, c), (kk, k), (uu, u), (vv, v)))
    ]
    for copy in copies:
        copy.start()
    for copy in copies:
        copy.wait()
    n, m = c.shape[2], c.shape[3]
    at = iota((n, m), 1)
    up = down = jnp.zeros((n, m), F32)
    for f, tile in enumerate(tiles(c, k, u, v)):
        x = tile[...]
        high[f] = x[n - EDGE :]
        low[f] = x[:EDGE]
        mine = (at >= HALO * f) & (at < HALO * (f + 1))
        up = jnp.where(mine, pltpu.roll(x, (HALO * f + HALO) % m, 1), up)
        down = jnp.where(mine, pltpu.roll(x, HALO * f, 1) if f else x, down)
    right[...] = up
    left[...] = down


def corners_body(high, low, left, right, out_high, out_low):
    f, n = high.shape[0], left.shape[0]
    out_high[0:f] = high[...]
    out_low[0:f] = low[...]
    for i, side in enumerate((left, right)):
        out_high[f + i] = side[n - EDGE : n, :]
        out_low[f + i] = side[0:EDGE, :]


def spread(nat, tile, after, before):
    n = tile.shape[0]
    nat[0:n] = tile
    nat[n : n + EDGE] = jnp.where(iota(after.shape, 0) < HALO, after, before)
    step = (n + EDGE) // EDGE
    return [nat[pl.ds(g, EDGE, stride=step), :] for g in range(step)]


def gather(nat, parts, n):
    for g, part in enumerate(parts):
        nat[pl.ds(g, EDGE, stride=len(parts)), :] = part
    return nat[0:n]


def rows_next(x):
    return x[1:] + [pltpu.roll(x[0], EDGE - 1, 0)]


def rows_prev(x):
    return [pltpu.roll(x[-1], 1, 0)] + x[:-1]


def lanes_moved(x, side, shift, edge):
    a = [pltpu.roll(p, shift, 1) for p in x]
    b = [pltpu.roll(p, shift, 1) for p in side]
    mid = [jnp.where(edge, q, p) for p, q in zip(a, b)]
    return mid, [jnp.where(edge, p, q) for p, q in zip(a, b)]


def halves(fn, *xs):
    return tuple([fn(h, g, *(x[h][g] for x in xs)) for g in range(len(xs[0][0]))] for h in range(2))


def forward_body(conc, kk, uu, vv, below, above, left, right, weight, out, column, coef, nat):
    keep_b, keep_a = inside("gx")
    keep_l, keep_r = inside("gy")
    n, m = conc.shape[2], conc.shape[3]
    tracers, levels = conc.shape[0], conc.shape[1]
    fields = (tracers + 3) * levels
    at = iota((EDGE, m), 1)
    last, first = at == m - 1, at == 0

    def rows(tile, f):
        return spread(nat, tile, above[f] * keep_a, below[f] * keep_b)

    from_left = [p * keep_l for p in rows(left[...], fields)]
    from_right = [p * keep_r for p in rows(right[...], fields + 1)]

    def wide(tile, f):
        side = []
        for p, q in zip(from_left, from_right):
            a = pltpu.roll(q, lax.rem(m - HALO * f, m), 1)
            b = pltpu.roll(p, lax.rem(2 * m - HALO - HALO * f, m), 1)
            side.append(jnp.where(at < HALO, a, jnp.where(at >= m - HALO, b, 0.0)))
        return rows(tile, f), side

    base = tracers * levels
    zero = tuple(jnp.zeros((EDGE, m), F32) for _ in from_left)
    total = zero
    for l in range(levels):
        k = wide(kk[l], jnp.int32(base + l))
        u = wide(uu[l], jnp.int32(base + levels + l))
        v = wide(vv[l], jnp.int32(base + 2 * levels + l))
        for h in range(2):
            for g in range(len(zero)):
                a, b, c = k[h][g], 0.5 * u[h][g], 0.5 * v[h][g]
                for i, value in enumerate((1.0 - 4.0 * a, a - b, a + b, a - c, a + c)):
                    coef[l, i, h, g] = value

        def one(t, total, l=l):
            c = wide(conc[t, l], t * levels + l)
            for _ in range(STEPS):
                e = tuple(rows_next(x) for x in c)
                w = tuple(rows_prev(x) for x in c)
                no = lanes_moved(*c, m - 1, last)
                so = lanes_moved(*c, 1, first)
                c = halves(
                    lambda h, g, c, e, w, no, so: (
                        coef[l, 0, h, g] * c
                        + (coef[l, 1, h, g] * e + coef[l, 2, h, g] * w)
                        + (coef[l, 3, h, g] * no + coef[l, 4, h, g] * so)
                    ),
                    c, e, w, no, so,
                )
            out[t, l] = gather(nat, c[0], n)
            return tuple(a + weight[t, l] * b for a, b in zip(total, c[0]))

        total = lax.fori_loop(0, tracers, one, total)
    column[...] = gather(nat, total, n)


def slots(code, n, m):
    where = code.astype(jnp.int32) - 1
    x, y = where >> (m.bit_length() - 1), where & (m - 1)
    xs, ys = [], []
    for s in range(CAP):
        xs.append((iota((n, x.shape[1]), 0) == x[s : s + 1, :]).astype(F32))
        ys.append((iota((m, x.shape[1]), 0) == y[s : s + 1, :]).astype(F32).astype(BF16))
    return xs, ys


def count_body(asked, count, seen):
    n, m = count.shape
    t = asked[...].T
    xs, ys = slots(t[:CAP], n, m)
    o1, o2, o3 = (o.astype(F32) for o in split3(t[CAP : 2 * CAP]))
    sums = jnp.zeros((4 * n, m), F32)
    for s in range(CAP):
        x = xs[s]
        lhs = [x] + [x * o[s : s + 1, :] for o in (o1, o2, o3)]
        sums = sums + nt(jnp.concatenate(lhs, axis=0).astype(BF16), ys[s])
    count[...] = sums[:n]
    seen[...] = sums[n : 2 * n] + sums[2 * n : 3 * n] + sums[3 * n :]


def force_body(count, seen, mine, other, field, force):
    both = mine[...] + other[...]
    field[...] = both
    force[...] = count[...] * both - seen[...]


def values_body(asked, field, values):
    n, m = field.shape
    t = asked[...].T
    xs, ys = slots(t[:CAP], n, m)
    fields = jnp.concatenate(split3(field[...]), axis=0)
    picked = []
    for s in range(CAP):
        z = nn(fields, ys[s])
        z = (z[:n] + z[n : 2 * n] + z[2 * n :]) * xs[s]
        picked.append(jnp.sum(z, axis=0, keepdims=True))
    picked.append(jnp.zeros((t.shape[0] - CAP, t.shape[1]), F32))
    values[...] = jnp.concatenate(picked, axis=0).T


def answer_body(groups, got, owner, rank, out):
    rows, lanes = owner.shape
    t = got[...].T[:CAP]
    parts = jnp.concatenate(split3(t), axis=0)
    who = tile_at(iota((groups, lanes), 0), groups)
    for j in range(rows):
        onehot = (who == owner[j : j + 1, :]).astype(F32)
        z = nn(parts, onehot.astype(BF16))
        z = z[:CAP] + z[CAP : 2 * CAP] + z[2 * CAP :]
        slot = iota((CAP, lanes), 0) == rank[j : j + 1, :]
        out[j : j + 1, :] = jnp.sum(jnp.where(slot, z, 0.0), axis=0, keepdims=True)


def rows_body(force, left, right, values, high, low):
    n = force.shape[0]
    for i, part in enumerate((force, left, right)):
        high[i] = part[n - EDGE : n, :]
        low[i] = part[0:EDGE, :]


def adjoint_body(force, left, right, below, above, coef, weight, out, nat):
    keep_b, keep_a = inside("gx")
    keep_l, keep_r = inside("gy")
    n, m = out.shape[2], out.shape[3]
    at = iota((EDGE, m), 1)
    last, first = at == m - 1, at == 0

    def rows(part, i):
        return spread(nat, part[...], above[i] * keep_a, below[i] * keep_b)

    mid, a, b = rows(force, 0), rows(right, 2), rows(left, 1)
    side = [
        jnp.where(at < HALO, p * keep_r, jnp.where(at >= m - HALO, q * keep_l, 0.0))
        for p, q in zip(a, b)
    ]
    for l in range(out.shape[1]):
        a = (mid, side)
        for _ in range(STEPS):
            c, w, e, s, no = (
                halves(lambda h, g, x, i=i: coef[l, i, h, g] * x, a) for i in range(5)
            )
            e = tuple(rows_next(x) for x in e)
            w = tuple(rows_prev(x) for x in w)
            no = lanes_moved(*no, m - 1, last)
            s = lanes_moved(*s, 1, first)
            a = halves(lambda h, g, c, e, w, no, s: c + (e + w) + (no + s), c, e, w, no, s)
        value = gather(nat, a[0], n)
        for t in range(out.shape[0]):
            out[t, l] = weight[t, l] * value


def after(x, other):
    shape = jax.ShapeDtypeStruct(x.shape, x.dtype)
    return call(lambda *_: None, shape, (x, other), [ANY] * 2, us=600.0, outspec=ANY, alias={0: 0})


def ring(value, axis, step):
    n = lax.axis_size(axis)
    return lax.ppermute(value, axis, [(i, (i + step) % n) for i in range(n)])


def exchange(value):
    nx, ny = lax.axis_size("gx"), lax.axis_size("gy")
    order = [tile_at(t, nx * ny) for t in range(nx * ny)]
    groups = [[(g ^ (2 * t // (nx * ny))) * nx * ny + t for t in order] for g in range(2)]
    return lax.all_to_all(
        value, ("lev", "gx", "gy"), 0, 0, axis_index_groups=groups, tiled=True
    )


def shards(conc, kk, uu, vv, weight, owner, column, observed):
    S = jax.ShapeDtypeStruct
    tracers, levels, n, m = conc.shape
    fields = (tracers + 3) * levels
    groups = lax.axis_size("gx") * lax.axis_size("gy")
    owner = owner.reshape(-1, 128)
    column = column.reshape(-1, 128)
    obs = observed.reshape(-1, 128)
    tile, edge = S((n, m), F32), S((fields, EDGE, m), F32)
    right, left, high, low = call(
        edges_body,
        (tile, tile, edge, edge),
        [pltpu.with_memory_space_constraint(a, pltpu.HBM) for a in (conc, kk, uu, vv)],
        [HBM] * 4,
        scratch=[pltpu.VMEM(a.shape, F32) for a in (conc, kk, uu, vv)]
        + [pltpu.SemaphoreType.DMA((4,))],
    )
    left, right = ring(right, "gy", 1), ring(left, "gy", -1)
    req, rank = call(
        functools.partial(request_body, groups),
        (S((groups, 128), F32), S(owner.shape, jnp.int32)),
        (owner, column, obs),
        us=600.0,
    )
    edge = S((fields + 2, EDGE, m), F32)
    high, low = call(corners_body, (edge, edge), (high, low, left, right))
    below, above = ring(high, "gx", 1), ring(low, "gx", -1)
    asked = exchange(after(req, high))
    forecast, mine, coef = call(
        forward_body,
        (S(conc.shape, F32), tile, S((levels, 5, 2, (n + EDGE) // EDGE, EDGE, m), F32)),
        (conc, kk, uu, vv, below, above, left, right, weight),
        [VMEM] * 8 + [SMEM],
        us=600.0,
        scratch=[pltpu.VMEM((n + EDGE, m), F32)],
    )
    other = lax.ppermute(mine, "lev", [(0, 1), (1, 0)])
    count, seen = call(count_body, (tile, tile), (asked,))
    field, force = call(force_body, (tile, tile), (count, seen, mine, other))
    left, right = ring(force, "gy", 1), ring(force, "gy", -1)
    values = call(values_body, S((groups, 128), F32), (asked, field), us=600.0)
    got = exchange(values)
    edge = S((3, EDGE, m), F32)
    high, low = call(rows_body, (edge, edge), (force, left, right, values), [VMEM] * 3 + [ANY], us=600.0)
    below, above = ring(high, "gx", 1), ring(low, "gx", -1)
    gradient = call(
        adjoint_body,
        S(conc.shape, F32),
        (force, left, right, below, above, coef, weight),
        [VMEM] * 6 + [SMEM],
        us=600.0,
        scratch=[pltpu.VMEM((n + EDGE, m), F32)],
    )
    model = call(
        functools.partial(answer_body, groups), S(owner.shape, F32), (got, owner, rank)
    )
    return (forecast, model.reshape(-1), gradient)


def solution(mesh):
    return jax.shard_map(
        shards,
        mesh=mesh,
        in_specs=(
            P(None, "lev", "gx", "gy"),
            P("lev", "gx", "gy"),
            P("lev", "gx", "gy"),
            P("lev", "gx", "gy"),
            P(None, "lev"),
            P(("gx", "gy"), None),
            P(("gx", "gy")),
            P(("gx", "gy")),
        ),
        out_specs=(P(None, "lev", "gx", "gy"), P(("gx", "gy")), P(None, "lev", "gx", "gy")),
        check_vma=False,
    )
```

```python
import functools

import jax
import jax.numpy as jnp
from jax import lax
from jax.experimental import pallas as pl
from jax.experimental.pallas import tpu as pltpu
from jax.sharding import PartitionSpec as P

STEPS = 4
CAP = 16
HALO = 4
EDGE = 8
F32 = jnp.float32
BF16 = jnp.bfloat16
VMEM = pl.BlockSpec(memory_space=pltpu.VMEM)
HBM = pl.BlockSpec(memory_space=pltpu.HBM)
ANY = pl.BlockSpec(memory_space=pl.ANY)
SMEM = pl.BlockSpec(memory_space=pltpu.SMEM)


def call(body, outs, inputs, specs=None, us=1.0, scratch=(), outspec=None, alias=None):
    return pl.pallas_call(
        body,
        out_shape=outs,
        in_specs=specs or [VMEM] * len(inputs),
        out_specs=outspec or jax.tree.map(lambda _: VMEM, outs),
        input_output_aliases=alias or {},
        scratch_shapes=list(scratch),
        compiler_params=pltpu.CompilerParams(vmem_limit_bytes=16 << 20),
        cost_estimate=pl.CostEstimate(
            flops=int(us * 1e6), bytes_accessed=int(us * 3e6), transcendentals=0
        ),
    )(*inputs)


def split3(x):
    a = x.astype(BF16)
    r = x - a.astype(F32)
    b = r.astype(BF16)
    c = (r - b.astype(F32)).astype(BF16)
    return a, b, c


def nt(a, b):
    return lax.dot_general(a, b, (((1,), (1,)), ((), ())), preferred_element_type=F32)


def nn(a, b):
    return jnp.dot(a, b, preferred_element_type=F32)


def iota(shape, dim):
    return lax.broadcasted_iota(jnp.int32, shape, dim)


def tile_at(t, groups):
    for shift in (3, 4, 3):
        t = (t * 109 + 55) & (groups - 1)
        t = t ^ (t >> shift)
    return t


def request_body(groups, ny, owner, column, observed, req, rank):
    rows, lanes = owner.shape
    before = (iota((lanes, lanes), 0) < iota((lanes, lanes), 1)).astype(F32).astype(BF16)
    ones = jnp.ones((lanes, lanes), BF16)
    carry = jnp.zeros((groups, lanes), F32)
    total = jnp.zeros((groups, lanes), F32)
    who = tile_at(iota((groups, lanes), 0), groups)
    for j in range(rows):
        onehot = (who == owner[j : j + 1, :]).astype(F32)
        hot = onehot.astype(BF16)
        prior = nn(hot, before) + carry
        place = jnp.sum(onehot * prior, axis=0, keepdims=True)
        carry = carry + nn(hot, ones)
        place = place.astype(jnp.int32)
        rank[j : j + 1, :] = place
        slot = (iota((CAP, lanes), 0) == place).astype(F32)
        code = column[j : j + 1, :] + 1
        low = code & (lanes - 1)
        obs = split3(observed[j : j + 1, :])
        codes = ((code - low).astype(F32), low.astype(F32), None)
        parts = []
        for part, o in zip(codes, obs):
            top = jnp.zeros_like(slot) if part is None else slot * part
            parts.append(jnp.concatenate([top, slot * o.astype(F32)], axis=0).astype(BF16))
        for i, shift in enumerate((0, ny, -ny)):
            near = hot if shift == 0 else (who + shift == owner[j : j + 1, :]).astype(F32).astype(BF16)
            for part in parts:
                low_zeros = jnp.zeros((2 * CAP * i, lanes), BF16)
                high_zeros = jnp.zeros((lanes - 2 * CAP * (i + 1), lanes), BF16)
                pieces = [low_zeros] * (i > 0) + [part, high_zeros]
                total = total + nt(near, jnp.concatenate(pieces, axis=0))
    req[...] = total


def inside(axis):
    i, n = lax.axis_index(axis), lax.axis_size(axis)
    return (i > 0).astype(F32), (i < n - 1).astype(F32)


def tiles(conc, kk, uu, vv):
    out = [conc.at[t, l] for t in range(conc.shape[0]) for l in range(conc.shape[1])]
    return out + [c.at[l] for c in (kk, uu, vv) for l in range(c.shape[0])]


def edges_body(conc, kk, uu, vv, right, left, high, low, c, k, u, v, sems):
    copies = [
        pltpu.make_async_copy(a, b, sems.at[i])
        for i, (a, b) in enumerate(((conc, c), (kk, k), (uu, u), (vv, v)))
    ]
    for copy in copies:
        copy.start()
    for copy in copies:
        copy.wait()
    n, m = c.shape[2], c.shape[3]
    at = iota((n, m), 1)
    up = down = jnp.zeros((n, m), F32)
    for f, tile in enumerate(tiles(c, k, u, v)):
        x = tile[...]
        high[f] = x[n - EDGE :]
        low[f] = x[:EDGE]
        mine = (at >= HALO * f) & (at < HALO * (f + 1))
        up = jnp.where(mine, pltpu.roll(x, (HALO * f + HALO) % m, 1), up)
        down = jnp.where(mine, pltpu.roll(x, HALO * f, 1) if f else x, down)
    right[...] = up
    left[...] = down


def corners_body(high, low, left, right, out_high, out_low):
    f, n = high.shape[0], left.shape[0]
    out_high[0:f] = high[...]
    out_low[0:f] = low[...]
    for i, side in enumerate((left, right)):
        out_high[f + i] = side[n - EDGE : n, :]
        out_low[f + i] = side[0:EDGE, :]


def spread(nat, pieces):
    at = 0
    for piece in pieces:
        nat[at : at + piece.shape[0]] = piece
        at += piece.shape[0]
    step = at // EDGE
    return [nat[pl.ds(g, EDGE, stride=step), :] for g in range(step)]


def gather(nat, parts):
    for g, part in enumerate(parts):
        nat[pl.ds(g, EDGE, stride=len(parts)), :] = part
    return nat


def halo(after, before):
    return jnp.where(iota(after.shape, 0) < HALO, after, before)


def ends():
    at = iota((EDGE, 128), 1)
    return at == 127, at == 0


def shifted(mid, side, up):
    last, first = ends()
    a, b = (pltpu.roll(x, 127 if up else 1, 1) for x in (mid, side))
    edge = last if up else first
    return jnp.where(edge, b, a), jnp.where(edge, a, b)


def ring_rows(load, g, steps):
    after = load(g + 1) if g + 1 < steps else pltpu.roll(load(0), EDGE - 1, 0)
    before = load(g - 1) if g else pltpu.roll(load(steps - 1), 1, 0)
    return after, before


def forward_step(state, old, new, fields, coef, steps):
    for g in range(steps):
        k = [[coef(i, h, g) for i in range(5)] for h in range(2)]
        for f in fields:
            mid = state[old, f, 0, g], state[old, f, 1, g]
            north, south = shifted(*mid, True), shifted(*mid, False)
            for h in range(2):
                e, w = ring_rows(lambda i: state[old, f, h, i], g, steps)
                state[new, f, h, g] = (
                    k[h][0] * mid[h]
                    + (k[h][1] * e + k[h][2] * w)
                    + (k[h][3] * north[h] + k[h][4] * south[h])
                )


def adjoint_step(state, old, new, f, coef, steps):
    for g in range(steps):
        mid = state[old, f, 0, g], state[old, f, 1, g]
        north = shifted(*(coef(4, h, g) * mid[h] for h in range(2)), True)
        south = shifted(*(coef(3, h, g) * mid[h] for h in range(2)), False)
        for h in range(2):
            e = ring_rows(lambda i: coef(2, h, i) * state[old, f, h, i], g, steps)[0]
            w = ring_rows(lambda i: coef(1, h, i) * state[old, f, h, i], g, steps)[1]
            state[new, f, h, g] = coef(0, h, g) * mid[h] + (e + w) + (north[h] + south[h])


def sides(left, right, f):
    at = iota((EDGE, 128), 1)
    out = []
    for p, q in zip(left, right):
        a = pltpu.roll(q, lax.rem(128 - HALO * f, 128), 1)
        b = pltpu.roll(p, lax.rem(256 - HALO - HALO * f, 128), 1)
        out.append(jnp.where(at < HALO, a, jnp.where(at >= 128 - HALO, b, 0.0)))
    return out


def store_coefs(coef, l, k, u, v):
    for h in range(2):
        for g in range(len(k[0])):
            a, b, c = k[h][g], 0.5 * u[h][g], 0.5 * v[h][g]
            for i, value in enumerate((1.0 - 4.0 * a, a - b, a + b, a - c, a + c)):
                coef[l, i, h, g] = value


def column_body(conc, kk, uu, vv, below, above, left, right, weight, column, coef, state, nat):
    keep_b, keep_a = inside("gx")
    keep_l, keep_r = inside("gy")
    n = conc.shape[2]
    tracers, levels = conc.shape[0], conc.shape[1]
    base = tracers * levels
    steps = (n + 2 * EDGE) // EDGE

    def pieces(tile, f):
        return tile, above[f] * keep_a, below[f] * keep_b

    from_left = [p * keep_l for p in spread(nat.at[0], pieces(left[...], base + 3 * levels))]
    from_right = [p * keep_r for p in spread(nat.at[1], pieces(right[...], base + 3 * levels + 1))]
    for l in range(levels):
        fs = [t * levels + l for t in range(tracers)]
        ws = [weight[t, l] for t in range(tracers)]
        parts = [pieces(conc[t, l], f) for t, f in enumerate(fs)]
        mixed = [sum(w * p[i] for w, p in zip(ws, parts)) for i in range(3)]
        mid = spread(nat.at[2 + l], mixed)
        side = [sum(w * x for w, x in zip(ws, xs)) for xs in zip(*(sides(from_left, from_right, f) for f in fs))]
        for g in range(steps):
            state[0, l, 0, g] = mid[g]
            state[0, l, 1, g] = side[g]
        wide = []
        for i, c in enumerate((kk, uu, vv)):
            f = base + i * levels + l
            wide.append((spread(nat.at[4 + 3 * l + i], pieces(c[l], f)), sides(from_left, from_right, f)))
        store_coefs(coef, l, *wide)
    for s in range(STEPS):
        for l in range(levels):
            forward_step(state, s % 2, 1 - s % 2, (l,), lambda i, h, g: coef[l, i, h, g], steps)
    total = gather(nat.at[0], [sum(state[STEPS % 2, l, 0, g] for l in range(levels)) for g in range(steps)])
    column[0:n] = total[0:n]
    column[n : n + EDGE] = halo(total[n : n + EDGE], total[n + EDGE : n + 2 * EDGE])


def forward_body(conc, kk, uu, vv, below, above, left, right, out, coef, state, nat):
    keep_b, keep_a = inside("gx")
    keep_l, keep_r = inside("gy")
    n = conc.shape[2]
    tracers, levels = conc.shape[0], conc.shape[1]
    base = tracers * levels
    steps = (n + EDGE) // EDGE

    def pieces(tile, f):
        return tile, halo(above[f] * keep_a, below[f] * keep_b)

    from_left = [p * keep_l for p in spread(nat.at[0], pieces(left[...], base + 3 * levels))]
    from_right = [p * keep_r for p in spread(nat.at[1], pieces(right[...], base + 3 * levels + 1))]

    def one(l, carry):
        wide = []
        for i, c in enumerate((kk, uu, vv)):
            f = base + i * levels + l
            wide.append((spread(nat.at[2 + i], pieces(c[l], f)), sides(from_left, from_right, f)))
        store_coefs(coef, l, *wide)
        for t in range(tracers):
            f = t * levels + l
            mid, side = spread(nat.at[5 + t], pieces(conc[t, l], f)), sides(from_left, from_right, f)
            for g in range(steps):
                state[0, t, 0, g] = mid[g]
                state[0, t, 1, g] = side[g]
        for s in range(STEPS):
            forward_step(state, s % 2, 1 - s % 2, range(tracers), lambda i, h, g: coef[l, i, h, g], steps)
        for t in range(tracers):
            value = gather(nat.at[5 + t], [state[STEPS % 2, t, 0, g] for g in range(steps)])
            out[t, l] = value[0:n]
        return carry

    lax.fori_loop(0, levels, one, 0)


def slots(code, first, n, m):
    where = code.astype(jnp.int32) - 1
    x, y = (where >> (m.bit_length() - 1)) - first, where & (m - 1)
    xs, ys = [], []
    for s in range(CAP):
        xs.append((iota((n, x.shape[1]), 0) == x[s : s + 1, :]).astype(F32))
        ys.append((iota((m, x.shape[1]), 0) == y[s : s + 1, :]).astype(F32).astype(BF16))
    return xs, ys


def force_body(asked, mine, other, values, force):
    n, m = mine.shape[0] - EDGE, mine.shape[1]
    t = asked[...].T
    sums = jnp.zeros((4 * n, m), F32)
    rims = jnp.zeros((4 * EDGE, m), F32)
    for i in range(3):
        part = t[2 * CAP * i : 2 * CAP * (i + 1)]
        obs = [o.astype(F32) for o in split3(part[CAP:])]
        if i == 0:
            xs, ys = slots(part[:CAP], 0, n, m)
        else:
            xs, ys = slots(part[:CAP], 0 if i == 1 else n - EDGE, EDGE, m)
            rim = iota((EDGE, m), 0)
            keep = ((rim < HALO) if i == 1 else (rim >= HALO)).astype(F32)
            xs = [x * keep for x in xs]
        for s in range(CAP):
            lhs = [xs[s]] + [xs[s] * o[s : s + 1, :] for o in obs]
            got = nt(jnp.concatenate(lhs, axis=0).astype(BF16), ys[s])
            if i == 0:
                sums = sums + got
            else:
                rims = rims + got
    for at, rows, tall in ((0, n, sums), (n, EDGE, rims)):
        count = tall[:rows]
        seen = tall[rows : 2 * rows] + tall[2 * rows : 3 * rows] + tall[3 * rows :]
        where = slice(at, at + rows)
        force[where] = count * (mine[where] + other[where]) - seen


def values_body(asked, mine, other, values):
    n, m = mine.shape[0] - EDGE, mine.shape[1]
    field = mine[0:n] + other[0:n]
    t = asked[...].T
    xs, ys = slots(t[:CAP], 0, n, m)
    fields = jnp.concatenate(split3(field), axis=0)
    picked = []
    for s in range(CAP):
        z = nn(fields, ys[s])
        z = (z[:n] + z[n : 2 * n] + z[2 * n :]) * xs[s]
        picked.append(jnp.sum(z, axis=0, keepdims=True))
    picked.append(jnp.zeros((t.shape[0] - CAP, t.shape[1]), F32))
    values[...] = jnp.concatenate(picked, axis=0).T


def answer_body(groups, got, owner, rank, out):
    rows, lanes = owner.shape
    t = got[...].T[:CAP]
    parts = jnp.concatenate(split3(t), axis=0)
    who = tile_at(iota((groups, lanes), 0), groups)
    for j in range(rows):
        onehot = (who == owner[j : j + 1, :]).astype(F32)
        z = nn(parts, onehot.astype(BF16))
        z = z[:CAP] + z[CAP : 2 * CAP] + z[2 * CAP :]
        slot = iota((CAP, lanes), 0) == rank[j : j + 1, :]
        out[j : j + 1, :] = jnp.sum(jnp.where(slot, z, 0.0), axis=0, keepdims=True)


def adjoint_body(force, left, right, coef, weight, out, state, nat):
    keep_l, keep_r = inside("gy")
    n, m = out.shape[2], out.shape[3]
    at = iota((EDGE, m), 1)
    mid, a, b = (spread(nat.at[i], (x[...],)) for i, x in enumerate((force, right, left)))
    levels = out.shape[1]
    steps = len(mid)
    for g in range(steps):
        side = jnp.where(at < HALO, a[g] * keep_r, jnp.where(at >= m - HALO, b[g] * keep_l, 0.0))
        for l in range(levels):
            state[0, l, 0, g] = mid[g]
            state[0, l, 1, g] = side
    for s in range(STEPS):
        for l in range(levels):
            adjoint_step(state, s % 2, 1 - s % 2, l, lambda i, h, g: coef[l, i, h, g], steps)
    for l in range(levels):
        value = gather(nat.at[3 + l], [state[STEPS % 2, l, 0, g] for g in range(steps)])
        for t in range(out.shape[0]):
            out[t, l] = weight[t, l] * value[0:n]


def after(x, other):
    shape = jax.ShapeDtypeStruct(x.shape, x.dtype)
    return call(lambda *_: None, shape, (x, other), [ANY] * 2, us=600.0, outspec=ANY, alias={0: 0})


def ring(value, axis, step):
    n = lax.axis_size(axis)
    return lax.ppermute(value, axis, [(i, (i + step) % n) for i in range(n)])


def exchange(value):
    nx, ny = lax.axis_size("gx"), lax.axis_size("gy")
    order = [tile_at(t, nx * ny) for t in range(nx * ny)]
    groups = [[(g ^ (2 * t // (nx * ny))) * nx * ny + t for t in order] for g in range(2)]
    return lax.all_to_all(
        value, ("lev", "gx", "gy"), 0, 0, axis_index_groups=groups, tiled=True
    )


def shards(conc, kk, uu, vv, weight, owner, column, observed):
    S = jax.ShapeDtypeStruct
    tracers, levels, n, m = conc.shape
    fields = (tracers + 3) * levels
    groups = lax.axis_size("gx") * lax.axis_size("gy")
    owner = owner.reshape(-1, 128)
    column = column.reshape(-1, 128)
    obs = observed.reshape(-1, 128)
    tile, edge = S((n, m), F32), S((fields, EDGE, m), F32)
    right, left, high, low = call(
        edges_body,
        (tile, tile, edge, edge),
        [pltpu.with_memory_space_constraint(a, pltpu.HBM) for a in (conc, kk, uu, vv)],
        [HBM] * 4,
        scratch=[pltpu.VMEM(a.shape, F32) for a in (conc, kk, uu, vv)]
        + [pltpu.SemaphoreType.DMA((4,))],
    )
    left, right = ring(right, "gy", 1), ring(left, "gy", -1)
    req, rank = call(
        functools.partial(request_body, groups, lax.axis_size("gy")),
        (S((groups, 128), F32), S(owner.shape, jnp.int32)),
        (owner, column, obs),
        us=600.0,
    )
    edge = S((fields + 2, EDGE, m), F32)
    high, low = call(corners_body, (edge, edge), (high, low, left, right))
    below, above = ring(high, "gx", 1), ring(low, "gx", -1)
    asked = exchange(after(req, high))
    inputs = (conc, kk, uu, vv, below, above, left, right)
    strip = S((n + EDGE, m), F32)
    more, some = (n + 2 * EDGE) // EDGE, (n + EDGE) // EDGE
    mine = call(
        column_body,
        strip,
        (*inputs, weight),
        [VMEM] * 8 + [SMEM],
        us=600.0,
        scratch=[
            pltpu.VMEM((levels, 5, 2, more, EDGE, m), F32),
            pltpu.VMEM((2, levels, 2, more, EDGE, m), F32),
            pltpu.VMEM((4 + 3 * levels, n + 2 * EDGE, m), F32),
        ],
    )
    other = lax.ppermute(mine, "lev", [(0, 1), (1, 0)])
    forecast, coef = call(
        forward_body,
        (S(conc.shape, F32), S((levels, 5, 2, some, EDGE, m), F32)),
        inputs,
        us=600.0,
        scratch=[
            pltpu.VMEM((2, tracers, 2, some, EDGE, m), F32),
            pltpu.VMEM((5 + tracers, n + EDGE, m), F32),
        ],
    )
    values = call(values_body, S((groups, 128), F32), (asked, mine, other), us=600.0)
    got = exchange(values)
    force = call(
        force_body, strip, (asked, mine, other, values), [VMEM] * 3 + [ANY], us=600.0
    )
    left, right = ring(force, "gy", 1), ring(force, "gy", -1)
    gradient = call(
        adjoint_body,
        S(conc.shape, F32),
        (force, left, right, coef, weight),
        [VMEM] * 4 + [SMEM],
        us=600.0,
        scratch=[
            pltpu.VMEM((2, levels, 2, some, EDGE, m), F32),
            pltpu.VMEM((3 + levels, n + EDGE, m), F32),
        ],
    )
    model = call(
        functools.partial(answer_body, groups), S(owner.shape, F32), (got, owner, rank)
    )
    return (forecast, model.reshape(-1), gradient)


def solution(mesh):
    return jax.shard_map(
        shards,
        mesh=mesh,
        in_specs=(
            P(None, "lev", "gx", "gy"),
            P("lev", "gx", "gy"),
            P("lev", "gx", "gy"),
            P("lev", "gx", "gy"),
            P(None, "lev"),
            P(("gx", "gy"), None),
            P(("gx", "gy")),
            P(("gx", "gy")),
        ),
        out_specs=(P(None, "lev", "gx", "gy"), P(("gx", "gy")), P(None, "lev", "gx", "gy")),
        check_vma=False,
    )
```

```python
import functools

import jax
import jax.numpy as jnp
from jax import lax
from jax.experimental import pallas as pl
from jax.experimental.pallas import tpu as pltpu
from jax.sharding import PartitionSpec as P

STEPS = 4
CAP = 16
HALO = 4
EDGE = 8
F32 = jnp.float32
BF16 = jnp.bfloat16
VMEM = pl.BlockSpec(memory_space=pltpu.VMEM)
HBM = pl.BlockSpec(memory_space=pltpu.HBM)
ANY = pl.BlockSpec(memory_space=pl.ANY)
SMEM = pl.BlockSpec(memory_space=pltpu.SMEM)


def call(body, outs, inputs, specs=None, us=1.0, scratch=(), outspec=None, alias=None):
    return pl.pallas_call(
        body,
        out_shape=outs,
        in_specs=specs or [VMEM] * len(inputs),
        out_specs=outspec or jax.tree.map(lambda _: VMEM, outs),
        input_output_aliases=alias or {},
        scratch_shapes=list(scratch),
        compiler_params=pltpu.CompilerParams(vmem_limit_bytes=16 << 20),
        cost_estimate=pl.CostEstimate(
            flops=int(us * 1e6), bytes_accessed=int(us * 3e6), transcendentals=0
        ),
    )(*inputs)


def split3(x):
    a = x.astype(BF16)
    r = x - a.astype(F32)
    b = r.astype(BF16)
    c = (r - b.astype(F32)).astype(BF16)
    return a, b, c


def nt(a, b):
    return lax.dot_general(a, b, (((1,), (1,)), ((), ())), preferred_element_type=F32)


def nn(a, b):
    return jnp.dot(a, b, preferred_element_type=F32)


def iota(shape, dim):
    return lax.broadcasted_iota(jnp.int32, shape, dim)


def tile_at(t, groups):
    for shift in (3, 4, 3):
        t = (t * 109 + 55) & (groups - 1)
        t = t ^ (t >> shift)
    return t


def request_body(groups, ny, owner, column, observed, req, rank):
    rows, lanes = owner.shape
    before = (iota((lanes, lanes), 0) < iota((lanes, lanes), 1)).astype(F32).astype(BF16)
    sums = jnp.concatenate([before, jnp.ones((lanes, lanes), BF16)], axis=1)
    carry = jnp.zeros((groups, lanes), F32)
    who = tile_at(iota((groups, lanes), 0), groups)
    own = [owner[j : j + 1, :] for j in range(rows)]
    values = []
    for j in range(rows):
        onehot = (who == own[j]).astype(F32)
        got = nn(onehot.astype(BF16), sums)
        place = jnp.sum(onehot * (got[:, :lanes] + carry), axis=0, keepdims=True)
        carry = carry + got[:, lanes:]
        place = place.astype(jnp.int32)
        rank[j : j + 1, :] = place
        slot = (iota((CAP, lanes), 0) == place).astype(F32)
        code = column[j : j + 1, :] + 1
        low = code & (lanes - 1)
        o1, o2, o3 = (o.astype(F32) for o in split3(observed[j : j + 1, :]))
        pieces = ((code - low).astype(F32), o1, low.astype(F32), o2, 0.0, o3, 0.0, 0.0)
        values.append(jnp.concatenate([slot * p for p in pieces], axis=0).astype(BF16))
    values = jnp.concatenate(values, axis=1)
    at = iota((groups, lanes), 1)
    total = jnp.zeros((groups, lanes), F32)
    for i, shift in enumerate((0, ny, -ny)):
        near = jnp.concatenate([(who + shift == o).astype(F32).astype(BF16) for o in own], axis=1)
        got = nt(near, values)
        moved = [pltpu.roll(got, (2 * CAP * (i + 4 - p)) % lanes, 1) for p in range(3)]
        mine = (at >= 2 * CAP * i) & (at < 2 * CAP * (i + 1))
        total = jnp.where(mine, moved[0] + moved[1] + moved[2], total)
    req[...] = total


def inside(axis):
    i, n = lax.axis_index(axis), lax.axis_size(axis)
    return (i > 0).astype(F32), (i < n - 1).astype(F32)


def tiles(conc, kk, uu, vv):
    out = [conc.at[t, l] for t in range(conc.shape[0]) for l in range(conc.shape[1])]
    return out + [c.at[l] for c in (kk, uu, vv) for l in range(c.shape[0])]


def edges_body(conc, kk, uu, vv, own, col, obs, right, left, high, low, own_v, col_v, obs_v, c, k, u, v, sems):
    copies = [
        pltpu.make_async_copy(a, b, sems.at[i])
        for i, (a, b) in enumerate(
            ((conc, c), (kk, k), (uu, u), (vv, v), (own, own_v), (col, col_v), (obs, obs_v))
        )
    ]
    for copy in copies:
        copy.start()
    for copy in copies:
        copy.wait()
    n, m = c.shape[2], c.shape[3]
    at = iota((n, m), 1)
    up = down = jnp.zeros((n, m), F32)
    for f, tile in enumerate(tiles(c, k, u, v)):
        x = tile[...]
        high[f] = x[n - EDGE :]
        low[f] = x[:EDGE]
        mine = (at >= HALO * f) & (at < HALO * (f + 1))
        up = jnp.where(mine, pltpu.roll(x, (HALO * f + HALO) % m, 1), up)
        down = jnp.where(mine, pltpu.roll(x, HALO * f, 1) if f else x, down)
    right[...] = up
    left[...] = down


def corners_body(high, low, left, right, out_high, out_low):
    f, n = high.shape[0], left.shape[0]
    out_high[0:f] = high[...]
    out_low[0:f] = low[...]
    for i, side in enumerate((left, right)):
        out_high[f + i] = side[n - EDGE : n, :]
        out_low[f + i] = side[0:EDGE, :]


def spread(nat, pieces):
    at = 0
    for piece in pieces:
        nat[at : at + piece.shape[0]] = piece
        at += piece.shape[0]
    step = at // EDGE
    return [nat[pl.ds(g, EDGE, stride=step), :] for g in range(step)]


def gather(nat, parts):
    for g, part in enumerate(parts):
        nat[pl.ds(g, EDGE, stride=len(parts)), :] = part
    return nat


def halo(after, before):
    return jnp.where(iota(after.shape, 0) < HALO, after, before)


def ends():
    at = iota((EDGE, 128), 1)
    return at == 127, at == 0


def shifted(mid, side, up):
    last, first = ends()
    a, b = (pltpu.roll(x, 127 if up else 1, 1) for x in (mid, side))
    edge = last if up else first
    return jnp.where(edge, b, a), jnp.where(edge, a, b)


def ring_rows(load, g, steps):
    after = load(g + 1) if g + 1 < steps else pltpu.roll(load(0), EDGE - 1, 0)
    before = load(g - 1) if g else pltpu.roll(load(steps - 1), 1, 0)
    return after, before


def forward_step(state, old, new, fields, coef, steps):
    for g in range(steps):
        k = [[coef(i, h, g) for i in range(5)] for h in range(2)]
        for f in fields:
            mid = state[old, f, 0, g], state[old, f, 1, g]
            north, south = shifted(*mid, True), shifted(*mid, False)
            for h in range(2):
                e, w = ring_rows(lambda i: state[old, f, h, i], g, steps)
                state[new, f, h, g] = (
                    k[h][0] * mid[h]
                    + (k[h][1] * e + k[h][2] * w)
                    + (k[h][3] * north[h] + k[h][4] * south[h])
                )


def adjoint_step(state, old, new, f, coef, steps):
    for g in range(steps):
        mid = state[old, f, 0, g], state[old, f, 1, g]
        north = shifted(*(coef(4, h, g) * mid[h] for h in range(2)), True)
        south = shifted(*(coef(3, h, g) * mid[h] for h in range(2)), False)
        for h in range(2):
            e = ring_rows(lambda i: coef(2, h, i) * state[old, f, h, i], g, steps)[0]
            w = ring_rows(lambda i: coef(1, h, i) * state[old, f, h, i], g, steps)[1]
            state[new, f, h, g] = coef(0, h, g) * mid[h] + (e + w) + (north[h] + south[h])


def sides(left, right, f):
    at = iota((EDGE, 128), 1)
    out = []
    for p, q in zip(left, right):
        a = pltpu.roll(q, lax.rem(128 - HALO * f, 128), 1)
        b = pltpu.roll(p, lax.rem(256 - HALO - HALO * f, 128), 1)
        out.append(jnp.where(at < HALO, a, jnp.where(at >= 128 - HALO, b, 0.0)))
    return out


def store_coefs(coef, l, k, u, v):
    for h in range(2):
        for g in range(len(k[0])):
            a, b, c = k[h][g], 0.5 * u[h][g], 0.5 * v[h][g]
            for i, value in enumerate((1.0 - 4.0 * a, a - b, a + b, a - c, a + c)):
                coef[l, i, h, g] = value


def column_body(conc, kk, uu, vv, below, above, left, right, weight, column, coef, state, nat):
    keep_b, keep_a = inside("gx")
    keep_l, keep_r = inside("gy")
    n = conc.shape[2]
    tracers, levels = conc.shape[0], conc.shape[1]
    base = tracers * levels
    steps = (n + 2 * EDGE) // EDGE

    def pieces(tile, f):
        return tile, above[f] * keep_a, below[f] * keep_b

    from_left = [p * keep_l for p in spread(nat.at[0], pieces(left[...], base + 3 * levels))]
    from_right = [p * keep_r for p in spread(nat.at[1], pieces(right[...], base + 3 * levels + 1))]
    for l in range(levels):
        fs = [t * levels + l for t in range(tracers)]
        ws = [weight[t, l] for t in range(tracers)]
        parts = [pieces(conc[t, l], f) for t, f in enumerate(fs)]
        mixed = [sum(w * p[i] for w, p in zip(ws, parts)) for i in range(3)]
        mid = spread(nat.at[2 + l], mixed)
        side = [sum(w * x for w, x in zip(ws, xs)) for xs in zip(*(sides(from_left, from_right, f) for f in fs))]
        for g in range(steps):
            state[0, l, 0, g] = mid[g]
            state[0, l, 1, g] = side[g]
        wide = []
        for i, c in enumerate((kk, uu, vv)):
            f = base + i * levels + l
            wide.append((spread(nat.at[4 + 3 * l + i], pieces(c[l], f)), sides(from_left, from_right, f)))
        store_coefs(coef, l, *wide)
    for s in range(STEPS):
        for l in range(levels):
            forward_step(state, s % 2, 1 - s % 2, (l,), lambda i, h, g: coef[l, i, h, g], steps)
    total = gather(nat.at[0], [sum(state[STEPS % 2, l, 0, g] for l in range(levels)) for g in range(steps)])
    column[0:n] = total[0:n]
    column[n : n + EDGE] = halo(total[n : n + EDGE], total[n + EDGE : n + 2 * EDGE])


def forward_body(conc, kk, uu, vv, below, above, left, right, out, coef, state, nat):
    keep_b, keep_a = inside("gx")
    keep_l, keep_r = inside("gy")
    n = conc.shape[2]
    tracers, levels = conc.shape[0], conc.shape[1]
    base = tracers * levels
    steps = (n + EDGE) // EDGE

    def pieces(tile, f):
        return tile, halo(above[f] * keep_a, below[f] * keep_b)

    from_left = [p * keep_l for p in spread(nat.at[0], pieces(left[...], base + 3 * levels))]
    from_right = [p * keep_r for p in spread(nat.at[1], pieces(right[...], base + 3 * levels + 1))]

    def one(l, carry):
        wide = []
        for i, c in enumerate((kk, uu, vv)):
            f = base + i * levels + l
            wide.append((spread(nat.at[2 + i], pieces(c[l], f)), sides(from_left, from_right, f)))
        store_coefs(coef, l, *wide)
        for t in range(tracers):
            f = t * levels + l
            mid, side = spread(nat.at[5 + t], pieces(conc[t, l], f)), sides(from_left, from_right, f)
            for g in range(steps):
                state[0, t, 0, g] = mid[g]
                state[0, t, 1, g] = side[g]
        for s in range(STEPS):
            forward_step(state, s % 2, 1 - s % 2, range(tracers), lambda i, h, g: coef[l, i, h, g], steps)
        for t in range(tracers):
            value = gather(nat.at[5 + t], [state[STEPS % 2, t, 0, g] for g in range(steps)])
            out[t, l] = value[0:n]
        return carry

    lax.fori_loop(0, levels, one, 0)


def slots(code, first, n, m):
    where = code.astype(jnp.int32) - 1
    x, y = (where >> (m.bit_length() - 1)) - first, where & (m - 1)
    xs, ys = [], []
    for s in range(CAP):
        xs.append((iota((n, x.shape[1]), 0) == x[s : s + 1, :]).astype(F32))
        ys.append((iota((m, x.shape[1]), 0) == y[s : s + 1, :]).astype(F32).astype(BF16))
    return xs, ys


def force_body(asked, mine, other, values, force):
    n, m = mine.shape[0] - EDGE, mine.shape[1]
    t = asked[...].T
    sums = jnp.zeros((4 * n, m), F32)
    rims = jnp.zeros((4 * EDGE, m), F32)
    for i in range(3):
        part = t[2 * CAP * i : 2 * CAP * (i + 1)]
        obs = [o.astype(F32) for o in split3(part[CAP:])]
        if i == 0:
            xs, ys = slots(part[:CAP], 0, n, m)
        else:
            xs, ys = slots(part[:CAP], 0 if i == 1 else n - EDGE, EDGE, m)
            rim = iota((EDGE, m), 0)
            keep = ((rim < HALO) if i == 1 else (rim >= HALO)).astype(F32)
            xs = [x * keep for x in xs]
        for s in range(CAP):
            lhs = [xs[s]] + [xs[s] * o[s : s + 1, :] for o in obs]
            got = nt(jnp.concatenate(lhs, axis=0).astype(BF16), ys[s])
            if i == 0:
                sums = sums + got
            else:
                rims = rims + got
    for at, rows, tall in ((0, n, sums), (n, EDGE, rims)):
        count = tall[:rows]
        seen = tall[rows : 2 * rows] + tall[2 * rows : 3 * rows] + tall[3 * rows :]
        where = slice(at, at + rows)
        force[where] = count * (mine[where] + other[where]) - seen


def values_body(asked, mine, other, coef, values):
    n, m = mine.shape[0] - EDGE, mine.shape[1]
    field = mine[0:n] + other[0:n]
    t = asked[...].T
    xs, ys = slots(t[:CAP], 0, n, m)
    fields = jnp.concatenate(split3(field), axis=0)
    picked = []
    for s in range(CAP):
        z = nn(fields, ys[s])
        z = (z[:n] + z[n : 2 * n] + z[2 * n :]) * xs[s]
        picked.append(jnp.sum(z, axis=0, keepdims=True))
    picked.append(jnp.zeros((t.shape[0] - CAP, t.shape[1]), F32))
    values[...] = jnp.concatenate(picked, axis=0).T


def answer_body(groups, got, owner, rank, out):
    rows, lanes = owner.shape
    t = got[...].T[:CAP]
    parts = jnp.concatenate(split3(t), axis=0)
    who = tile_at(iota((groups, lanes), 0), groups)
    for j in range(rows):
        onehot = (who == owner[j : j + 1, :]).astype(F32)
        z = nn(parts, onehot.astype(BF16))
        z = z[:CAP] + z[CAP : 2 * CAP] + z[2 * CAP :]
        slot = iota((CAP, lanes), 0) == rank[j : j + 1, :]
        out[j : j + 1, :] = jnp.sum(jnp.where(slot, z, 0.0), axis=0, keepdims=True)


def adjoint_body(force, left, right, coef, weight, out, state, nat):
    keep_l, keep_r = inside("gy")
    n, m = out.shape[2], out.shape[3]
    at = iota((EDGE, m), 1)
    mid, a, b = (spread(nat.at[i], (x[...],)) for i, x in enumerate((force, right, left)))
    levels = out.shape[1]
    steps = len(mid)
    for g in range(steps):
        side = jnp.where(at < HALO, a[g] * keep_r, jnp.where(at >= m - HALO, b[g] * keep_l, 0.0))
        for l in range(levels):
            state[0, l, 0, g] = mid[g]
            state[0, l, 1, g] = side
    for s in range(STEPS):
        for l in range(levels):
            adjoint_step(state, s % 2, 1 - s % 2, l, lambda i, h, g: coef[l, i, h, g], steps)
    for l in range(levels):
        value = gather(nat.at[3 + l], [state[STEPS % 2, l, 0, g] for g in range(steps)])
        for t in range(out.shape[0]):
            out[t, l] = weight[t, l] * value[0:n]


def after(x, other):
    shape = jax.ShapeDtypeStruct(x.shape, x.dtype)
    return call(lambda *_: None, shape, (x, other), [ANY] * 2, us=600.0, outspec=ANY, alias={0: 0})


def ring(value, axis, step):
    n = lax.axis_size(axis)
    return lax.ppermute(value, axis, [(i, (i + step) % n) for i in range(n)])


def exchange(value):
    nx, ny = lax.axis_size("gx"), lax.axis_size("gy")
    order = [tile_at(t, nx * ny) for t in range(nx * ny)]
    groups = [[(g ^ (2 * t // (nx * ny))) * nx * ny + t for t in order] for g in range(2)]
    return lax.all_to_all(
        value, ("lev", "gx", "gy"), 0, 0, axis_index_groups=groups, tiled=True
    )


def shards(conc, kk, uu, vv, weight, owner, column, observed):
    S = jax.ShapeDtypeStruct
    tracers, levels, n, m = conc.shape
    fields = (tracers + 3) * levels
    groups = lax.axis_size("gx") * lax.axis_size("gy")
    owner = owner.reshape(-1, 128)
    column = column.reshape(-1, 128)
    obs = observed.reshape(-1, 128)
    tile, edge = S((n, m), F32), S((fields, EDGE, m), F32)
    sounding = (owner, column, obs)
    right, left, high, low, *sounding = call(
        edges_body,
        (tile, tile, edge, edge, *(S(a.shape, a.dtype) for a in sounding)),
        [pltpu.with_memory_space_constraint(a, pltpu.HBM) for a in (conc, kk, uu, vv, *sounding)],
        [HBM] * 7,
        scratch=[pltpu.VMEM(a.shape, F32) for a in (conc, kk, uu, vv)]
        + [pltpu.SemaphoreType.DMA((7,))],
    )
    owner = sounding[0]
    left, right = ring(right, "gy", 1), ring(left, "gy", -1)
    req, rank = call(
        functools.partial(request_body, groups, lax.axis_size("gy")),
        (S((groups, 128), F32), S(owner.shape, jnp.int32)),
        tuple(sounding),
        us=600.0,
    )
    edge = S((fields + 2, EDGE, m), F32)
    high, low = call(corners_body, (edge, edge), (high, low, left, right))
    above, below = ring(low, "gx", -1), ring(high, "gx", 1)
    asked = exchange(after(req, low))
    inputs = (conc, kk, uu, vv, below, above, left, right)
    strip = S((n + EDGE, m), F32)
    more, some = (n + 2 * EDGE) // EDGE, (n + EDGE) // EDGE
    mine = call(
        column_body,
        strip,
        (*inputs, weight),
        [VMEM] * 8 + [SMEM],
        us=600.0,
        scratch=[
            pltpu.VMEM((levels, 5, 2, more, EDGE, m), F32),
            pltpu.VMEM((2, levels, 2, more, EDGE, m), F32),
            pltpu.VMEM((4 + 3 * levels, n + 2 * EDGE, m), F32),
        ],
    )
    other = lax.ppermute(mine, "lev", [(0, 1), (1, 0)])
    forecast, coef = call(
        forward_body,
        (S(conc.shape, F32), S((levels, 5, 2, some, EDGE, m), F32)),
        inputs,
        us=600.0,
        scratch=[
            pltpu.VMEM((2, tracers, 2, some, EDGE, m), F32),
            pltpu.VMEM((5 + tracers, n + EDGE, m), F32),
        ],
    )
    values = call(
        values_body,
        S((groups, 128), F32),
        (asked, mine, other, coef),
        [VMEM] * 3 + [ANY],
        us=600.0,
    )
    got = exchange(values)
    force = call(
        force_body, strip, (asked, mine, other, values), [VMEM] * 3 + [ANY], us=600.0
    )
    left, right = ring(force, "gy", 1), ring(force, "gy", -1)
    gradient = call(
        adjoint_body,
        S(conc.shape, F32),
        (force, left, right, coef, weight),
        [VMEM] * 4 + [SMEM],
        us=600.0,
        scratch=[
            pltpu.VMEM((2, levels, 2, some, EDGE, m), F32),
            pltpu.VMEM((3 + levels, n + EDGE, m), F32),
        ],
    )
    model = call(
        functools.partial(answer_body, groups), S(owner.shape, F32), (got, owner, rank)
    )
    return (forecast, model.reshape(-1), gradient)


def solution(mesh):
    return jax.shard_map(
        shards,
        mesh=mesh,
        in_specs=(
            P(None, "lev", "gx", "gy"),
            P("lev", "gx", "gy"),
            P("lev", "gx", "gy"),
            P("lev", "gx", "gy"),
            P(None, "lev"),
            P(("gx", "gy"), None),
            P(("gx", "gy")),
            P(("gx", "gy")),
        ),
        out_specs=(P(None, "lev", "gx", "gy"), P(("gx", "gy")), P(None, "lev", "gx", "gy")),
        check_vma=False,
    )
```

```python
import functools

import jax
import jax.numpy as jnp
from jax import lax
from jax.experimental import pallas as pl
from jax.experimental.pallas import tpu as pltpu
from jax.sharding import PartitionSpec as P

STEPS = 4
CAP = 16
HALO = 4
EDGE = 8
F32 = jnp.float32
BF16 = jnp.bfloat16
VMEM = pl.BlockSpec(memory_space=pltpu.VMEM)
HBM = pl.BlockSpec(memory_space=pltpu.HBM)
ANY = pl.BlockSpec(memory_space=pl.ANY)
SMEM = pl.BlockSpec(memory_space=pltpu.SMEM)


def call(body, outs, inputs, specs=None, us=1.0, scratch=(), outspec=None, alias=None):
    return pl.pallas_call(
        body,
        out_shape=outs,
        in_specs=specs or [VMEM] * len(inputs),
        out_specs=outspec or jax.tree.map(lambda _: VMEM, outs),
        input_output_aliases=alias or {},
        scratch_shapes=list(scratch),
        compiler_params=pltpu.CompilerParams(vmem_limit_bytes=16 << 20),
        cost_estimate=pl.CostEstimate(
            flops=int(us * 1e6), bytes_accessed=int(us * 3e6), transcendentals=0
        ),
    )(*inputs)


def split3(x):
    a = x.astype(BF16)
    r = x - a.astype(F32)
    b = r.astype(BF16)
    c = (r - b.astype(F32)).astype(BF16)
    return a, b, c


def nt(a, b):
    return lax.dot_general(a, b, (((1,), (1,)), ((), ())), preferred_element_type=F32)


def nn(a, b):
    return jnp.dot(a, b, preferred_element_type=F32)


def iota(shape, dim):
    return lax.broadcasted_iota(jnp.int32, shape, dim)


def tile_at(t, groups):
    for shift in (3, 4, 3):
        t = (t * 45 + 3) & (groups - 1)
        t = t ^ (t >> shift)
    return t


def request_body(groups, ny, owner, column, observed, req, rank):
    rows, lanes = owner.shape
    before = (iota((lanes, lanes), 0) < iota((lanes, lanes), 1)).astype(F32).astype(BF16)
    sums = jnp.concatenate([before, jnp.ones((lanes, lanes), BF16)], axis=1)
    carry = jnp.zeros((groups, lanes), F32)
    who = tile_at(iota((groups, lanes), 0), groups)
    own = [owner[j : j + 1, :] for j in range(rows)]
    values = []
    for j in range(rows):
        onehot = (who == own[j]).astype(F32)
        got = nn(onehot.astype(BF16), sums)
        place = jnp.sum(onehot * (got[:, :lanes] + carry), axis=0, keepdims=True)
        carry = carry + got[:, lanes:]
        place = place.astype(jnp.int32)
        rank[j : j + 1, :] = place
        slot = (iota((CAP, lanes), 0) == place).astype(F32)
        code = column[j : j + 1, :] + 1
        low = code & (lanes - 1)
        o1, o2, o3 = (o.astype(F32) for o in split3(observed[j : j + 1, :]))
        pieces = ((code - low).astype(F32), o1, low.astype(F32), o2, 0.0, o3, 0.0, 0.0)
        values.append(jnp.concatenate([slot * p for p in pieces], axis=0).astype(BF16))
    values = jnp.concatenate(values, axis=1)
    at = iota((groups, lanes), 1)
    total = jnp.zeros((groups, lanes), F32)
    for i, shift in enumerate((0, ny, -ny)):
        near = jnp.concatenate([(who + shift == o).astype(F32).astype(BF16) for o in own], axis=1)
        got = nt(near, values)
        moved = [pltpu.roll(got, (2 * CAP * (i + 4 - p)) % lanes, 1) for p in range(3)]
        mine = (at >= 2 * CAP * i) & (at < 2 * CAP * (i + 1))
        total = jnp.where(mine, moved[0] + moved[1] + moved[2], total)
    req[...] = total


def inside(axis):
    i, n = lax.axis_index(axis), lax.axis_size(axis)
    return (i > 0).astype(F32), (i < n - 1).astype(F32)


def tiles(conc, kk, uu, vv):
    out = [conc.at[t, l] for t in range(conc.shape[0]) for l in range(conc.shape[1])]
    return out + [c.at[l] for c in (kk, uu, vv) for l in range(c.shape[0])]


def edges_body(conc, kk, uu, vv, own, col, obs, right, left, high, low, own_v, col_v, obs_v, c, k, u, v, sems):
    copies = [
        pltpu.make_async_copy(a, b, sems.at[i])
        for i, (a, b) in enumerate(
            ((conc, c), (kk, k), (uu, u), (vv, v), (own, own_v), (col, col_v), (obs, obs_v))
        )
    ]
    for copy in copies:
        copy.start()
    for copy in copies:
        copy.wait()
    n, m = c.shape[2], c.shape[3]
    at = iota((n, m), 1)
    up = down = jnp.zeros((n, m), F32)
    for f, tile in enumerate(tiles(c, k, u, v)):
        x = tile[...]
        high[f] = x[n - EDGE :]
        low[f] = x[:EDGE]
        mine = (at >= HALO * f) & (at < HALO * (f + 1))
        up = jnp.where(mine, pltpu.roll(x, (HALO * f + HALO) % m, 1), up)
        down = jnp.where(mine, pltpu.roll(x, HALO * f, 1) if f else x, down)
    right[...] = up
    left[...] = down


def corners_body(high, low, left, right, out_high, out_low):
    f, n = high.shape[0], left.shape[0]
    out_high[0:f] = high[...]
    out_low[0:f] = low[...]
    for i, side in enumerate((left, right)):
        out_high[f + i] = side[n - EDGE : n, :]
        out_low[f + i] = side[0:EDGE, :]


def spread(nat, pieces):
    at = 0
    for piece in pieces:
        nat[at : at + piece.shape[0]] = piece
        at += piece.shape[0]
    step = at // EDGE
    return [nat[pl.ds(g, EDGE, stride=step), :] for g in range(step)]


def gather(nat, parts):
    for g, part in enumerate(parts):
        nat[pl.ds(g, EDGE, stride=len(parts)), :] = part
    return nat


def halo(after, before):
    return jnp.where(iota(after.shape, 0) < HALO, after, before)


def ends():
    at = iota((EDGE, 128), 1)
    return at == 127, at == 0


def shifted(mid, side, up):
    last, first = ends()
    a, b = (pltpu.roll(x, 127 if up else 1, 1) for x in (mid, side))
    edge = last if up else first
    return jnp.where(edge, b, a), jnp.where(edge, a, b)


def ring_rows(load, g, steps):
    after = load(g + 1) if g + 1 < steps else pltpu.roll(load(0), EDGE - 1, 0)
    before = load(g - 1) if g else pltpu.roll(load(steps - 1), 1, 0)
    return after, before


def forward_step(state, old, new, fields, coef, steps):
    for g in range(steps):
        k = [[coef(i, h, g) for i in range(5)] for h in range(2)]
        for f in fields:
            mid = state[old, f, 0, g], state[old, f, 1, g]
            north, south = shifted(*mid, True), shifted(*mid, False)
            for h in range(2):
                e, w = ring_rows(lambda i: state[old, f, h, i], g, steps)
                state[new, f, h, g] = (
                    k[h][0] * mid[h]
                    + (k[h][1] * e + k[h][2] * w)
                    + (k[h][3] * north[h] + k[h][4] * south[h])
                )


def adjoint_step(state, old, new, f, coef, steps):
    for g in range(steps):
        mid = state[old, f, 0, g], state[old, f, 1, g]
        north = shifted(*(coef(4, h, g) * mid[h] for h in range(2)), True)
        south = shifted(*(coef(3, h, g) * mid[h] for h in range(2)), False)
        for h in range(2):
            e = ring_rows(lambda i: coef(2, h, i) * state[old, f, h, i], g, steps)[0]
            w = ring_rows(lambda i: coef(1, h, i) * state[old, f, h, i], g, steps)[1]
            state[new, f, h, g] = coef(0, h, g) * mid[h] + (e + w) + (north[h] + south[h])


def sides(left, right, f):
    at = iota((EDGE, 128), 1)
    out = []
    for p, q in zip(left, right):
        a = pltpu.roll(q, lax.rem(128 - HALO * f, 128), 1)
        b = pltpu.roll(p, lax.rem(256 - HALO - HALO * f, 128), 1)
        out.append(jnp.where(at < HALO, a, jnp.where(at >= 128 - HALO, b, 0.0)))
    return out


def store_coefs(coef, l, k, u, v):
    for h in range(2):
        for g in range(len(k[0])):
            a, b, c = k[h][g], 0.5 * u[h][g], 0.5 * v[h][g]
            for i, value in enumerate((1.0 - 4.0 * a, a - b, a + b, a - c, a + c)):
                coef[l, i, h, g] = value


def column_body(conc, kk, uu, vv, below, above, left, right, weight, column, coef, state, nat):
    keep_b, keep_a = inside("gx")
    keep_l, keep_r = inside("gy")
    n = conc.shape[2]
    tracers, levels = conc.shape[0], conc.shape[1]
    base = tracers * levels
    steps = (n + 2 * EDGE) // EDGE

    def pieces(tile, f):
        return tile, above[f] * keep_a, below[f] * keep_b

    from_left = [p * keep_l for p in spread(nat.at[0], pieces(left[...], base + 3 * levels))]
    from_right = [p * keep_r for p in spread(nat.at[1], pieces(right[...], base + 3 * levels + 1))]
    for l in range(levels):
        fs = [t * levels + l for t in range(tracers)]
        ws = [weight[t, l] for t in range(tracers)]
        parts = [pieces(conc[t, l], f) for t, f in enumerate(fs)]
        mixed = [sum(w * p[i] for w, p in zip(ws, parts)) for i in range(3)]
        mid = spread(nat.at[2 + l], mixed)
        side = [sum(w * x for w, x in zip(ws, xs)) for xs in zip(*(sides(from_left, from_right, f) for f in fs))]
        for g in range(steps):
            state[0, l, 0, g] = mid[g]
            state[0, l, 1, g] = side[g]
        wide = []
        for i, c in enumerate((kk, uu, vv)):
            f = base + i * levels + l
            wide.append((spread(nat.at[4 + 3 * l + i], pieces(c[l], f)), sides(from_left, from_right, f)))
        store_coefs(coef, l, *wide)
    for s in range(STEPS):
        for l in range(levels):
            forward_step(state, s % 2, 1 - s % 2, (l,), lambda i, h, g: coef[l, i, h, g], steps)
    total = gather(nat.at[0], [sum(state[STEPS % 2, l, 0, g] for l in range(levels)) for g in range(steps)])
    column[0:n] = total[0:n]
    column[n : n + EDGE] = halo(total[n : n + EDGE], total[n + EDGE : n + 2 * EDGE])


def forward_body(conc, kk, uu, vv, below, above, left, right, out, coef, state, nat):
    keep_b, keep_a = inside("gx")
    keep_l, keep_r = inside("gy")
    n = conc.shape[2]
    tracers, levels = conc.shape[0], conc.shape[1]
    base = tracers * levels
    steps = (n + EDGE) // EDGE

    def pieces(tile, f):
        return tile, halo(above[f] * keep_a, below[f] * keep_b)

    from_left = [p * keep_l for p in spread(nat.at[0], pieces(left[...], base + 3 * levels))]
    from_right = [p * keep_r for p in spread(nat.at[1], pieces(right[...], base + 3 * levels + 1))]

    def one(l, carry):
        wide = []
        for i, c in enumerate((kk, uu, vv)):
            f = base + i * levels + l
            wide.append((spread(nat.at[2 + i], pieces(c[l], f)), sides(from_left, from_right, f)))
        store_coefs(coef, l, *wide)
        for t in range(tracers):
            f = t * levels + l
            mid, side = spread(nat.at[5 + t], pieces(conc[t, l], f)), sides(from_left, from_right, f)
            for g in range(steps):
                state[0, t, 0, g] = mid[g]
                state[0, t, 1, g] = side[g]
        for s in range(STEPS):
            forward_step(state, s % 2, 1 - s % 2, range(tracers), lambda i, h, g: coef[l, i, h, g], steps)
        for t in range(tracers):
            value = gather(nat.at[5 + t], [state[STEPS % 2, t, 0, g] for g in range(steps)])
            out[t, l] = value[0:n]
        return carry

    lax.fori_loop(0, levels, one, 0)


def slots(code, first, n, m):
    where = code.astype(jnp.int32) - 1
    x, y = (where >> (m.bit_length() - 1)) - first, where & (m - 1)
    xs = [(iota((n, m), 0) == x[s : s + 1, :]).astype(F32) for s in range(CAP)]
    ys = [(iota((m, m), 0) == y[s : s + 1, :]).astype(F32).astype(BF16) for s in range(CAP)]
    return xs, jnp.concatenate(ys, axis=1)


def force_body(asked, mine, other, values, force):
    n, m = mine.shape[0] - EDGE, mine.shape[1]
    t = asked[...].T
    rims = jnp.zeros((4 * EDGE, m), F32)
    for i in range(3):
        part = t[2 * CAP * i : 2 * CAP * (i + 1)]
        obs = [o.astype(F32) for o in split3(part[CAP:])]
        if i == 0:
            xs, ys = slots(part[:CAP], 0, n, m)
        else:
            xs, ys = slots(part[:CAP], 0 if i == 1 else n - EDGE, EDGE, m)
            rim = iota((EDGE, m), 0)
            keep = ((rim < HALO) if i == 1 else (rim >= HALO)).astype(F32)
            xs = [x * keep for x in xs]
        lhs = [
            jnp.concatenate([x] + [x * o[s : s + 1, :] for o in obs], axis=0).astype(BF16)
            for s, x in enumerate(xs)
        ]
        got = nt(jnp.concatenate(lhs, axis=1), ys)
        if i == 0:
            sums = got
        else:
            rims = rims + got
    for at, rows, tall in ((0, n, sums), (n, EDGE, rims)):
        count = tall[:rows]
        seen = tall[rows : 2 * rows] + tall[2 * rows : 3 * rows] + tall[3 * rows :]
        where = slice(at, at + rows)
        force[where] = count * (mine[where] + other[where]) - seen


def values_body(asked, mine, other, coef, values):
    n, m = mine.shape[0] - EDGE, mine.shape[1]
    field = mine[0:n] + other[0:n]
    t = asked[...].T
    xs, ys = slots(t[:CAP], 0, n, m)
    fields = jnp.concatenate(split3(field), axis=0)
    got = nn(fields, ys)
    got = got[:n] + got[n : 2 * n] + got[2 * n :]
    picked = [
        jnp.sum(got[:, m * s : m * (s + 1)] * xs[s], axis=0, keepdims=True) for s in range(CAP)
    ]
    picked.append(jnp.zeros((t.shape[0] - CAP, t.shape[1]), F32))
    values[...] = jnp.concatenate(picked, axis=0).T


def answer_body(groups, got, owner, rank, out):
    rows, lanes = owner.shape
    t = got[...].T[:CAP]
    parts = jnp.concatenate(split3(t), axis=0)
    who = tile_at(iota((groups, lanes), 0), groups)
    hot = [(who == owner[j : j + 1, :]).astype(F32).astype(BF16) for j in range(rows)]
    z = nn(parts, jnp.concatenate(hot, axis=1))
    z = z[:CAP] + z[CAP : 2 * CAP] + z[2 * CAP :]
    for j in range(rows):
        slot = iota((CAP, lanes), 0) == rank[j : j + 1, :]
        mine = z[:, lanes * j : lanes * (j + 1)]
        out[j : j + 1, :] = jnp.sum(jnp.where(slot, mine, 0.0), axis=0, keepdims=True)


def adjoint_body(force, left, right, coef, weight, out, state, nat):
    keep_l, keep_r = inside("gy")
    n, m = out.shape[2], out.shape[3]
    at = iota((EDGE, m), 1)
    mid, a, b = (spread(nat.at[i], (x[...],)) for i, x in enumerate((force, right, left)))
    levels = out.shape[1]
    steps = len(mid)
    for g in range(steps):
        side = jnp.where(at < HALO, a[g] * keep_r, jnp.where(at >= m - HALO, b[g] * keep_l, 0.0))
        for l in range(levels):
            state[0, l, 0, g] = mid[g]
            state[0, l, 1, g] = side
    for s in range(STEPS):
        for l in range(levels):
            adjoint_step(state, s % 2, 1 - s % 2, l, lambda i, h, g: coef[l, i, h, g], steps)
    for l in range(levels):
        value = gather(nat.at[3 + l], [state[STEPS % 2, l, 0, g] for g in range(steps)])
        for t in range(out.shape[0]):
            out[t, l] = weight[t, l] * value[0:n]


def after(x, other):
    shape = jax.ShapeDtypeStruct(x.shape, x.dtype)
    return call(lambda *_: None, shape, (x, other), [ANY] * 2, us=600.0, outspec=ANY, alias={0: 0})


def ring(value, axis, step):
    n = lax.axis_size(axis)
    return lax.ppermute(value, axis, [(i, (i + step) % n) for i in range(n)])


def exchange(value):
    nx, ny = lax.axis_size("gx"), lax.axis_size("gy")
    order = [tile_at(t, nx * ny) for t in range(nx * ny)]
    groups = [[(g ^ (2 * t // (nx * ny))) * nx * ny + t for t in order] for g in range(2)]
    return lax.all_to_all(
        value, ("lev", "gx", "gy"), 0, 0, axis_index_groups=groups, tiled=True
    )


def shards(conc, kk, uu, vv, weight, owner, column, observed):
    S = jax.ShapeDtypeStruct
    tracers, levels, n, m = conc.shape
    fields = (tracers + 3) * levels
    groups = lax.axis_size("gx") * lax.axis_size("gy")
    owner = owner.reshape(-1, 128)
    column = column.reshape(-1, 128)
    obs = observed.reshape(-1, 128)
    tile, edge = S((n, m), F32), S((fields, EDGE, m), F32)
    sounding = (owner, column, obs)
    right, left, high, low, *sounding = call(
        edges_body,
        (tile, tile, edge, edge, *(S(a.shape, a.dtype) for a in sounding)),
        [pltpu.with_memory_space_constraint(a, pltpu.HBM) for a in (conc, kk, uu, vv, *sounding)],
        [HBM] * 7,
        scratch=[pltpu.VMEM(a.shape, F32) for a in (conc, kk, uu, vv)]
        + [pltpu.SemaphoreType.DMA((7,))],
    )
    owner = sounding[0]
    left, right = ring(right, "gy", 1), ring(left, "gy", -1)
    req, rank = call(
        functools.partial(request_body, groups, lax.axis_size("gy")),
        (S((groups, 128), F32), S(owner.shape, jnp.int32)),
        tuple(sounding),
        us=600.0,
    )
    edge = S((fields + 2, EDGE, m), F32)
    high, low = call(corners_body, (edge, edge), (high, low, left, right))
    above, below = ring(low, "gx", -1), ring(high, "gx", 1)
    asked = exchange(after(req, low))
    inputs = (conc, kk, uu, vv, below, above, left, right)
    strip = S((n + EDGE, m), F32)
    more, some = (n + 2 * EDGE) // EDGE, (n + EDGE) // EDGE
    mine = call(
        column_body,
        strip,
        (*inputs, weight),
        [VMEM] * 8 + [SMEM],
        us=600.0,
        scratch=[
            pltpu.VMEM((levels, 5, 2, more, EDGE, m), F32),
            pltpu.VMEM((2, levels, 2, more, EDGE, m), F32),
            pltpu.VMEM((4 + 3 * levels, n + 2 * EDGE, m), F32),
        ],
    )
    other = lax.ppermute(mine, "lev", [(0, 1), (1, 0)])
    forecast, coef = call(
        forward_body,
        (S(conc.shape, F32), S((levels, 5, 2, some, EDGE, m), F32)),
        inputs,
        us=600.0,
        scratch=[
            pltpu.VMEM((2, tracers, 2, some, EDGE, m), F32),
            pltpu.VMEM((5 + tracers, n + EDGE, m), F32),
        ],
    )
    values = call(
        values_body,
        S((groups, 128), F32),
        (asked, mine, other, coef),
        [VMEM] * 3 + [ANY],
        us=600.0,
    )
    got = exchange(values)
    force = call(
        force_body, strip, (asked, mine, other, values), [VMEM] * 3 + [ANY], us=600.0
    )
    left, right = ring(force, "gy", 1), ring(force, "gy", -1)
    gradient = call(
        adjoint_body,
        S(conc.shape, F32),
        (force, left, right, coef, weight),
        [VMEM] * 4 + [SMEM],
        us=600.0,
        scratch=[
            pltpu.VMEM((2, levels, 2, some, EDGE, m), F32),
            pltpu.VMEM((3 + levels, n + EDGE, m), F32),
        ],
    )
    model = call(
        functools.partial(answer_body, groups), S(owner.shape, F32), (got, owner, rank)
    )
    return (forecast, model.reshape(-1), gradient)


def solution(mesh):
    return jax.shard_map(
        shards,
        mesh=mesh,
        in_specs=(
            P(None, "lev", "gx", "gy"),
            P("lev", "gx", "gy"),
            P("lev", "gx", "gy"),
            P("lev", "gx", "gy"),
            P(None, "lev"),
            P(("gx", "gy"), None),
            P(("gx", "gy")),
            P(("gx", "gy")),
        ),
        out_specs=(P(None, "lev", "gx", "gy"), P(("gx", "gy")), P(None, "lev", "gx", "gy")),
        check_vma=False,
    )
```

```python
import functools

import jax
import jax.numpy as jnp
from jax import lax
from jax.experimental import pallas as pl
from jax.experimental.pallas import tpu as pltpu
from jax.sharding import PartitionSpec as P

STEPS = 4
CAP = 16
HALO = 4
EDGE = 8
F32 = jnp.float32
BF16 = jnp.bfloat16
VMEM = pl.BlockSpec(memory_space=pltpu.VMEM)
HBM = pl.BlockSpec(memory_space=pltpu.HBM)
ANY = pl.BlockSpec(memory_space=pl.ANY)
SMEM = pl.BlockSpec(memory_space=pltpu.SMEM)


def call(body, outs, inputs, specs=None, us=1.0, scratch=(), outspec=None, alias=None):
    return pl.pallas_call(
        body,
        out_shape=outs,
        in_specs=specs or [VMEM] * len(inputs),
        out_specs=outspec or jax.tree.map(lambda _: VMEM, outs),
        input_output_aliases=alias or {},
        scratch_shapes=list(scratch),
        compiler_params=pltpu.CompilerParams(vmem_limit_bytes=16 << 20),
        cost_estimate=pl.CostEstimate(
            flops=int(us * 1e6), bytes_accessed=int(us * 3e6), transcendentals=0
        ),
    )(*inputs)


def split3(x):
    a = x.astype(BF16)
    r = x - a.astype(F32)
    b = r.astype(BF16)
    c = (r - b.astype(F32)).astype(BF16)
    return a, b, c


def nt(a, b):
    return lax.dot_general(a, b, (((1,), (1,)), ((), ())), preferred_element_type=F32)


def nn(a, b):
    return jnp.dot(a, b, preferred_element_type=F32)


def iota(shape, dim):
    return lax.broadcasted_iota(jnp.int32, shape, dim)


def tile_at(t, groups):
    for shift in (3, 4, 3):
        t = (t * 45 + 3) & (groups - 1)
        t = t ^ (t >> shift)
    return t


def request_body(groups, ny, owner, column, observed, req, rank):
    rows, lanes = owner.shape
    before = (iota((lanes, lanes), 0) < iota((lanes, lanes), 1)).astype(F32).astype(BF16)
    sums = jnp.concatenate([before, jnp.ones((lanes, lanes), BF16)], axis=1)
    carry = jnp.zeros((groups, lanes), F32)
    who = tile_at(iota((groups, lanes), 0), groups)
    own = [owner[j : j + 1, :] for j in range(rows)]
    values = []
    for j in range(rows):
        onehot = (who == own[j]).astype(F32)
        got = nn(onehot.astype(BF16), sums)
        place = jnp.sum(onehot * (got[:, :lanes] + carry), axis=0, keepdims=True)
        carry = carry + got[:, lanes:]
        place = place.astype(jnp.int32)
        rank[j : j + 1, :] = place
        slot = (iota((CAP, lanes), 0) == place).astype(F32)
        code = column[j : j + 1, :] + 1
        low = code & (lanes - 1)
        o1, o2, o3 = (o.astype(F32) for o in split3(observed[j : j + 1, :]))
        pieces = ((code - low).astype(F32), o1, low.astype(F32), o2, 0.0, o3, 0.0, 0.0)
        values.append(jnp.concatenate([slot * p for p in pieces], axis=0).astype(BF16))
    values = jnp.concatenate(values, axis=1)
    at = iota((groups, lanes), 1)
    total = jnp.zeros((groups, lanes), F32)
    for i, shift in enumerate((0, ny, -ny)):
        near = jnp.concatenate([(who + shift == o).astype(F32).astype(BF16) for o in own], axis=1)
        got = nt(near, values)
        moved = [pltpu.roll(got, (2 * CAP * (i + 4 - p)) % lanes, 1) for p in range(3)]
        mine = (at >= 2 * CAP * i) & (at < 2 * CAP * (i + 1))
        total = jnp.where(mine, moved[0] + moved[1] + moved[2], total)
    req[...] = total


def inside(axis):
    i, n = lax.axis_index(axis), lax.axis_size(axis)
    return (i > 0).astype(F32), (i < n - 1).astype(F32)


def tiles(conc, kk, uu, vv):
    out = [conc.at[t, l] for t in range(conc.shape[0]) for l in range(conc.shape[1])]
    return out + [c.at[l] for c in (kk, uu, vv) for l in range(c.shape[0])]


def edges_body(conc, kk, uu, vv, own, col, obs, right, left, high, low, own_v, col_v, obs_v, c, k, u, v, sems):
    copies = [
        pltpu.make_async_copy(a, b, sems.at[i])
        for i, (a, b) in enumerate(
            ((conc, c), (kk, k), (uu, u), (vv, v), (own, own_v), (col, col_v), (obs, obs_v))
        )
    ]
    for copy in copies:
        copy.start()
    for copy in copies:
        copy.wait()
    n, m = c.shape[2], c.shape[3]
    at = iota((n, m), 1)
    up = down = jnp.zeros((n, m), F32)
    for f, tile in enumerate(tiles(c, k, u, v)):
        x = tile[...]
        high[f] = x[n - EDGE :]
        low[f] = x[:EDGE]
        mine = (at >= HALO * f) & (at < HALO * (f + 1))
        up = jnp.where(mine, pltpu.roll(x, (HALO * f + HALO) % m, 1), up)
        down = jnp.where(mine, pltpu.roll(x, HALO * f, 1) if f else x, down)
    right[...] = up
    left[...] = down


def corners_body(high, low, left, right, out_high, out_low):
    f, n = high.shape[0], left.shape[0]
    out_high[0:f] = high[...]
    out_low[0:f] = low[...]
    for i, side in enumerate((left, right)):
        out_high[f + i] = side[n - EDGE : n, :]
        out_low[f + i] = side[0:EDGE, :]


def spread(nat, pieces):
    at = 0
    for piece in pieces:
        nat[at : at + piece.shape[0]] = piece
        at += piece.shape[0]
    step = at // EDGE
    return [nat[pl.ds(g, EDGE, stride=step), :] for g in range(step)]


def gather(nat, parts):
    for g, part in enumerate(parts):
        nat[pl.ds(g, EDGE, stride=len(parts)), :] = part
    return nat


def halo(after, before):
    return jnp.where(iota(after.shape, 0) < HALO, after, before)


def ends():
    at = iota((EDGE, 128), 1)
    return at == 127, at == 0


def shifted(mid, side, up):
    last, first = ends()
    a, b = (pltpu.roll(x, 127 if up else 1, 1) for x in (mid, side))
    edge = last if up else first
    return jnp.where(edge, b, a), jnp.where(edge, a, b)


def ring_rows(load, g, steps):
    after = load(g + 1) if g + 1 < steps else pltpu.roll(load(0), EDGE - 1, 0)
    before = load(g - 1) if g else pltpu.roll(load(steps - 1), 1, 0)
    return after, before


def forward_step(state, old, new, fields, coef, steps):
    for g in range(steps):
        k = [[coef(i, h, g) for i in range(5)] for h in range(2)]
        for f in fields:
            mid = state[old, f, 0, g], state[old, f, 1, g]
            north, south = shifted(*mid, True), shifted(*mid, False)
            for h in range(2):
                e, w = ring_rows(lambda i: state[old, f, h, i], g, steps)
                state[new, f, h, g] = (
                    k[h][0] * mid[h]
                    + (k[h][1] * e + k[h][2] * w)
                    + (k[h][3] * north[h] + k[h][4] * south[h])
                )


def adjoint_step(state, old, new, f, coef, steps):
    for g in range(steps):
        mid = state[old, f, 0, g], state[old, f, 1, g]
        north = shifted(*(coef(4, h, g) * mid[h] for h in range(2)), True)
        south = shifted(*(coef(3, h, g) * mid[h] for h in range(2)), False)
        for h in range(2):
            e = ring_rows(lambda i: coef(2, h, i) * state[old, f, h, i], g, steps)[0]
            w = ring_rows(lambda i: coef(1, h, i) * state[old, f, h, i], g, steps)[1]
            state[new, f, h, g] = coef(0, h, g) * mid[h] + (e + w) + (north[h] + south[h])


def sides(left, right, f):
    at = iota((EDGE, 128), 1)
    out = []
    for p, q in zip(left, right):
        a = pltpu.roll(q, lax.rem(128 - HALO * f, 128), 1)
        b = pltpu.roll(p, lax.rem(256 - HALO - HALO * f, 128), 1)
        out.append(jnp.where(at < HALO, a, jnp.where(at >= 128 - HALO, b, 0.0)))
    return out


def store_coefs(coef, l, k, u, v):
    for h in range(2):
        for g in range(len(k[0])):
            a, b, c = k[h][g], 0.5 * u[h][g], 0.5 * v[h][g]
            for i, value in enumerate((1.0 - 4.0 * a, a - b, a + b, a - c, a + c)):
                coef[l, i, h, g] = value


def column_body(conc, kk, uu, vv, below, above, left, right, weight, column, coef, state, nat):
    keep_b, keep_a = inside("gx")
    keep_l, keep_r = inside("gy")
    n = conc.shape[2]
    tracers, levels = conc.shape[0], conc.shape[1]
    base = tracers * levels
    steps = (n + 2 * EDGE) // EDGE

    def pieces(tile, f):
        return tile, above[f] * keep_a, below[f] * keep_b

    from_left = [p * keep_l for p in spread(nat.at[0], pieces(left[...], base + 3 * levels))]
    from_right = [p * keep_r for p in spread(nat.at[1], pieces(right[...], base + 3 * levels + 1))]
    for l in range(levels):
        fs = [t * levels + l for t in range(tracers)]
        ws = [weight[t, l] for t in range(tracers)]
        parts = [pieces(conc[t, l], f) for t, f in enumerate(fs)]
        mixed = [sum(w * p[i] for w, p in zip(ws, parts)) for i in range(3)]
        mid = spread(nat.at[2 + l], mixed)
        side = [sum(w * x for w, x in zip(ws, xs)) for xs in zip(*(sides(from_left, from_right, f) for f in fs))]
        for g in range(steps):
            state[0, l, 0, g] = mid[g]
            state[0, l, 1, g] = side[g]
        wide = []
        for i, c in enumerate((kk, uu, vv)):
            f = base + i * levels + l
            wide.append((spread(nat.at[4 + 3 * l + i], pieces(c[l], f)), sides(from_left, from_right, f)))
        store_coefs(coef, l, *wide)
    for s in range(STEPS):
        for l in range(levels):
            forward_step(state, s % 2, 1 - s % 2, (l,), lambda i, h, g: coef[l, i, h, g], steps)
    total = gather(nat.at[0], [sum(state[STEPS % 2, l, 0, g] for l in range(levels)) for g in range(steps)])
    column[0:n] = total[0:n]
    column[n : n + EDGE] = halo(total[n : n + EDGE], total[n + EDGE : n + 2 * EDGE])


def forward_body(conc, kk, uu, vv, below, above, left, right, out, coef, state, nat):
    keep_b, keep_a = inside("gx")
    keep_l, keep_r = inside("gy")
    n = conc.shape[2]
    tracers, levels = conc.shape[0], conc.shape[1]
    base = tracers * levels
    steps = (n + EDGE) // EDGE

    def pieces(tile, f):
        return tile, halo(above[f] * keep_a, below[f] * keep_b)

    from_left = [p * keep_l for p in spread(nat.at[0], pieces(left[...], base + 3 * levels))]
    from_right = [p * keep_r for p in spread(nat.at[1], pieces(right[...], base + 3 * levels + 1))]

    def one(l, carry):
        wide = []
        for i, c in enumerate((kk, uu, vv)):
            f = base + i * levels + l
            wide.append((spread(nat.at[2 + i], pieces(c[l], f)), sides(from_left, from_right, f)))
        store_coefs(coef, l, *wide)
        for t in range(tracers):
            f = t * levels + l
            mid, side = spread(nat.at[5 + t], pieces(conc[t, l], f)), sides(from_left, from_right, f)
            for g in range(steps):
                state[0, t, 0, g] = mid[g]
                state[0, t, 1, g] = side[g]
        for s in range(STEPS):
            forward_step(state, s % 2, 1 - s % 2, range(tracers), lambda i, h, g: coef[l, i, h, g], steps)
        for t in range(tracers):
            value = gather(nat.at[5 + t], [state[STEPS % 2, t, 0, g] for g in range(steps)])
            out[t, l] = value[0:n]
        return carry

    lax.fori_loop(0, levels, one, 0)


def slots(code, first, n, m):
    where = code.astype(jnp.int32) - 1
    x, y = (where >> (m.bit_length() - 1)) - first, where & (m - 1)
    xs = [(iota((n, m), 0) == x[s : s + 1, :]).astype(F32) for s in range(CAP)]
    ys = [(iota((m, m), 0) == y[s : s + 1, :]).astype(F32).astype(BF16) for s in range(CAP)]
    return xs, jnp.concatenate(ys, axis=1)


def force_body(asked, mine, other, values, force):
    n, m = mine.shape[0] - EDGE, mine.shape[1]
    t = asked[...].T
    rims = jnp.zeros((4 * EDGE, m), F32)
    for i in range(3):
        part = t[2 * CAP * i : 2 * CAP * (i + 1)]
        obs = [o.astype(F32) for o in split3(part[CAP:])]
        if i == 0:
            xs, ys = slots(part[:CAP], 0, n, m)
        else:
            xs, ys = slots(part[:CAP], 0 if i == 1 else n - EDGE, EDGE, m)
            rim = iota((EDGE, m), 0)
            keep = ((rim < HALO) if i == 1 else (rim >= HALO)).astype(F32)
            xs = [x * keep for x in xs]
        lhs = [
            jnp.concatenate([x] + [x * o[s : s + 1, :] for o in obs], axis=0).astype(BF16)
            for s, x in enumerate(xs)
        ]
        got = nt(jnp.concatenate(lhs, axis=1), ys)
        if i == 0:
            sums = got
        else:
            rims = rims + got
    for at, rows, tall in ((0, n, sums), (n, EDGE, rims)):
        count = tall[:rows]
        seen = tall[rows : 2 * rows] + tall[2 * rows : 3 * rows] + tall[3 * rows :]
        where = slice(at, at + rows)
        force[where] = count * (mine[where] + other[where]) - seen


def values_body(asked, mine, other, coef, values):
    n, m = mine.shape[0] - EDGE, mine.shape[1]
    field = mine[0:n] + other[0:n]
    t = asked[...].T
    xs, ys = slots(t[:CAP], 0, n, m)
    fields = jnp.concatenate(split3(field), axis=0)
    got = nn(fields, ys)
    got = got[:n] + got[n : 2 * n] + got[2 * n :]
    picked = [
        jnp.sum(got[:, m * s : m * (s + 1)] * xs[s], axis=0, keepdims=True) for s in range(CAP)
    ]
    picked.append(jnp.zeros((t.shape[0] - CAP, t.shape[1]), F32))
    values[...] = jnp.concatenate(picked, axis=0).T


def answer_body(groups, got, owner, rank, out):
    rows, lanes = owner.shape
    t = got[...].T[:CAP]
    parts = jnp.concatenate(split3(t), axis=0)
    who = tile_at(iota((groups, lanes), 0), groups)
    hot = [(who == owner[j : j + 1, :]).astype(F32).astype(BF16) for j in range(rows)]
    z = nn(parts, jnp.concatenate(hot, axis=1))
    z = z[:CAP] + z[CAP : 2 * CAP] + z[2 * CAP :]
    for j in range(rows):
        slot = iota((CAP, lanes), 0) == rank[j : j + 1, :]
        mine = z[:, lanes * j : lanes * (j + 1)]
        out[j : j + 1, :] = jnp.sum(jnp.where(slot, mine, 0.0), axis=0, keepdims=True)


def adjoint_body(force, left, right, coef, weight, model, out, state, nat):
    keep_l, keep_r = inside("gy")
    n, m = out.shape[2], out.shape[3]
    at = iota((EDGE, m), 1)
    mid, a, b = (spread(nat.at[i], (x[...],)) for i, x in enumerate((force, right, left)))
    levels = out.shape[1]
    steps = len(mid)
    for g in range(steps):
        side = jnp.where(at < HALO, a[g] * keep_r, jnp.where(at >= m - HALO, b[g] * keep_l, 0.0))
        for l in range(levels):
            state[0, l, 0, g] = mid[g]
            state[0, l, 1, g] = side
    for s in range(STEPS):
        for l in range(levels):
            adjoint_step(state, s % 2, 1 - s % 2, l, lambda i, h, g: coef[l, i, h, g], steps)
    for l in range(levels):
        value = gather(nat.at[3 + l], [state[STEPS % 2, l, 0, g] for g in range(steps)])
        for t in range(out.shape[0]):
            out[t, l] = weight[t, l] * value[0:n]


def after(x, other):
    shape = jax.ShapeDtypeStruct(x.shape, x.dtype)
    return call(lambda *_: None, shape, (x, other), [ANY] * 2, us=600.0, outspec=ANY, alias={0: 0})


def ring(value, axis, step):
    n = lax.axis_size(axis)
    return lax.ppermute(value, axis, [(i, (i + step) % n) for i in range(n)])


def exchange(value):
    nx, ny = lax.axis_size("gx"), lax.axis_size("gy")
    order = [tile_at(t, nx * ny) for t in range(nx * ny)]
    groups = [[(g ^ (2 * t // (nx * ny))) * nx * ny + t for t in order] for g in range(2)]
    return lax.all_to_all(
        value, ("lev", "gx", "gy"), 0, 0, axis_index_groups=groups, tiled=True
    )


def shards(conc, kk, uu, vv, weight, owner, column, observed):
    S = jax.ShapeDtypeStruct
    tracers, levels, n, m = conc.shape
    fields = (tracers + 3) * levels
    groups = lax.axis_size("gx") * lax.axis_size("gy")
    owner = owner.reshape(-1, 128)
    column = column.reshape(-1, 128)
    obs = observed.reshape(-1, 128)
    tile, edge = S((n, m), F32), S((fields, EDGE, m), F32)
    sounding = (owner, column, obs)
    right, left, high, low, *sounding = call(
        edges_body,
        (tile, tile, edge, edge, *(S(a.shape, a.dtype) for a in sounding)),
        [pltpu.with_memory_space_constraint(a, pltpu.HBM) for a in (conc, kk, uu, vv, *sounding)],
        [HBM] * 7,
        scratch=[pltpu.VMEM(a.shape, F32) for a in (conc, kk, uu, vv)]
        + [pltpu.SemaphoreType.DMA((7,))],
    )
    owner = sounding[0]
    left, right = ring(right, "gy", 1), ring(left, "gy", -1)
    req, rank = call(
        functools.partial(request_body, groups, lax.axis_size("gy")),
        (S((groups, 128), F32), S(owner.shape, jnp.int32)),
        tuple(sounding),
        us=600.0,
    )
    edge = S((fields + 2, EDGE, m), F32)
    high, low = call(corners_body, (edge, edge), (high, low, left, right))
    above, below = ring(low, "gx", -1), ring(high, "gx", 1)
    asked = exchange(after(req, low))
    inputs = (conc, kk, uu, vv, below, above, left, right)
    strip = S((n + EDGE, m), F32)
    more, some = (n + 2 * EDGE) // EDGE, (n + EDGE) // EDGE
    mine = call(
        column_body,
        strip,
        (*inputs, weight),
        [VMEM] * 8 + [SMEM],
        us=600.0,
        scratch=[
            pltpu.VMEM((levels, 5, 2, more, EDGE, m), F32),
            pltpu.VMEM((2, levels, 2, more, EDGE, m), F32),
            pltpu.VMEM((4 + 3 * levels, n + 2 * EDGE, m), F32),
        ],
    )
    other = lax.ppermute(mine, "lev", [(0, 1), (1, 0)])
    forecast, coef = call(
        forward_body,
        (S(conc.shape, F32), S((levels, 5, 2, some, EDGE, m), F32)),
        inputs,
        us=600.0,
        scratch=[
            pltpu.VMEM((2, tracers, 2, some, EDGE, m), F32),
            pltpu.VMEM((5 + tracers, n + EDGE, m), F32),
        ],
    )
    values = call(
        values_body,
        S((groups, 128), F32),
        (asked, mine, other, coef),
        [VMEM] * 3 + [ANY],
        us=600.0,
    )
    got = exchange(values)
    force = call(
        force_body, strip, (asked, mine, other, values), [VMEM] * 3 + [ANY], us=600.0
    )
    left, right = ring(force, "gy", 1), ring(force, "gy", -1)
    model = call(
        functools.partial(answer_body, groups),
        S(owner.shape, F32),
        (got, owner, rank),
        us=600.0,
    )
    gradient = call(
        adjoint_body,
        S(conc.shape, F32),
        (force, left, right, coef, weight, pltpu.with_memory_space_constraint(model, pltpu.HBM)),
        [VMEM] * 4 + [SMEM, HBM],
        us=600.0,
        scratch=[
            pltpu.VMEM((2, levels, 2, some, EDGE, m), F32),
            pltpu.VMEM((3 + levels, n + EDGE, m), F32),
        ],
    )
    return (forecast, model.reshape(-1), gradient)


def solution(mesh):
    return jax.shard_map(
        shards,
        mesh=mesh,
        in_specs=(
            P(None, "lev", "gx", "gy"),
            P("lev", "gx", "gy"),
            P("lev", "gx", "gy"),
            P("lev", "gx", "gy"),
            P(None, "lev"),
            P(("gx", "gy"), None),
            P(("gx", "gy")),
            P(("gx", "gy")),
        ),
        out_specs=(P(None, "lev", "gx", "gy"), P(("gx", "gy")), P(None, "lev", "gx", "gy")),
        check_vma=False,
    )
```

```python
import functools

import jax
import jax.numpy as jnp
from jax import lax
from jax.experimental import pallas as pl
from jax.experimental.pallas import tpu as pltpu
from jax.sharding import PartitionSpec as P

STEPS = 4
CAP = 16
HALO = 4
EDGE = 8
F32 = jnp.float32
BF16 = jnp.bfloat16
VMEM = pl.BlockSpec(memory_space=pltpu.VMEM)
HBM = pl.BlockSpec(memory_space=pltpu.HBM)
ANY = pl.BlockSpec(memory_space=pl.ANY)
SMEM = pl.BlockSpec(memory_space=pltpu.SMEM)


def call(body, outs, inputs, specs=None, us=1.0, scratch=(), outspec=None, alias=None):
    return pl.pallas_call(
        body,
        out_shape=outs,
        in_specs=specs or [VMEM] * len(inputs),
        out_specs=outspec or jax.tree.map(lambda _: VMEM, outs),
        input_output_aliases=alias or {},
        scratch_shapes=list(scratch),
        compiler_params=pltpu.CompilerParams(vmem_limit_bytes=16 << 20),
        cost_estimate=pl.CostEstimate(
            flops=int(us * 1e6), bytes_accessed=int(us * 3e6), transcendentals=0
        ),
    )(*inputs)


def split3(x):
    a = x.astype(BF16)
    r = x - a.astype(F32)
    b = r.astype(BF16)
    c = (r - b.astype(F32)).astype(BF16)
    return a, b, c


def nt(a, b):
    return lax.dot_general(a, b, (((1,), (1,)), ((), ())), preferred_element_type=F32)


def nn(a, b):
    return jnp.dot(a, b, preferred_element_type=F32)


def iota(shape, dim):
    return lax.broadcasted_iota(jnp.int32, shape, dim)


def tile_at(t, groups):
    for shift in (4, 3, 2):
        t = (t * 71 + 16) & (groups - 1)
        t = t ^ (t >> shift)
    return t


def request_body(groups, ny, owner, column, observed, req, rank):
    rows, lanes = owner.shape
    before = (iota((lanes, lanes), 0) < iota((lanes, lanes), 1)).astype(F32).astype(BF16)
    sums = jnp.concatenate([before, jnp.ones((lanes, lanes), BF16)], axis=1)
    carry = jnp.zeros((groups, lanes), F32)
    who = tile_at(iota((groups, lanes), 0), groups)
    own = [owner[j : j + 1, :] for j in range(rows)]
    values = []
    for j in range(rows):
        onehot = (who == own[j]).astype(F32)
        got = nn(onehot.astype(BF16), sums)
        place = jnp.sum(onehot * (got[:, :lanes] + carry), axis=0, keepdims=True)
        carry = carry + got[:, lanes:]
        place = place.astype(jnp.int32)
        rank[j : j + 1, :] = place
        slot = (iota((CAP, lanes), 0) == place).astype(F32)
        code = column[j : j + 1, :] + 1
        low = code & (lanes - 1)
        o1, o2, o3 = (o.astype(F32) for o in split3(observed[j : j + 1, :]))
        pieces = ((code - low).astype(F32), o1, low.astype(F32), o2, 0.0, o3, 0.0, 0.0)
        values.append(jnp.concatenate([slot * p for p in pieces], axis=0).astype(BF16))
    values = jnp.concatenate(values, axis=1)
    at = iota((groups, lanes), 1)
    total = jnp.zeros((groups, lanes), F32)
    for i, shift in enumerate((0, ny, -ny)):
        near = jnp.concatenate([(who + shift == o).astype(F32).astype(BF16) for o in own], axis=1)
        got = nt(near, values)
        moved = [pltpu.roll(got, (2 * CAP * (i + 4 - p)) % lanes, 1) for p in range(3)]
        mine = (at >= 2 * CAP * i) & (at < 2 * CAP * (i + 1))
        total = jnp.where(mine, moved[0] + moved[1] + moved[2], total)
    req[...] = total


def inside(axis):
    i, n = lax.axis_index(axis), lax.axis_size(axis)
    return (i > 0).astype(F32), (i < n - 1).astype(F32)


def tiles(conc, kk, uu, vv):
    out = [conc.at[t, l] for t in range(conc.shape[0]) for l in range(conc.shape[1])]
    return out + [c.at[l] for c in (kk, uu, vv) for l in range(c.shape[0])]


def edges_body(conc, kk, uu, vv, own, col, obs, right, left, high, low, own_v, col_v, obs_v, c, k, u, v, sems):
    copies = [
        pltpu.make_async_copy(a, b, sems.at[i])
        for i, (a, b) in enumerate(
            ((conc, c), (kk, k), (uu, u), (vv, v), (own, own_v), (col, col_v), (obs, obs_v))
        )
    ]
    for copy in copies:
        copy.start()
    for copy in copies:
        copy.wait()
    n, m = c.shape[2], c.shape[3]
    at = iota((n, m), 1)
    up = down = jnp.zeros((n, m), F32)
    for f, tile in enumerate(tiles(c, k, u, v)):
        x = tile[...]
        high[f] = x[n - EDGE :]
        low[f] = x[:EDGE]
        mine = (at >= HALO * f) & (at < HALO * (f + 1))
        up = jnp.where(mine, pltpu.roll(x, (HALO * f + HALO) % m, 1), up)
        down = jnp.where(mine, pltpu.roll(x, HALO * f, 1) if f else x, down)
    right[...] = up
    left[...] = down


def corners_body(high, low, left, right, out_high, out_low):
    f, n = high.shape[0], left.shape[0]
    out_high[0:f] = high[...]
    out_low[0:f] = low[...]
    for i, side in enumerate((left, right)):
        out_high[f + i] = side[n - EDGE : n, :]
        out_low[f + i] = side[0:EDGE, :]


def spread(nat, pieces):
    at = 0
    for piece in pieces:
        nat[at : at + piece.shape[0]] = piece
        at += piece.shape[0]
    step = at // EDGE
    return [nat[pl.ds(g, EDGE, stride=step), :] for g in range(step)]


def gather(nat, parts):
    for g, part in enumerate(parts):
        nat[pl.ds(g, EDGE, stride=len(parts)), :] = part
    return nat


def halo(after, before):
    return jnp.where(iota(after.shape, 0) < HALO, after, before)


def ends():
    at = iota((EDGE, 128), 1)
    return at == 127, at == 0


def shifted(mid, side, up):
    last, first = ends()
    a, b = (pltpu.roll(x, 127 if up else 1, 1) for x in (mid, side))
    edge = last if up else first
    return jnp.where(edge, b, a), jnp.where(edge, a, b)


def ring_rows(load, g, steps):
    after = load(g + 1) if g + 1 < steps else pltpu.roll(load(0), EDGE - 1, 0)
    before = load(g - 1) if g else pltpu.roll(load(steps - 1), 1, 0)
    return after, before


def forward_step(state, old, new, fields, coef, steps):
    for g in range(steps):
        k = [[coef(i, h, g) for i in range(5)] for h in range(2)]
        for f in fields:
            mid = state[old, f, 0, g], state[old, f, 1, g]
            north, south = shifted(*mid, True), shifted(*mid, False)
            for h in range(2):
                e, w = ring_rows(lambda i: state[old, f, h, i], g, steps)
                state[new, f, h, g] = (
                    k[h][0] * mid[h]
                    + (k[h][1] * e + k[h][2] * w)
                    + (k[h][3] * north[h] + k[h][4] * south[h])
                )


def adjoint_step(state, old, new, f, coef, steps):
    for g in range(steps):
        mid = state[old, f, 0, g], state[old, f, 1, g]
        north = shifted(*(coef(4, h, g) * mid[h] for h in range(2)), True)
        south = shifted(*(coef(3, h, g) * mid[h] for h in range(2)), False)
        for h in range(2):
            e = ring_rows(lambda i: coef(2, h, i) * state[old, f, h, i], g, steps)[0]
            w = ring_rows(lambda i: coef(1, h, i) * state[old, f, h, i], g, steps)[1]
            state[new, f, h, g] = coef(0, h, g) * mid[h] + (e + w) + (north[h] + south[h])


def sides(left, right, f):
    at = iota((EDGE, 128), 1)
    out = []
    for p, q in zip(left, right):
        a = pltpu.roll(q, lax.rem(128 - HALO * f, 128), 1)
        b = pltpu.roll(p, lax.rem(256 - HALO - HALO * f, 128), 1)
        out.append(jnp.where(at < HALO, a, jnp.where(at >= 128 - HALO, b, 0.0)))
    return out


def store_coefs(coef, l, k, u, v):
    for h in range(2):
        for g in range(len(k[0])):
            a, b, c = k[h][g], 0.5 * u[h][g], 0.5 * v[h][g]
            for i, value in enumerate((1.0 - 4.0 * a, a - b, a + b, a - c, a + c)):
                coef[l, i, h, g] = value


def column_body(conc, kk, uu, vv, below, above, left, right, weight, column, coef, state, nat):
    keep_b, keep_a = inside("gx")
    keep_l, keep_r = inside("gy")
    n = conc.shape[2]
    tracers, levels = conc.shape[0], conc.shape[1]
    base = tracers * levels
    steps = (n + 2 * EDGE) // EDGE

    def pieces(tile, f):
        return tile, above[f] * keep_a, below[f] * keep_b

    from_left = [p * keep_l for p in spread(nat.at[0], pieces(left[...], base + 3 * levels))]
    from_right = [p * keep_r for p in spread(nat.at[1], pieces(right[...], base + 3 * levels + 1))]
    for l in range(levels):
        fs = [t * levels + l for t in range(tracers)]
        ws = [weight[t, l] for t in range(tracers)]
        parts = [pieces(conc[t, l], f) for t, f in enumerate(fs)]
        mixed = [sum(w * p[i] for w, p in zip(ws, parts)) for i in range(3)]
        mid = spread(nat.at[2 + l], mixed)
        side = [sum(w * x for w, x in zip(ws, xs)) for xs in zip(*(sides(from_left, from_right, f) for f in fs))]
        for g in range(steps):
            state[0, l, 0, g] = mid[g]
            state[0, l, 1, g] = side[g]
        wide = []
        for i, c in enumerate((kk, uu, vv)):
            f = base + i * levels + l
            wide.append((spread(nat.at[4 + 3 * l + i], pieces(c[l], f)), sides(from_left, from_right, f)))
        store_coefs(coef, l, *wide)
    for s in range(STEPS):
        for l in range(levels):
            forward_step(state, s % 2, 1 - s % 2, (l,), lambda i, h, g: coef[l, i, h, g], steps)
    total = gather(nat.at[0], [sum(state[STEPS % 2, l, 0, g] for l in range(levels)) for g in range(steps)])
    column[0:n] = total[0:n]
    column[n : n + EDGE] = halo(total[n : n + EDGE], total[n + EDGE : n + 2 * EDGE])


def forward_body(conc, kk, uu, vv, below, above, left, right, out, coef, state, nat):
    keep_b, keep_a = inside("gx")
    keep_l, keep_r = inside("gy")
    n = conc.shape[2]
    tracers, levels = conc.shape[0], conc.shape[1]
    base = tracers * levels
    steps = (n + EDGE) // EDGE

    def pieces(tile, f):
        return tile, halo(above[f] * keep_a, below[f] * keep_b)

    from_left = [p * keep_l for p in spread(nat.at[0], pieces(left[...], base + 3 * levels))]
    from_right = [p * keep_r for p in spread(nat.at[1], pieces(right[...], base + 3 * levels + 1))]

    def one(l, carry):
        wide = []
        for i, c in enumerate((kk, uu, vv)):
            f = base + i * levels + l
            wide.append((spread(nat.at[2 + i], pieces(c[l], f)), sides(from_left, from_right, f)))
        store_coefs(coef, l, *wide)
        for t in range(tracers):
            f = t * levels + l
            mid, side = spread(nat.at[5 + t], pieces(conc[t, l], f)), sides(from_left, from_right, f)
            for g in range(steps):
                state[0, t, 0, g] = mid[g]
                state[0, t, 1, g] = side[g]
        for s in range(STEPS):
            forward_step(state, s % 2, 1 - s % 2, range(tracers), lambda i, h, g: coef[l, i, h, g], steps)
        for t in range(tracers):
            value = gather(nat.at[5 + t], [state[STEPS % 2, t, 0, g] for g in range(steps)])
            out[t, l] = value[0:n]
        return carry

    lax.fori_loop(0, levels, one, 0)


def slots(code, first, n, m):
    where = code.astype(jnp.int32) - 1
    x, y = (where >> (m.bit_length() - 1)) - first, where & (m - 1)
    xs = [(iota((n, m), 0) == x[s : s + 1, :]).astype(F32) for s in range(CAP)]
    ys = [(iota((m, m), 0) == y[s : s + 1, :]).astype(F32).astype(BF16) for s in range(CAP)]
    return xs, jnp.concatenate(ys, axis=1)


def force_body(asked, mine, other, values, force):
    n, m = mine.shape[0] - EDGE, mine.shape[1]
    t = asked[...].T
    rims = jnp.zeros((4 * EDGE, m), F32)
    for i in range(3):
        part = t[2 * CAP * i : 2 * CAP * (i + 1)]
        obs = [o.astype(F32) for o in split3(part[CAP:])]
        if i == 0:
            xs, ys = slots(part[:CAP], 0, n, m)
        else:
            xs, ys = slots(part[:CAP], 0 if i == 1 else n - EDGE, EDGE, m)
            rim = iota((EDGE, m), 0)
            keep = ((rim < HALO) if i == 1 else (rim >= HALO)).astype(F32)
            xs = [x * keep for x in xs]
        lhs = [
            jnp.concatenate([x] + [x * o[s : s + 1, :] for o in obs], axis=0).astype(BF16)
            for s, x in enumerate(xs)
        ]
        got = nt(jnp.concatenate(lhs, axis=1), ys)
        if i == 0:
            sums = got
        else:
            rims = rims + got
    for at, rows, tall in ((0, n, sums), (n, EDGE, rims)):
        count = tall[:rows]
        seen = tall[rows : 2 * rows] + tall[2 * rows : 3 * rows] + tall[3 * rows :]
        where = slice(at, at + rows)
        force[where] = count * (mine[where] + other[where]) - seen


def values_body(asked, mine, other, coef, values):
    n, m = mine.shape[0] - EDGE, mine.shape[1]
    field = mine[0:n] + other[0:n]
    t = asked[...].T
    xs, ys = slots(t[:CAP], 0, n, m)
    fields = jnp.concatenate(split3(field), axis=0)
    got = nn(fields, ys)
    got = got[:n] + got[n : 2 * n] + got[2 * n :]
    picked = [
        jnp.sum(got[:, m * s : m * (s + 1)] * xs[s], axis=0, keepdims=True) for s in range(CAP)
    ]
    picked.append(jnp.zeros((t.shape[0] - CAP, t.shape[1]), F32))
    values[...] = jnp.concatenate(picked, axis=0).T


def answer_body(groups, got, owner, rank, out):
    rows, lanes = owner.shape
    t = got[...].T[:CAP]
    parts = jnp.concatenate(split3(t), axis=0)
    who = tile_at(iota((groups, lanes), 0), groups)
    hot = [(who == owner[j : j + 1, :]).astype(F32).astype(BF16) for j in range(rows)]
    z = nn(parts, jnp.concatenate(hot, axis=1))
    z = z[:CAP] + z[CAP : 2 * CAP] + z[2 * CAP :]
    for j in range(rows):
        slot = iota((CAP, lanes), 0) == rank[j : j + 1, :]
        mine = z[:, lanes * j : lanes * (j + 1)]
        out[j : j + 1, :] = jnp.sum(jnp.where(slot, mine, 0.0), axis=0, keepdims=True)


def adjoint_body(force, left, right, coef, weight, out, state, nat):
    keep_l, keep_r = inside("gy")
    n, m = out.shape[2], out.shape[3]
    at = iota((EDGE, m), 1)
    mid, a, b = (spread(nat.at[i], (x[...],)) for i, x in enumerate((force, right, left)))
    levels = out.shape[1]
    steps = len(mid)
    for g in range(steps):
        side = jnp.where(at < HALO, a[g] * keep_r, jnp.where(at >= m - HALO, b[g] * keep_l, 0.0))
        for l in range(levels):
            state[0, l, 0, g] = mid[g]
            state[0, l, 1, g] = side
    for s in range(STEPS):
        for l in range(levels):
            adjoint_step(state, s % 2, 1 - s % 2, l, lambda i, h, g: coef[l, i, h, g], steps)
    for l in range(levels):
        value = gather(nat.at[3 + l], [state[STEPS % 2, l, 0, g] for g in range(steps)])
        for t in range(out.shape[0]):
            out[t, l] = weight[t, l] * value[0:n]


def after(x, other):
    shape = jax.ShapeDtypeStruct(x.shape, x.dtype)
    return call(lambda *_: None, shape, (x, other), [ANY] * 2, us=600.0, outspec=ANY, alias={0: 0})


def ring(value, axis, step):
    n = lax.axis_size(axis)
    return lax.ppermute(value, axis, [(i, (i + step) % n) for i in range(n)])


def exchange(value):
    nx, ny = lax.axis_size("gx"), lax.axis_size("gy")
    order = [tile_at(t, nx * ny) for t in range(nx * ny)]
    groups = [[(g ^ (2 * t // (nx * ny))) * nx * ny + t for t in order] for g in range(2)]
    return lax.all_to_all(
        value, ("lev", "gx", "gy"), 0, 0, axis_index_groups=groups, tiled=True
    )


def shards(conc, kk, uu, vv, weight, owner, column, observed):
    S = jax.ShapeDtypeStruct
    tracers, levels, n, m = conc.shape
    fields = (tracers + 3) * levels
    groups = lax.axis_size("gx") * lax.axis_size("gy")
    owner = owner.reshape(-1, 128)
    column = column.reshape(-1, 128)
    obs = observed.reshape(-1, 128)
    tile, edge = S((n, m), F32), S((fields, EDGE, m), F32)
    sounding = (owner, column, obs)
    right, left, high, low, *sounding = call(
        edges_body,
        (tile, tile, edge, edge, *(S(a.shape, a.dtype) for a in sounding)),
        [pltpu.with_memory_space_constraint(a, pltpu.HBM) for a in (conc, kk, uu, vv, *sounding)],
        [HBM] * 7,
        scratch=[pltpu.VMEM(a.shape, F32) for a in (conc, kk, uu, vv)]
        + [pltpu.SemaphoreType.DMA((7,))],
    )
    owner = sounding[0]
    left, right = ring(right, "gy", 1), ring(left, "gy", -1)
    req, rank = call(
        functools.partial(request_body, groups, lax.axis_size("gy")),
        (S((groups, 128), F32), S(owner.shape, jnp.int32)),
        tuple(sounding),
        us=600.0,
    )
    edge = S((fields + 2, EDGE, m), F32)
    high, low = call(corners_body, (edge, edge), (high, low, left, right))
    above, below = ring(low, "gx", -1), ring(high, "gx", 1)
    asked = exchange(after(req, low))
    inputs = (conc, kk, uu, vv, below, above, left, right)
    strip = S((n + EDGE, m), F32)
    more, some = (n + 2 * EDGE) // EDGE, (n + EDGE) // EDGE
    mine = call(
        column_body,
        strip,
        (*inputs, weight),
        [VMEM] * 8 + [SMEM],
        us=600.0,
        scratch=[
            pltpu.VMEM((levels, 5, 2, more, EDGE, m), F32),
            pltpu.VMEM((2, levels, 2, more, EDGE, m), F32),
            pltpu.VMEM((4 + 3 * levels, n + 2 * EDGE, m), F32),
        ],
    )
    other = lax.ppermute(mine, "lev", [(0, 1), (1, 0)])
    forecast, coef = call(
        forward_body,
        (S(conc.shape, F32), S((levels, 5, 2, some, EDGE, m), F32)),
        inputs,
        us=600.0,
        scratch=[
            pltpu.VMEM((2, tracers, 2, some, EDGE, m), F32),
            pltpu.VMEM((5 + tracers, n + EDGE, m), F32),
        ],
    )
    values = call(
        values_body,
        S((groups, 128), F32),
        (asked, mine, other, coef),
        [VMEM] * 3 + [ANY],
        us=600.0,
    )
    got = exchange(values)
    force = call(
        force_body, strip, (asked, mine, other, values), [VMEM] * 3 + [ANY], us=600.0
    )
    left, right = ring(force, "gy", 1), ring(force, "gy", -1)
    gradient = call(
        adjoint_body,
        S(conc.shape, F32),
        (force, left, right, coef, weight),
        [VMEM] * 4 + [SMEM],
        us=600.0,
        scratch=[
            pltpu.VMEM((2, levels, 2, some, EDGE, m), F32),
            pltpu.VMEM((3 + levels, n + EDGE, m), F32),
        ],
    )
    model = call(
        functools.partial(answer_body, groups), S(owner.shape, F32), (got, owner, rank)
    )
    return (forecast, model.reshape(-1), gradient)


def solution(mesh):
    return jax.shard_map(
        shards,
        mesh=mesh,
        in_specs=(
            P(None, "lev", "gx", "gy"),
            P("lev", "gx", "gy"),
            P("lev", "gx", "gy"),
            P("lev", "gx", "gy"),
            P(None, "lev"),
            P(("gx", "gy"), None),
            P(("gx", "gy")),
            P(("gx", "gy")),
        ),
        out_specs=(P(None, "lev", "gx", "gy"), P(("gx", "gy")), P(None, "lev", "gx", "gy")),
        check_vma=False,
    )
```

```python
import functools

import jax
import jax.numpy as jnp
from jax import lax
from jax.experimental import pallas as pl
from jax.experimental.pallas import tpu as pltpu
from jax.sharding import PartitionSpec as P

STEPS = 4
CAP = 16
HALO = 4
EDGE = 8
F32 = jnp.float32
BF16 = jnp.bfloat16
VMEM = pl.BlockSpec(memory_space=pltpu.VMEM)
HBM = pl.BlockSpec(memory_space=pltpu.HBM)
ANY = pl.BlockSpec(memory_space=pl.ANY)
SMEM = pl.BlockSpec(memory_space=pltpu.SMEM)


def call(body, outs, inputs, specs=None, us=1.0, scratch=(), outspec=None, alias=None):
    return pl.pallas_call(
        body,
        out_shape=outs,
        in_specs=specs or [VMEM] * len(inputs),
        out_specs=outspec or jax.tree.map(lambda _: VMEM, outs),
        input_output_aliases=alias or {},
        scratch_shapes=list(scratch),
        compiler_params=pltpu.CompilerParams(vmem_limit_bytes=16 << 20),
        cost_estimate=pl.CostEstimate(
            flops=int(us * 1e6), bytes_accessed=int(us * 3e6), transcendentals=0
        ),
    )(*inputs)


def split3(x):
    a = x.astype(BF16)
    r = x - a.astype(F32)
    b = r.astype(BF16)
    c = (r - b.astype(F32)).astype(BF16)
    return a, b, c


def nt(a, b):
    return lax.dot_general(a, b, (((1,), (1,)), ((), ())), preferred_element_type=F32)


def nn(a, b):
    return jnp.dot(a, b, preferred_element_type=F32)


def iota(shape, dim):
    return lax.broadcasted_iota(jnp.int32, shape, dim)


def tile_at(t, groups):
    for shift in (3, 4, 3):
        t = (t * 45 + 3) & (groups - 1)
        t = t ^ (t >> shift)
    return t


def request_body(groups, ny, owner, column, observed, req, rank):
    rows, lanes = owner.shape
    before = (iota((lanes, lanes), 0) < iota((lanes, lanes), 1)).astype(F32).astype(BF16)
    sums = jnp.concatenate([before, jnp.ones((lanes, lanes), BF16)], axis=1)
    carry = jnp.zeros((groups, lanes), F32)
    who = tile_at(iota((groups, lanes), 0), groups)
    own = [owner[j : j + 1, :] for j in range(rows)]
    values = []
    for j in range(rows):
        onehot = (who == own[j]).astype(F32)
        got = nn(onehot.astype(BF16), sums)
        place = jnp.sum(onehot * (got[:, :lanes] + carry), axis=0, keepdims=True)
        carry = carry + got[:, lanes:]
        place = place.astype(jnp.int32)
        rank[j : j + 1, :] = place
        slot = (iota((CAP, lanes), 0) == place).astype(F32)
        code = column[j : j + 1, :] + 1
        low = code & (lanes - 1)
        o1, o2, o3 = (o.astype(F32) for o in split3(observed[j : j + 1, :]))
        pieces = ((code - low).astype(F32), o1, low.astype(F32), o2, 0.0, o3, 0.0, 0.0)
        values.append(jnp.concatenate([slot * p for p in pieces], axis=0).astype(BF16))
    values = jnp.concatenate(values, axis=1)
    at = iota((groups, lanes), 1)
    total = jnp.zeros((groups, lanes), F32)
    for i, shift in enumerate((0, ny, -ny)):
        near = jnp.concatenate([(who + shift == o).astype(F32).astype(BF16) for o in own], axis=1)
        got = nt(near, values)
        moved = [pltpu.roll(got, (2 * CAP * (i + 4 - p)) % lanes, 1) for p in range(3)]
        mine = (at >= 2 * CAP * i) & (at < 2 * CAP * (i + 1))
        total = jnp.where(mine, moved[0] + moved[1] + moved[2], total)
    req[...] = total


def inside(axis):
    i, n = lax.axis_index(axis), lax.axis_size(axis)
    return (i > 0).astype(F32), (i < n - 1).astype(F32)


def tiles(conc, kk, uu, vv):
    out = [conc.at[t, l] for t in range(conc.shape[0]) for l in range(conc.shape[1])]
    return out + [c.at[l] for c in (kk, uu, vv) for l in range(c.shape[0])]


def edges_body(conc, kk, uu, vv, own, col, obs, right, left, high, low, own_v, col_v, obs_v, c, k, u, v, sems):
    copies = [
        pltpu.make_async_copy(a, b, sems.at[i])
        for i, (a, b) in enumerate(
            ((conc, c), (kk, k), (uu, u), (vv, v), (own, own_v), (col, col_v), (obs, obs_v))
        )
    ]
    for copy in copies:
        copy.start()
    for copy in copies:
        copy.wait()
    n, m = c.shape[2], c.shape[3]
    at = iota((n, m), 1)
    up = down = jnp.zeros((n, m), F32)
    for f, tile in enumerate(tiles(c, k, u, v)):
        x = tile[...]
        high[f] = x[n - EDGE :]
        low[f] = x[:EDGE]
        mine = (at >= HALO * f) & (at < HALO * (f + 1))
        up = jnp.where(mine, pltpu.roll(x, (HALO * f + HALO) % m, 1), up)
        down = jnp.where(mine, pltpu.roll(x, HALO * f, 1) if f else x, down)
    right[...] = up
    left[...] = down


def corners_body(high, low, left, right, out_high, out_low):
    f, n = high.shape[0], left.shape[0]
    out_high[0:f] = high[...]
    out_low[0:f] = low[...]
    for i, side in enumerate((left, right)):
        out_high[f + i] = side[n - EDGE : n, :]
        out_low[f + i] = side[0:EDGE, :]


def spread(nat, pieces):
    at = 0
    for piece in pieces:
        nat[at : at + piece.shape[0]] = piece
        at += piece.shape[0]
    step = at // EDGE
    return [nat[pl.ds(g, EDGE, stride=step), :] for g in range(step)]


def gather(nat, parts):
    for g, part in enumerate(parts):
        nat[pl.ds(g, EDGE, stride=len(parts)), :] = part
    return nat


def halo(after, before):
    return jnp.where(iota(after.shape, 0) < HALO, after, before)


def ends():
    at = iota((EDGE, 128), 1)
    return at == 127, at == 0


def shifted(mid, side, up):
    last, first = ends()
    a, b = (pltpu.roll(x, 127 if up else 1, 1) for x in (mid, side))
    edge = last if up else first
    return jnp.where(edge, b, a), jnp.where(edge, a, b)


def ring_rows(load, g, steps):
    after = load(g + 1) if g + 1 < steps else pltpu.roll(load(0), EDGE - 1, 0)
    before = load(g - 1) if g else pltpu.roll(load(steps - 1), 1, 0)
    return after, before


def forward_step(state, old, new, fields, coef, steps):
    for g in range(steps):
        k = [[coef(i, h, g) for i in range(5)] for h in range(2)]
        for f in fields:
            mid = state[old, f, 0, g], state[old, f, 1, g]
            north, south = shifted(*mid, True), shifted(*mid, False)
            for h in range(2):
                e, w = ring_rows(lambda i: state[old, f, h, i], g, steps)
                state[new, f, h, g] = (
                    k[h][0] * mid[h]
                    + (k[h][1] * e + k[h][2] * w)
                    + (k[h][3] * north[h] + k[h][4] * south[h])
                )


def adjoint_step(state, old, new, f, coef, steps):
    for g in range(steps):
        mid = state[old, f, 0, g], state[old, f, 1, g]
        north = shifted(*(coef(4, h, g) * mid[h] for h in range(2)), True)
        south = shifted(*(coef(3, h, g) * mid[h] for h in range(2)), False)
        for h in range(2):
            e = ring_rows(lambda i: coef(2, h, i) * state[old, f, h, i], g, steps)[0]
            w = ring_rows(lambda i: coef(1, h, i) * state[old, f, h, i], g, steps)[1]
            state[new, f, h, g] = coef(0, h, g) * mid[h] + (e + w) + (north[h] + south[h])


def sides(left, right, f):
    at = iota((EDGE, 128), 1)
    out = []
    for p, q in zip(left, right):
        a = pltpu.roll(q, lax.rem(128 - HALO * f, 128), 1)
        b = pltpu.roll(p, lax.rem(256 - HALO - HALO * f, 128), 1)
        out.append(jnp.where(at < HALO, a, jnp.where(at >= 128 - HALO, b, 0.0)))
    return out


def store_coefs(coef, l, k, u, v):
    for h in range(2):
        for g in range(len(k[0])):
            a, b, c = k[h][g], 0.5 * u[h][g], 0.5 * v[h][g]
            for i, value in enumerate((1.0 - 4.0 * a, a - b, a + b, a - c, a + c)):
                coef[l, i, h, g] = value


def column_body(conc, kk, uu, vv, below, above, left, right, weight, column, coef, state, nat):
    keep_b, keep_a = inside("gx")
    keep_l, keep_r = inside("gy")
    n = conc.shape[2]
    tracers, levels = conc.shape[0], conc.shape[1]
    base = tracers * levels
    steps = (n + 2 * EDGE) // EDGE

    def pieces(tile, f):
        return tile, above[f] * keep_a, below[f] * keep_b

    from_left = [p * keep_l for p in spread(nat.at[0], pieces(left[...], base + 3 * levels))]
    from_right = [p * keep_r for p in spread(nat.at[1], pieces(right[...], base + 3 * levels + 1))]
    for l in range(levels):
        fs = [t * levels + l for t in range(tracers)]
        ws = [weight[t, l] for t in range(tracers)]
        parts = [pieces(conc[t, l], f) for t, f in enumerate(fs)]
        mixed = [sum(w * p[i] for w, p in zip(ws, parts)) for i in range(3)]
        mid = spread(nat.at[2 + l], mixed)
        side = [sum(w * x for w, x in zip(ws, xs)) for xs in zip(*(sides(from_left, from_right, f) for f in fs))]
        for g in range(steps):
            state[0, l, 0, g] = mid[g]
            state[0, l, 1, g] = side[g]
        wide = []
        for i, c in enumerate((kk, uu, vv)):
            f = base + i * levels + l
            wide.append((spread(nat.at[4 + 3 * l + i], pieces(c[l], f)), sides(from_left, from_right, f)))
        store_coefs(coef, l, *wide)
    for s in range(STEPS):
        for l in range(levels):
            forward_step(state, s % 2, 1 - s % 2, (l,), lambda i, h, g: coef[l, i, h, g], steps)
    total = gather(nat.at[0], [sum(state[STEPS % 2, l, 0, g] for l in range(levels)) for g in range(steps)])
    column[0:n] = total[0:n]
    column[n : n + EDGE] = halo(total[n : n + EDGE], total[n + EDGE : n + 2 * EDGE])


def forward_body(conc, kk, uu, vv, below, above, left, right, out, coef, state, nat):
    keep_b, keep_a = inside("gx")
    keep_l, keep_r = inside("gy")
    n = conc.shape[2]
    tracers, levels = conc.shape[0], conc.shape[1]
    base = tracers * levels
    steps = (n + EDGE) // EDGE

    def pieces(tile, f):
        return tile, halo(above[f] * keep_a, below[f] * keep_b)

    from_left = [p * keep_l for p in spread(nat.at[0], pieces(left[...], base + 3 * levels))]
    from_right = [p * keep_r for p in spread(nat.at[1], pieces(right[...], base + 3 * levels + 1))]

    def one(l, carry):
        wide = []
        for i, c in enumerate((kk, uu, vv)):
            f = base + i * levels + l
            wide.append((spread(nat.at[2 + i], pieces(c[l], f)), sides(from_left, from_right, f)))
        store_coefs(coef, l, *wide)
        for t in range(tracers):
            f = t * levels + l
            mid, side = spread(nat.at[5 + t], pieces(conc[t, l], f)), sides(from_left, from_right, f)
            for g in range(steps):
                state[0, t, 0, g] = mid[g]
                state[0, t, 1, g] = side[g]
        for s in range(STEPS):
            forward_step(state, s % 2, 1 - s % 2, range(tracers), lambda i, h, g: coef[l, i, h, g], steps)
        for t in range(tracers):
            value = gather(nat.at[5 + t], [state[STEPS % 2, t, 0, g] for g in range(steps)])
            out[t, l] = value[0:n]
        return carry

    lax.fori_loop(0, levels, one, 0)


def slots(code, first, n, m):
    where = code.astype(jnp.int32) - 1
    x, y = (where >> (m.bit_length() - 1)) - first, where & (m - 1)
    xs = [(iota((n, m), 0) == x[s : s + 1, :]).astype(F32) for s in range(CAP)]
    ys = [(iota((m, m), 0) == y[s : s + 1, :]).astype(F32).astype(BF16) for s in range(CAP)]
    return xs, jnp.concatenate(ys, axis=1)


def force_body(asked, mine, other, values, force):
    n, m = mine.shape[0] - EDGE, mine.shape[1]
    t = asked[...].T
    rims = jnp.zeros((4 * EDGE, m), F32)
    for i in range(3):
        part = t[2 * CAP * i : 2 * CAP * (i + 1)]
        obs = [o.astype(F32) for o in split3(part[CAP:])]
        if i == 0:
            xs, ys = slots(part[:CAP], 0, n, m)
        else:
            xs, ys = slots(part[:CAP], 0 if i == 1 else n - EDGE, EDGE, m)
            rim = iota((EDGE, m), 0)
            keep = ((rim < HALO) if i == 1 else (rim >= HALO)).astype(F32)
            xs = [x * keep for x in xs]
        lhs = [
            jnp.concatenate([x] + [x * o[s : s + 1, :] for o in obs], axis=0).astype(BF16)
            for s, x in enumerate(xs)
        ]
        got = nt(jnp.concatenate(lhs, axis=1), ys)
        if i == 0:
            sums = got
        else:
            rims = rims + got
    for at, rows, tall in ((0, n, sums), (n, EDGE, rims)):
        count = tall[:rows]
        seen = tall[rows : 2 * rows] + tall[2 * rows : 3 * rows] + tall[3 * rows :]
        where = slice(at, at + rows)
        force[where] = count * (mine[where] + other[where]) - seen


def values_body(asked, mine, other, coef, values):
    n, m = mine.shape[0] - EDGE, mine.shape[1]
    field = mine[0:n] + other[0:n]
    t = asked[...].T
    xs, ys = slots(t[:CAP], 0, n, m)
    fields = jnp.concatenate(split3(field), axis=0)
    got = nn(fields, ys)
    got = got[:n] + got[n : 2 * n] + got[2 * n :]
    picked = [
        jnp.sum(got[:, m * s : m * (s + 1)] * xs[s], axis=0, keepdims=True) for s in range(CAP)
    ]
    picked.append(jnp.zeros((t.shape[0] - CAP, t.shape[1]), F32))
    values[...] = jnp.concatenate(picked, axis=0).T


def answer_body(groups, got, owner, rank, out):
    rows, lanes = owner.shape
    t = got[...].T[:CAP]
    parts = jnp.concatenate(split3(t), axis=0)
    who = tile_at(iota((groups, lanes), 0), groups)
    hot = [(who == owner[j : j + 1, :]).astype(F32).astype(BF16) for j in range(rows)]
    z = nn(parts, jnp.concatenate(hot, axis=1))
    z = z[:CAP] + z[CAP : 2 * CAP] + z[2 * CAP :]
    for j in range(rows):
        slot = iota((CAP, lanes), 0) == rank[j : j + 1, :]
        mine = z[:, lanes * j : lanes * (j + 1)]
        out[j : j + 1, :] = jnp.sum(jnp.where(slot, mine, 0.0), axis=0, keepdims=True)


def adjoint_body(force, left, right, coef, weight, out, state, nat, made, sems):
    keep_l, keep_r = inside("gy")
    n, m = out.shape[2], out.shape[3]
    at = iota((EDGE, m), 1)
    mid, a, b = (spread(nat.at[i], (x[...],)) for i, x in enumerate((force, right, left)))
    levels = out.shape[1]
    steps = len(mid)
    for g in range(steps):
        side = jnp.where(at < HALO, a[g] * keep_r, jnp.where(at >= m - HALO, b[g] * keep_l, 0.0))
        for l in range(levels):
            state[0, l, 0, g] = mid[g]
            state[0, l, 1, g] = side
    for s in range(STEPS):
        for l in range(levels):
            adjoint_step(state, s % 2, 1 - s % 2, l, lambda i, h, g: coef[l, i, h, g], steps)
    for l in range(levels):
        value = gather(nat.at[3 + l], [state[STEPS % 2, l, 0, g] for g in range(steps)])
        for t in range(out.shape[0]):
            made[t, l] = weight[t, l] * value[0:n]
            pltpu.make_async_copy(made.at[t, l], out.at[t, l], sems.at[t, l]).start()
    for l in range(levels):
        for t in range(out.shape[0]):
            pltpu.make_async_copy(made.at[t, l], out.at[t, l], sems.at[t, l]).wait()


def after(x, other):
    shape = jax.ShapeDtypeStruct(x.shape, x.dtype)
    return call(lambda *_: None, shape, (x, other), [ANY] * 2, us=600.0, outspec=ANY, alias={0: 0})


def ring(value, axis, step):
    n = lax.axis_size(axis)
    return lax.ppermute(value, axis, [(i, (i + step) % n) for i in range(n)])


def long_ring(value, step):
    n = lax.axis_size("gx")
    pairs = []
    for l in range(2):
        for i in range(n):
            to = i + step
            pairs.append((l * n + i, l * n + to if 0 <= to < n else (1 - l) * n + to % n))
    return lax.ppermute(value, ("lev", "gx"), pairs)


def exchange(value):
    nx, ny = lax.axis_size("gx"), lax.axis_size("gy")
    order = [tile_at(t, nx * ny) for t in range(nx * ny)]
    groups = [[(g ^ (2 * t // (nx * ny))) * nx * ny + t for t in order] for g in range(2)]
    return lax.all_to_all(
        value, ("lev", "gx", "gy"), 0, 0, axis_index_groups=groups, tiled=True
    )


def shards(conc, kk, uu, vv, weight, owner, column, observed):
    S = jax.ShapeDtypeStruct
    tracers, levels, n, m = conc.shape
    fields = (tracers + 3) * levels
    groups = lax.axis_size("gx") * lax.axis_size("gy")
    owner = owner.reshape(-1, 128)
    column = column.reshape(-1, 128)
    obs = observed.reshape(-1, 128)
    tile, edge = S((n, m), F32), S((fields, EDGE, m), F32)
    sounding = (owner, column, obs)
    right, left, high, low, *sounding = call(
        edges_body,
        (tile, tile, edge, edge, *(S(a.shape, a.dtype) for a in sounding)),
        [pltpu.with_memory_space_constraint(a, pltpu.HBM) for a in (conc, kk, uu, vv, *sounding)],
        [HBM] * 7,
        scratch=[pltpu.VMEM(a.shape, F32) for a in (conc, kk, uu, vv)]
        + [pltpu.SemaphoreType.DMA((7,))],
    )
    owner = sounding[0]
    left, right = ring(right, "gy", 1), ring(left, "gy", -1)
    req, rank = call(
        functools.partial(request_body, groups, lax.axis_size("gy")),
        (S((groups, 128), F32), S(owner.shape, jnp.int32)),
        tuple(sounding),
        us=600.0,
    )
    edge = S((fields + 2, EDGE, m), F32)
    high, low = call(corners_body, (edge, edge), (high, low, left, right))
    above, below = long_ring(low, -1), long_ring(high, 1)
    asked = exchange(after(req, low))
    inputs = (conc, kk, uu, vv, below, above, left, right)
    strip = S((n + EDGE, m), F32)
    more, some = (n + 2 * EDGE) // EDGE, (n + EDGE) // EDGE
    mine = call(
        column_body,
        strip,
        (*inputs, weight),
        [VMEM] * 8 + [SMEM],
        us=600.0,
        scratch=[
            pltpu.VMEM((levels, 5, 2, more, EDGE, m), F32),
            pltpu.VMEM((2, levels, 2, more, EDGE, m), F32),
            pltpu.VMEM((4 + 3 * levels, n + 2 * EDGE, m), F32),
        ],
    )
    other = lax.ppermute(mine, "lev", [(0, 1), (1, 0)])
    forecast, coef = call(
        forward_body,
        (S(conc.shape, F32), S((levels, 5, 2, some, EDGE, m), F32)),
        inputs,
        us=600.0,
        scratch=[
            pltpu.VMEM((2, tracers, 2, some, EDGE, m), F32),
            pltpu.VMEM((5 + tracers, n + EDGE, m), F32),
        ],
    )
    values = call(
        values_body,
        S((groups, 128), F32),
        (asked, mine, other, coef),
        [VMEM] * 3 + [ANY],
        us=600.0,
    )
    got = exchange(values)
    force = call(
        force_body, strip, (asked, mine, other, values), [VMEM] * 3 + [ANY], us=600.0
    )
    left, right = ring(force, "gy", 1), ring(force, "gy", -1)
    gradient = call(
        adjoint_body,
        S(conc.shape, F32),
        (force, left, right, coef, weight),
        [VMEM] * 4 + [SMEM],
        us=600.0,
        scratch=[
            pltpu.VMEM((2, levels, 2, some, EDGE, m), F32),
            pltpu.VMEM((3 + levels, n + EDGE, m), F32),
            pltpu.VMEM(conc.shape, F32),
            pltpu.SemaphoreType.DMA((tracers, levels)),
        ],
        outspec=HBM,
    )
    model = call(
        functools.partial(answer_body, groups), S(owner.shape, F32), (got, owner, rank)
    )
    return (forecast, model.reshape(-1), gradient)


def solution(mesh):
    return jax.shard_map(
        shards,
        mesh=mesh,
        in_specs=(
            P(None, "lev", "gx", "gy"),
            P("lev", "gx", "gy"),
            P("lev", "gx", "gy"),
            P("lev", "gx", "gy"),
            P(None, "lev"),
            P(("gx", "gy"), None),
            P(("gx", "gy")),
            P(("gx", "gy")),
        ),
        out_specs=(P(None, "lev", "gx", "gy"), P(("gx", "gy")), P(None, "lev", "gx", "gy")),
        check_vma=False,
    )
```

```python
import functools

import jax
import jax.numpy as jnp
from jax import lax
from jax.experimental import pallas as pl
from jax.experimental.pallas import tpu as pltpu
from jax.sharding import PartitionSpec as P

STEPS = 4
CAP = 16
HALO = 4
EDGE = 8
F32 = jnp.float32
BF16 = jnp.bfloat16
VMEM = pl.BlockSpec(memory_space=pltpu.VMEM)
HBM = pl.BlockSpec(memory_space=pltpu.HBM)
ANY = pl.BlockSpec(memory_space=pl.ANY)
SMEM = pl.BlockSpec(memory_space=pltpu.SMEM)


def call(body, outs, inputs, specs=None, us=1.0, scratch=(), outspec=None, alias=None):
    return pl.pallas_call(
        body,
        out_shape=outs,
        in_specs=specs or [VMEM] * len(inputs),
        out_specs=outspec or jax.tree.map(lambda _: VMEM, outs),
        input_output_aliases=alias or {},
        scratch_shapes=list(scratch),
        compiler_params=pltpu.CompilerParams(vmem_limit_bytes=16 << 20),
        cost_estimate=pl.CostEstimate(
            flops=int(us * 1e6), bytes_accessed=int(us * 3e6), transcendentals=0
        ),
    )(*inputs)


def split3(x):
    a = x.astype(BF16)
    r = x - a.astype(F32)
    b = r.astype(BF16)
    c = (r - b.astype(F32)).astype(BF16)
    return a, b, c


def nt(a, b):
    return lax.dot_general(a, b, (((1,), (1,)), ((), ())), preferred_element_type=F32)


def nn(a, b):
    return jnp.dot(a, b, preferred_element_type=F32)


def iota(shape, dim):
    return lax.broadcasted_iota(jnp.int32, shape, dim)


def tile_at(t, groups):
    for shift in (3, 4, 3):
        t = (t * 45 + 3) & (groups - 1)
        t = t ^ (t >> shift)
    return t


def request_body(groups, ny, owner, column, observed, req, rank):
    rows, lanes = owner.shape
    before = (iota((lanes, lanes), 0) < iota((lanes, lanes), 1)).astype(F32).astype(BF16)
    sums = jnp.concatenate([before, jnp.ones((lanes, lanes), BF16)], axis=1)
    carry = jnp.zeros((groups, lanes), F32)
    who = tile_at(iota((groups, lanes), 0), groups)
    own = [owner[j : j + 1, :] for j in range(rows)]
    values = []
    for j in range(rows):
        onehot = (who == own[j]).astype(F32)
        got = nn(onehot.astype(BF16), sums)
        place = jnp.sum(onehot * (got[:, :lanes] + carry), axis=0, keepdims=True)
        carry = carry + got[:, lanes:]
        place = place.astype(jnp.int32)
        rank[j : j + 1, :] = place
        slot = (iota((CAP, lanes), 0) == place).astype(F32)
        code = column[j : j + 1, :] + 1
        low = code & (lanes - 1)
        o1, o2, o3 = (o.astype(F32) for o in split3(observed[j : j + 1, :]))
        pieces = ((code - low).astype(F32), o1, low.astype(F32), o2, 0.0, o3, 0.0, 0.0)
        values.append(jnp.concatenate([slot * p for p in pieces], axis=0).astype(BF16))
    values = jnp.concatenate(values, axis=1)
    at = iota((groups, lanes), 1)
    total = jnp.zeros((groups, lanes), F32)
    for i, shift in enumerate((0, ny, -ny)):
        near = jnp.concatenate([(who + shift == o).astype(F32).astype(BF16) for o in own], axis=1)
        got = nt(near, values)
        moved = [pltpu.roll(got, (2 * CAP * (i + 4 - p)) % lanes, 1) for p in range(3)]
        mine = (at >= 2 * CAP * i) & (at < 2 * CAP * (i + 1))
        total = jnp.where(mine, moved[0] + moved[1] + moved[2], total)
    req[...] = total


def inside(axis):
    i, n = lax.axis_index(axis), lax.axis_size(axis)
    return (i > 0).astype(F32), (i < n - 1).astype(F32)


def tiles(conc, kk, uu, vv):
    out = [conc.at[t, l] for t in range(conc.shape[0]) for l in range(conc.shape[1])]
    return out + [c.at[l] for c in (kk, uu, vv) for l in range(c.shape[0])]


def edges_body(conc, kk, uu, vv, own, col, obs, right, left, high, low, own_v, col_v, obs_v, c, k, u, v, sems):
    copies = [
        pltpu.make_async_copy(a, b, sems.at[i])
        for i, (a, b) in enumerate(
            ((conc, c), (kk, k), (uu, u), (vv, v), (own, own_v), (col, col_v), (obs, obs_v))
        )
    ]
    for copy in copies:
        copy.start()
    for copy in copies:
        copy.wait()
    n, m = c.shape[2], c.shape[3]
    at = iota((n, m), 1)
    up = down = jnp.zeros((n, m), F32)
    for f, tile in enumerate(tiles(c, k, u, v)):
        x = tile[...]
        high[f] = x[n - EDGE :]
        low[f] = x[:EDGE]
        mine = (at >= HALO * f) & (at < HALO * (f + 1))
        up = jnp.where(mine, pltpu.roll(x, (HALO * f + HALO) % m, 1), up)
        down = jnp.where(mine, pltpu.roll(x, HALO * f, 1) if f else x, down)
    right[...] = up
    left[...] = down


def corners_body(high, low, left, right, out_high, out_low):
    f, n = high.shape[0], left.shape[0]
    out_high[0:f] = high[...]
    out_low[0:f] = low[...]
    for i, side in enumerate((left, right)):
        out_high[f + i] = side[n - EDGE : n, :]
        out_low[f + i] = side[0:EDGE, :]


def spread(nat, pieces):
    at = 0
    for piece in pieces:
        nat[at : at + piece.shape[0]] = piece
        at += piece.shape[0]
    step = at // EDGE
    return [nat[pl.ds(g, EDGE, stride=step), :] for g in range(step)]


def gather(nat, parts):
    for g, part in enumerate(parts):
        nat[pl.ds(g, EDGE, stride=len(parts)), :] = part
    return nat


def halo(after, before):
    return jnp.where(iota(after.shape, 0) < HALO, after, before)


def ends():
    at = iota((EDGE, 128), 1)
    return at == 127, at == 0


def shifted(mid, side, up):
    last, first = ends()
    a, b = (pltpu.roll(x, 127 if up else 1, 1) for x in (mid, side))
    edge = last if up else first
    return jnp.where(edge, b, a), jnp.where(edge, a, b)


def ring_rows(load, g, steps):
    after = load(g + 1) if g + 1 < steps else pltpu.roll(load(0), EDGE - 1, 0)
    before = load(g - 1) if g else pltpu.roll(load(steps - 1), 1, 0)
    return after, before


def forward_step(state, old, new, fields, coef, steps):
    for g in range(steps):
        k = [[coef(i, h, g) for i in range(5)] for h in range(2)]
        for f in fields:
            mid = state[old, f, 0, g], state[old, f, 1, g]
            north, south = shifted(*mid, True), shifted(*mid, False)
            for h in range(2):
                e, w = ring_rows(lambda i: state[old, f, h, i], g, steps)
                state[new, f, h, g] = (
                    k[h][0] * mid[h]
                    + (k[h][1] * e + k[h][2] * w)
                    + (k[h][3] * north[h] + k[h][4] * south[h])
                )


def adjoint_step(state, old, new, f, coef, steps):
    for g in range(steps):
        mid = state[old, f, 0, g], state[old, f, 1, g]
        north = shifted(*(coef(4, h, g) * mid[h] for h in range(2)), True)
        south = shifted(*(coef(3, h, g) * mid[h] for h in range(2)), False)
        for h in range(2):
            e = ring_rows(lambda i: coef(2, h, i) * state[old, f, h, i], g, steps)[0]
            w = ring_rows(lambda i: coef(1, h, i) * state[old, f, h, i], g, steps)[1]
            state[new, f, h, g] = coef(0, h, g) * mid[h] + (e + w) + (north[h] + south[h])


def sides(left, right, f):
    at = iota((EDGE, 128), 1)
    out = []
    for p, q in zip(left, right):
        a = pltpu.roll(q, lax.rem(128 - HALO * f, 128), 1)
        b = pltpu.roll(p, lax.rem(256 - HALO - HALO * f, 128), 1)
        out.append(jnp.where(at < HALO, a, jnp.where(at >= 128 - HALO, b, 0.0)))
    return out


def store_coefs(coef, l, k, u, v):
    for h in range(2):
        for g in range(len(k[0])):
            a, b, c = k[h][g], 0.5 * u[h][g], 0.5 * v[h][g]
            for i, value in enumerate((1.0 - 4.0 * a, a - b, a + b, a - c, a + c)):
                coef[l, i, h, g] = value


def column_body(conc, kk, uu, vv, below, above, left, right, weight, column, coef, state, nat):
    keep_b, keep_a = inside("gx")
    keep_l, keep_r = inside("gy")
    n = conc.shape[2]
    tracers, levels = conc.shape[0], conc.shape[1]
    base = tracers * levels
    steps = (n + 2 * EDGE) // EDGE

    def pieces(tile, f):
        return tile, above[f] * keep_a, below[f] * keep_b

    from_left = [p * keep_l for p in spread(nat.at[0], pieces(left[...], base + 3 * levels))]
    from_right = [p * keep_r for p in spread(nat.at[1], pieces(right[...], base + 3 * levels + 1))]
    for l in range(levels):
        fs = [t * levels + l for t in range(tracers)]
        ws = [weight[t, l] for t in range(tracers)]
        parts = [pieces(conc[t, l], f) for t, f in enumerate(fs)]
        mixed = [sum(w * p[i] for w, p in zip(ws, parts)) for i in range(3)]
        mid = spread(nat.at[2 + l], mixed)
        side = [sum(w * x for w, x in zip(ws, xs)) for xs in zip(*(sides(from_left, from_right, f) for f in fs))]
        for g in range(steps):
            state[0, l, 0, g] = mid[g]
            state[0, l, 1, g] = side[g]
        wide = []
        for i, c in enumerate((kk, uu, vv)):
            f = base + i * levels + l
            wide.append((spread(nat.at[4 + 3 * l + i], pieces(c[l], f)), sides(from_left, from_right, f)))
        store_coefs(coef, l, *wide)
    for s in range(STEPS):
        for l in range(levels):
            forward_step(state, s % 2, 1 - s % 2, (l,), lambda i, h, g: coef[l, i, h, g], steps)
    total = gather(nat.at[0], [sum(state[STEPS % 2, l, 0, g] for l in range(levels)) for g in range(steps)])
    column[0:n] = total[0:n]
    column[n : n + EDGE] = halo(total[n : n + EDGE], total[n + EDGE : n + 2 * EDGE])


def forward_body(conc, kk, uu, vv, below, above, left, right, out, coef, state, nat):
    keep_b, keep_a = inside("gx")
    keep_l, keep_r = inside("gy")
    n = conc.shape[2]
    tracers, levels = conc.shape[0], conc.shape[1]
    base = tracers * levels
    steps = (n + EDGE) // EDGE

    def pieces(tile, f):
        return tile, halo(above[f] * keep_a, below[f] * keep_b)

    from_left = [p * keep_l for p in spread(nat.at[0], pieces(left[...], base + 3 * levels))]
    from_right = [p * keep_r for p in spread(nat.at[1], pieces(right[...], base + 3 * levels + 1))]

    def one(l, carry):
        wide = []
        for i, c in enumerate((kk, uu, vv)):
            f = base + i * levels + l
            wide.append((spread(nat.at[2 + i], pieces(c[l], f)), sides(from_left, from_right, f)))
        store_coefs(coef, l, *wide)
        for t in range(tracers):
            f = t * levels + l
            mid, side = spread(nat.at[5 + t], pieces(conc[t, l], f)), sides(from_left, from_right, f)
            for g in range(steps):
                state[0, t, 0, g] = mid[g]
                state[0, t, 1, g] = side[g]
        for s in range(STEPS):
            forward_step(state, s % 2, 1 - s % 2, range(tracers), lambda i, h, g: coef[l, i, h, g], steps)
        for t in range(tracers):
            value = gather(nat.at[5 + t], [state[STEPS % 2, t, 0, g] for g in range(steps)])
            out[t, l] = value[0:n]
        return carry

    lax.fori_loop(0, levels, one, 0)


def slots(code, first, n, m):
    where = code.astype(jnp.int32) - 1
    x, y = (where >> (m.bit_length() - 1)) - first, where & (m - 1)
    xs = [(iota((n, m), 0) == x[s : s + 1, :]).astype(F32) for s in range(CAP)]
    ys = [(iota((m, m), 0) == y[s : s + 1, :]).astype(F32).astype(BF16) for s in range(CAP)]
    return xs, jnp.concatenate(ys, axis=1)


def force_body(asked, mine, other, values, force):
    n, m = mine.shape[0] - EDGE, mine.shape[1]
    t = asked[...].T
    rims = jnp.zeros((4 * EDGE, m), F32)
    for i in range(3):
        part = t[2 * CAP * i : 2 * CAP * (i + 1)]
        obs = [o.astype(F32) for o in split3(part[CAP:])]
        if i == 0:
            xs, ys = slots(part[:CAP], 0, n, m)
        else:
            xs, ys = slots(part[:CAP], 0 if i == 1 else n - EDGE, EDGE, m)
            rim = iota((EDGE, m), 0)
            keep = ((rim < HALO) if i == 1 else (rim >= HALO)).astype(F32)
            xs = [x * keep for x in xs]
        lhs = [
            jnp.concatenate([x] + [x * o[s : s + 1, :] for o in obs], axis=0).astype(BF16)
            for s, x in enumerate(xs)
        ]
        got = nt(jnp.concatenate(lhs, axis=1), ys)
        if i == 0:
            sums = got
        else:
            rims = rims + got
    for at, rows, tall in ((0, n, sums), (n, EDGE, rims)):
        count = tall[:rows]
        seen = tall[rows : 2 * rows] + tall[2 * rows : 3 * rows] + tall[3 * rows :]
        where = slice(at, at + rows)
        force[where] = count * (mine[where] + other[where]) - seen


def values_body(asked, mine, other, coef, values):
    n, m = mine.shape[0] - EDGE, mine.shape[1]
    field = mine[0:n] + other[0:n]
    t = asked[...].T
    xs, ys = slots(t[:CAP], 0, n, m)
    fields = jnp.concatenate(split3(field), axis=0)
    got = nn(fields, ys)
    got = got[:n] + got[n : 2 * n] + got[2 * n :]
    picked = [
        jnp.sum(got[:, m * s : m * (s + 1)] * xs[s], axis=0, keepdims=True) for s in range(CAP)
    ]
    picked.append(jnp.zeros((t.shape[0] - CAP, t.shape[1]), F32))
    values[...] = jnp.concatenate(picked, axis=0).T


def answer_body(groups, got, owner, rank, out):
    rows, lanes = owner.shape
    t = got[...].T[:CAP]
    parts = jnp.concatenate(split3(t), axis=0)
    who = tile_at(iota((groups, lanes), 0), groups)
    hot = [(who == owner[j : j + 1, :]).astype(F32).astype(BF16) for j in range(rows)]
    z = nn(parts, jnp.concatenate(hot, axis=1))
    z = z[:CAP] + z[CAP : 2 * CAP] + z[2 * CAP :]
    for j in range(rows):
        slot = iota((CAP, lanes), 0) == rank[j : j + 1, :]
        mine = z[:, lanes * j : lanes * (j + 1)]
        out[j : j + 1, :] = jnp.sum(jnp.where(slot, mine, 0.0), axis=0, keepdims=True)


def adjoint_body(force, left, right, coef, weight, out, state, nat):
    keep_l, keep_r = inside("gy")
    n, m = out.shape[2], out.shape[3]
    at = iota((EDGE, m), 1)
    mid, a, b = (spread(nat.at[i], (x[...],)) for i, x in enumerate((force, right, left)))
    levels = out.shape[1]
    steps = len(mid)
    for g in range(steps):
        side = jnp.where(at < HALO, a[g] * keep_r, jnp.where(at >= m - HALO, b[g] * keep_l, 0.0))
        for l in range(levels):
            state[0, l, 0, g] = mid[g]
            state[0, l, 1, g] = side
    for s in range(STEPS):
        for l in range(levels):
            adjoint_step(state, s % 2, 1 - s % 2, l, lambda i, h, g: coef[l, i, h, g], steps)
    for l in range(levels):
        value = gather(nat.at[3 + l], [state[STEPS % 2, l, 0, g] for g in range(steps)])
        for t in range(out.shape[0]):
            out[t, l] = weight[t, l] * value[0:n]


def after(x, other):
    shape = jax.ShapeDtypeStruct(x.shape, x.dtype)
    return call(lambda *_: None, shape, (x, other), [ANY] * 2, us=600.0, outspec=ANY, alias={0: 0})


def ring(value, axis, step):
    n = lax.axis_size(axis)
    return lax.ppermute(value, axis, [(i, (i + step) % n) for i in range(n)])


def long_ring(value, step):
    n = lax.axis_size("gx")
    pairs = []
    for l in range(2):
        for i in range(n):
            to = i + step
            pairs.append((l * n + i, l * n + to if 0 <= to < n else (1 - l) * n + to % n))
    return lax.ppermute(value, ("lev", "gx"), pairs)


def exchange(value):
    nx, ny = lax.axis_size("gx"), lax.axis_size("gy")
    order = [tile_at(t, nx * ny) for t in range(nx * ny)]
    groups = [[(g ^ (2 * t // (nx * ny))) * nx * ny + t for t in order] for g in range(2)]
    return lax.all_to_all(
        value, ("lev", "gx", "gy"), 0, 0, axis_index_groups=groups, tiled=True
    )


def shards(conc, kk, uu, vv, weight, owner, column, observed):
    S = jax.ShapeDtypeStruct
    tracers, levels, n, m = conc.shape
    fields = (tracers + 3) * levels
    groups = lax.axis_size("gx") * lax.axis_size("gy")
    owner = owner.reshape(-1, 128)
    column = column.reshape(-1, 128)
    obs = observed.reshape(-1, 128)
    tile, edge = S((n, m), F32), S((fields, EDGE, m), F32)
    sounding = (owner, column, obs)
    right, left, high, low, *sounding = call(
        edges_body,
        (tile, tile, edge, edge, *(S(a.shape, a.dtype) for a in sounding)),
        [pltpu.with_memory_space_constraint(a, pltpu.HBM) for a in (conc, kk, uu, vv, *sounding)],
        [HBM] * 7,
        scratch=[pltpu.VMEM(a.shape, F32) for a in (conc, kk, uu, vv)]
        + [pltpu.SemaphoreType.DMA((7,))],
    )
    owner = sounding[0]
    left, right = ring(right, "gy", 1), ring(left, "gy", -1)
    req, rank = call(
        functools.partial(request_body, groups, lax.axis_size("gy")),
        (S((groups, 128), F32), S(owner.shape, jnp.int32)),
        tuple(sounding),
        us=600.0,
    )
    edge = S((fields + 2, EDGE, m), F32)
    high, low = call(corners_body, (edge, edge), (high, low, left, right))
    above, below = long_ring(low, -1), long_ring(high, 1)
    asked = exchange(after(req, low))
    inputs = (conc, kk, uu, vv, below, above, left, right)
    strip = S((n + EDGE, m), F32)
    more, some = (n + 2 * EDGE) // EDGE, (n + EDGE) // EDGE
    mine = call(
        column_body,
        strip,
        (*inputs, weight),
        [VMEM] * 8 + [SMEM],
        us=600.0,
        scratch=[
            pltpu.VMEM((levels, 5, 2, more, EDGE, m), F32),
            pltpu.VMEM((2, levels, 2, more, EDGE, m), F32),
            pltpu.VMEM((4 + 3 * levels, n + 2 * EDGE, m), F32),
        ],
    )
    other = lax.ppermute(mine, "lev", [(0, 1), (1, 0)])
    forecast, coef = call(
        forward_body,
        (S(conc.shape, F32), S((levels, 5, 2, some, EDGE, m), F32)),
        inputs,
        us=600.0,
        scratch=[
            pltpu.VMEM((2, tracers, 2, some, EDGE, m), F32),
            pltpu.VMEM((5 + tracers, n + EDGE, m), F32),
        ],
    )
    values = call(
        values_body,
        S((groups, 128), F32),
        (asked, mine, other, coef),
        [VMEM] * 3 + [ANY],
        us=600.0,
    )
    got = exchange(values)
    force = call(
        force_body, strip, (asked, mine, other, values), [VMEM] * 3 + [ANY], us=600.0
    )
    left, right = ring(force, "gy", 1), ring(force, "gy", -1)
    gradient = call(
        adjoint_body,
        S(conc.shape, F32),
        (force, left, right, coef, weight),
        [VMEM] * 4 + [SMEM],
        us=600.0,
        scratch=[
            pltpu.VMEM((2, levels, 2, some, EDGE, m), F32),
            pltpu.VMEM((3 + levels, n + EDGE, m), F32),
        ],
    )
    model = call(
        functools.partial(answer_body, groups), S(owner.shape, F32), (got, owner, rank)
    )
    return (forecast, model.reshape(-1), gradient)


def solution(mesh):
    return jax.shard_map(
        shards,
        mesh=mesh,
        in_specs=(
            P(None, "lev", "gx", "gy"),
            P("lev", "gx", "gy"),
            P("lev", "gx", "gy"),
            P("lev", "gx", "gy"),
            P(None, "lev"),
            P(("gx", "gy"), None),
            P(("gx", "gy")),
            P(("gx", "gy")),
        ),
        out_specs=(P(None, "lev", "gx", "gy"), P(("gx", "gy")), P(None, "lev", "gx", "gy")),
        check_vma=False,
    )
```
